32 devices in a mesh: dp: 16 (over z, y, x), head: 2 (over core).
Axes of the slice: x: 2, y: 2, z: 4, core: 2. Of those that a mesh axis runs over, the one named last changes fastest.
Arguments:
- tokens: bfloat16 [96, 197, 768], P(('dp', 'head')), may hold values from -6 to 6
- kept_index: int32 [96, 98], P(('dp', 'head')), may hold values from 0 to 196, as said below
- kept_count: int32 [96], P(('dp', 'head')), may hold values from 49 to 98, as said below
- ln1_gain: float32 [768], replicated, may hold values from 0.5 to 1.5
- ln1_bias: float32 [768], replicated, may hold values from -1 to 1
- w_qkv: bfloat16 [3, 768, 768], P(None, None, 'head'), may hold values from -0.3125 to 0.3125
- w_proj: bfloat16 [768, 768], P('head'), may hold values from -0.875 to 0.875
- proj_bias: float32 [768], replicated, may hold values from -1 to 1
- ln2_gain: float32 [768], replicated, may hold values from 0.5 to 1.5
- ln2_bias: float32 [768], replicated, may hold values from -1 to 1
- w_fc1: bfloat16 [768, 3072], P(None, 'head'), may hold values from -0.21875 to 0.21875
- fc1_bias: float32 [3072], P('head'), may hold values from -1 to 1
- w_fc2: bfloat16 [3072, 768], P('head'), may hold values from -0.15625 to 0.15625
- fc2_bias: float32 [768], replicated, may hold values from -1 to 1
- w_router: float32 [768], replicated, may hold values from -0.4375 to 0.4375
- cotangent: bfloat16 [96, 197, 768], P(('dp', 'head')), may hold values from -6 to 6
Outputs:
- out: bfloat16 [96, 197, 768], P(('dp', 'head'))
- input_grad: bfloat16 [96, 197, 768], P(('dp', 'head'))
- ln1_gain_grad: float32 [768], replicated
- ln1_bias_grad: float32 [768], replicated
- qkv_grad: float32 [3, 768, 768], P(None, 'dp', 'head')
- proj_grad: float32 [768, 768], P('head', 'dp')
- proj_bias_grad: float32 [768], replicated
- ln2_gain_grad: float32 [768], replicated
- ln2_bias_grad: float32 [768], replicated
- fc1_grad: float32 [768, 3072], P('dp', 'head')
- fc1_bias_grad: float32 [3072], P('head')
- fc2_grad: float32 [3072, 768], P('head', 'dp')
- fc2_bias_grad: float32 [768], replicated
- router_grad: float32 [768], replicated
The draws below stay inside these ranges and needn't reach their ends.
Inputs may be any that keep to these rules, and one draw needn't show every extreme that they name: `kept_index`: each row holds 98 distinct slot numbers of its image in ascending order; the first kept_count of them are the image's kept slots, the rest pass unchanged like the slots not named. `kept_count`: some image keeps all 98 in every draw.
All inputs are finite; a program needn't handle non-finite values.
Results may differ from the reference program's by a relative error of at most 0.012.
The reference program's roundings to bfloat16 on the way count: a program that leaves them out, or rounds other values in their place, can miss the bound.
Values may be sent and summed in bfloat16 or wider, within the bound.
No kernel may reach another device: no remote copies, remote signals or barrier semaphores. Data moves between devices by JAX's collectives and lax.ppermute only.
A program may use at most 128 MiB of HBM per device.

```python
import jax
import jax.numpy as jnp
from jax import lax

D = 768
HEADS = 12
HEAD_DIM = 64
FF = 3072
SLOTS = 197
CAP = 98
IMG_DEV = 3
IMAGES = 96


def draw_kept_index(key, part):
    noise = jax.random.randint(jax.random.fold_in(key, 11), (IMAGES, SLOTS), 0, 1 << 20)
    ranked = noise * SLOTS + jnp.arange(SLOTS, dtype=jnp.int32)[None, :]
    order = jnp.argsort(ranked, axis=1, stable=True)
    return jnp.sort(order[:, :CAP], axis=1).astype(jnp.int32)


def draw_kept_count(key, part):
    counts = jax.random.randint(jax.random.fold_in(key, 21), (IMAGES,), CAP // 2, CAP + 1)
    chosen = jax.random.randint(jax.random.fold_in(key, 22), (), 0, IMAGES)
    return counts.at[chosen].set(CAP).astype(jnp.int32)


def with_spikes(values, key, source, target, blocks, factor):
    def block_of(position):
        return (jnp.arange(values.shape[position]) // (values.shape[position] // blocks)).reshape((-1,) + (1,) * (values.ndim - 1 - position))

    one_side = jax.random.permutation(key, blocks)[block_of(target)]
    other_side = (block_of(target) + blocks // 2) % blocks
    return jnp.where((block_of(source) == one_side) | (block_of(source) == other_side), factor * values, values)


def steps_of(stream_key, dims, split, low, top_value):
    loudness, own = 1.0, jax.random.fold_in(stream_key, 6)
    for dim, shards_of in split:
        draws = jnp.exp(jax.random.uniform(jax.random.fold_in(own, dim), (shards_of,), jnp.float32, low / len(split), top_value / len(split)))
        loudness = loudness * jnp.repeat(draws, dims[dim] // shards_of).reshape([-1 if axis == dim else 1 for axis in range(len(dims))])
    return loudness


def gaussian(own_key, shape, width, most, split=(), held_as=jnp.bfloat16):
    array = jax.random.normal(own_key, shape, jnp.float32) * width
    if len(split) > 0:
        array = steps_of(own_key, shape, split, -0.22, 0.18) * array
    return jnp.clip(array, min=-most, max=most).astype(held_as)


def heavy_noise(own_key, shape, scale, most, cuts, heavy, kind=jnp.bfloat16):
    values = scale * jax.random.normal(own_key, shape, jnp.float32)
    if cuts:
        values = values * steps_of(own_key, shape, cuts, -0.22, 0.18)
    return jnp.clip(with_spikes(values, jax.random.fold_in(own_key, 3), *heavy), -most, most).astype(kind)


def setup_inputs(seed: int = 0) -> dict:
    key_of = jax.random.split(jax.random.key(seed), 17)
    return {
        "tokens": heavy_noise(key_of[0], (IMAGES, SLOTS, D), 1.0, 6.0, ((0, 32),), (0, 2, 32, 2.75)),
        "kept_index": draw_kept_index(jax.random.fold_in(key_of[16], 71), 0),
        "kept_count": draw_kept_count(jax.random.fold_in(key_of[16], 71), 0),
        "ln1_gain": jnp.clip(1.0 + 0.1 * jax.random.normal(key_of[3], (D,), jnp.float32), 0.5, 1.5),
        "ln1_bias": gaussian(key_of[4], (D,), 0.2, 1.0, (), jnp.float32),
        "w_qkv": gaussian(key_of[5], (3, D, D), (D // 2) ** -0.5, 0.3125, ((2, 2),)),
        "w_proj": gaussian(key_of[6], (D, D), (D // 16) ** -0.5, 0.875, ((0, 2),)),
        "proj_bias": gaussian(key_of[7], (D,), 0.2, 1.0, (), jnp.float32),
        "ln2_gain": jnp.clip(1.0 + 0.1 * jax.random.normal(key_of[8], (D,), jnp.float32), 0.5, 1.5),
        "ln2_bias": gaussian(key_of[9], (D,), 0.2, 1.0, (), jnp.float32),
        "w_fc1": gaussian(key_of[10], (D, FF), D ** -0.5, 0.21875, ((1, 2),)),
        "fc1_bias": gaussian(key_of[11], (FF,), 0.2, 1.0, ((0, 2),), jnp.float32),
        "w_fc2": gaussian(key_of[12], (FF, D), (FF // 2) ** -0.5, 0.15625, ((0, 2),)),
        "fc2_bias": gaussian(key_of[13], (D,), 0.2, 1.0, (), jnp.float32),
        "w_router": gaussian(key_of[14], (D,), (D // 4) ** -0.5, 0.4375, (), jnp.float32),
        "cotangent": heavy_noise(key_of[15], (IMAGES, SLOTS, D), 1.0, 6.0, ((0, 32),), (0, 2, 32, 2.75)),
    }


@jax.custom_vjp
def low(v):
    return lax.optimization_barrier(v.astype(jnp.bfloat16)).astype(jnp.float32)

@jax.custom_vjp
def low_back(v):
    return v

def low_keep(v):
    return (low(v), None)

def low_pass(kept, grad):
    return (grad,)

def back_keep(v):
    return (v, None)

def back_low(kept, grad):
    return (low(grad),)
low.defvjp(low_keep, low_pass)
low_back.defvjp(back_keep, back_low)
highest = lax.Precision.HIGHEST
norm_eps = 1e-06
root_half = 0.7071067811865476

def layer_norm(values, gain, shift):
    row_mean = lax.optimization_barrier(jnp.mean(values, axis=-1, keepdims=True))
    centered = values - row_mean
    variance = lax.optimization_barrier(jnp.mean(centered * centered, axis=-1, keepdims=True))
    return centered * lax.rsqrt(variance + norm_eps) * gain + shift

def gelu_exact(values):
    return 0.5 * values * (1.0 + lax.erf(values * root_half))

def forward(image_block, params, slot_index, slot_count):
    ln1_gain, ln1_bias, w_qkv, w_proj, proj_bias, ln2_gain, ln2_bias, w_fc1, fc1_bias, w_fc2, fc2_bias, w_router = params
    image_total = image_block.shape[0]
    batch_rows = jnp.arange(image_total)[:, None]
    picked = image_block[batch_rows, slot_index]
    live_mask = (jnp.arange(CAP)[None, :] < slot_count[:, None]).astype(jnp.float32)
    router = jax.nn.sigmoid(jnp.einsum('bcd,d->bc', picked, w_router, precision=highest))
    first_normed = low(layer_norm(picked, ln1_gain, ln1_bias))
    projected = low(low_back(jnp.einsum('bcd,tde->tbce', first_normed, w_qkv, precision=highest)))
    shaped = projected.reshape(3, image_total, CAP, HEADS, HEAD_DIM)
    scores = jnp.einsum('bqhd,bkhd->bhqk', shaped[0], shaped[1], precision=highest) * HEAD_DIM ** (-0.5)
    scores = low_back(scores)
    scores = jnp.where(live_mask[:, None, None, :] > 0, scores, -1e+30)
    top_score = lax.optimization_barrier(jnp.max(scores, axis=-1, keepdims=True))
    exp_scores = jnp.exp(scores - top_score)
    probabilities = low(exp_scores / lax.optimization_barrier(jnp.sum(exp_scores, axis=-1, keepdims=True)))
    mixed_heads = jnp.einsum('bhqk,bkhd->bqhd', probabilities, shaped[2], precision=highest).reshape(image_total, CAP, D)
    mixed_heads = low(low_back(mixed_heads))
    attention = low_back(jnp.einsum('bce,ed->bcd', mixed_heads, w_proj, precision=highest)) + proj_bias
    second = low(layer_norm(picked + attention, ln2_gain, ln2_bias))
    pre_act = low_back(jnp.einsum('bcd,df->bcf', second, w_fc1, precision=highest)) + fc1_bias
    activation = low(gelu_exact(pre_act))
    mlp_out = low_back(jnp.einsum('bcf,fd->bcd', activation, w_fc2, precision=highest)) + fc2_bias
    update = (live_mask * router)[:, :, None] * (attention + mlp_out)
    return image_block.at[batch_rows, slot_index].add(update)

def reference(tokens, kept_index, kept_count, ln1_gain, ln1_bias, w_qkv, w_proj, proj_bias, ln2_gain, ln2_bias, w_fc1, fc1_bias, w_fc2, fc2_bias, w_router, cotangent):
    params = tuple((weight.astype(jnp.float32) for weight in (ln1_gain, ln1_bias, w_qkv, w_proj, proj_bias, ln2_gain, ln2_bias, w_fc1, fc1_bias, w_fc2, fc2_bias, w_router)))
    group_size = 4 * IMG_DEV
    group_total = IMAGES // group_size
    token_groups = tokens.reshape(group_total, group_size, SLOTS, D)
    grad_groups = cotangent.reshape(group_total, group_size, SLOTS, D)
    index_groups = kept_index.reshape(group_total, group_size, CAP).astype(jnp.int32)
    count_groups = kept_count.reshape(group_total, group_size).astype(jnp.int32)

    def scan_step(totals, scan_item):
        image_block, grad_block, slot_index, slot_count = scan_item

        def run_forward(block_float, weights):
            return forward(block_float, weights, slot_index, slot_count)
        result, pull_back = jax.vjp(run_forward, image_block.astype(jnp.float32), params)
        grad_input, grad_params = pull_back(grad_block.astype(jnp.float32))
        totals = tuple((first_term + second_term for first_term, second_term in zip(totals, grad_params)))
        return (totals, (result.astype(jnp.bfloat16), grad_input.astype(jnp.bfloat16)))
    zero_grads = tuple((jnp.zeros_like(weight) for weight in params))
    totals, (outputs, input_grads) = lax.scan(scan_step, zero_grads, (token_groups, grad_groups, index_groups, count_groups))
    out = outputs.reshape(IMAGES, SLOTS, D)
    input_grad = input_grads.reshape(IMAGES, SLOTS, D)
    return (out, input_grad, totals[0], totals[1], totals[2], totals[3], totals[4], totals[5], totals[6], totals[7], totals[8], totals[9], totals[10], totals[11])
```

```python
import jax
import jax.numpy as jnp
from jax import lax
from jax.sharding import PartitionSpec as P

HEAD_DIM = 64
norm_eps = 1e-06
root_half = 0.7071067811865476
inv_root_two_pi = 0.3989422804014327
f32, bf16 = jnp.float32, jnp.bfloat16


def norm_stats(values):
    row_mean = jnp.mean(values, axis=-1, keepdims=True)
    centered = values - row_mean
    inv_std = lax.rsqrt(jnp.mean(centered * centered, axis=-1, keepdims=True) + norm_eps)
    return centered * inv_std, inv_std


def norm_back(grad_normed, gain, normed, inv_std):
    unit = grad_normed * gain
    return inv_std * (
        unit
        - jnp.mean(unit, axis=-1, keepdims=True)
        - normed * jnp.mean(unit * normed, axis=-1, keepdims=True)
    )


def dot(a, b, dims):
    return lax.dot_general(a, b, (dims, ((), ())), preferred_element_type=f32)


def other_core(value):
    return lax.ppermute(value, "head", [(0, 1), (1, 0)])


def partners(count, bit):
    return [(i, i ^ (1 << bit)) for i in range(count)]


class Halving:
    def __init__(self, grad, order, count):
        self.count, self.order, self.bits = count, order, len(order)
        self.terms = [grad.reshape((2,) * self.bits + (grad.shape[0] // count, grad.shape[1]))]
        self.step = 0

    def send(self, place):
        bit = self.order[self.step]
        axis = self.bits - 1 - bit
        mine = (place >> bit) & 1
        away = sum(
            lax.dynamic_slice_in_dim(t, 1 - mine, 1, axis).astype(f32) for t in self.terms
        ).astype(bf16)
        self.terms = [lax.dynamic_slice_in_dim(t, mine, 1, axis) for t in self.terms]
        self.terms.append(lax.ppermute(away, "dp", partners(self.count, bit)))
        self.step += 1

    def result(self):
        total = sum(t.astype(f32) for t in self.terms)
        return total.reshape(total.shape[self.bits :])


def reduce_rows(grad, count, place):
    bits = count.bit_length() - 1
    width = grad.shape[1] // 3
    low = min(3, bits)
    parts = []
    for i in range(3):
        order = [(i + j) % low for j in range(low)] + list(range(low, bits))
        parts.append(Halving(grad[:, i * width : (i + 1) * width], order, count))
    for _ in range(bits):
        for part in parts:
            part.send(place)
    return jnp.concatenate([part.result() for part in parts], axis=1)


def on_device(
    tokens,
    kept_index,
    kept_count,
    ln1_gain,
    ln1_bias,
    w_qkv,
    w_proj,
    proj_bias,
    ln2_gain,
    ln2_bias,
    w_fc1,
    fc1_bias,
    w_fc2,
    fc2_bias,
    w_router,
    cotangent,
):
    images, slots, width = tokens.shape
    capacity = kept_index.shape[1]
    padded = -(-capacity // 8) * 8
    rows = images * padded
    local = w_qkv.shape[2]
    heads = local // HEAD_DIM
    units = w_fc1.shape[1]
    factor = HEAD_DIM ** (-0.5)
    dp_count = lax.axis_size("dp")
    place = lax.axis_index("dp")

    w_qkv2 = (w_qkv, other_core(w_qkv))
    w_proj2 = (w_proj, other_core(w_proj))
    w_fc12 = (w_fc1, other_core(w_fc1))
    fc1_bias2 = (fc1_bias, other_core(fc1_bias))
    w_fc22 = (w_fc2, other_core(w_fc2))

    index = jnp.pad(kept_index, ((0, 0), (0, padded - capacity)), constant_values=-1)
    hot = (index[:, :, None] == jnp.arange(slots)[None, None, :]).astype(bf16)
    live = (jnp.arange(padded)[None, :] < kept_count[:, None]).astype(f32)

    def pick(array):
        got = lax.dot_general(
            hot, array, (((2,), (1,)), ((0,), (0,))), preferred_element_type=f32
        )
        return got.reshape(rows, width)

    def put(array):
        high = array.astype(bf16)
        low = (array - high.astype(f32)).astype(bf16)
        both = [
            lax.dot_general(
                hot,
                piece.reshape(images, padded, width),
                (((1,), (1,)), ((0,), (0,))),
                preferred_element_type=f32,
            )
            for piece in (high, low)
        ]
        return both[0] + both[1]

    picked = pick(tokens)
    grad_picked = pick(cotangent)
    live_row = live.reshape(rows, 1)
    router = jax.nn.sigmoid(jnp.sum(picked * w_router, axis=-1, keepdims=True))
    scale_rows = live_row * router
    grad_branch = scale_rows * grad_picked
    grad_mlp = grad_branch.astype(bf16)
    normed_one, inv_one = norm_stats(picked)
    first = (normed_one * ln1_gain + ln1_bias).astype(bf16)
    first_par = other_core(first)
    grad_mlp_par = other_core(grad_mlp)

    def split_heads(array):
        return array.reshape(images, padded, heads, HEAD_DIM)

    saved = []
    attention = proj_bias
    for side in range(2):
        q, k, v = (
            split_heads(dot(first, w_qkv2[side][t], ((1,), (0,))).astype(bf16)) for t in range(3)
        )
        scores = jnp.einsum("bqhd,bkhd->bhqk", q, k, preferred_element_type=f32) * factor
        scores = jnp.where(live[:, None, None, :] > 0, scores, -1e30)
        top = jnp.max(scores, axis=-1, keepdims=True)
        raised = jnp.exp(scores - top)
        probs = raised / jnp.sum(raised, axis=-1, keepdims=True)
        probs_low = probs.astype(bf16)
        mixed = jnp.einsum("bhqk,bkhd->bqhd", probs_low, v, preferred_element_type=f32)
        mixed = mixed.reshape(rows, local).astype(bf16)
        attention = attention + dot(mixed, w_proj2[side], ((1,), (0,)))
        saved.append((q, k, v, probs, probs_low, mixed))
    mixed_par = other_core(saved[1][5])
    normed_two, inv_two = norm_stats(picked + attention)
    second = (normed_two * ln2_gain + ln2_bias).astype(bf16)
    second_par = other_core(second)

    mlp_out = fc2_bias
    grad_second = 0.0
    acts, grad_pres, unit_sums = [None] * 2, [None] * 2, [None] * 2
    for side in (1, 0):
        pre = dot(second, w_fc12[side], ((1,), (0,))) + fc1_bias2[side]
        half = 0.5 * (1.0 + lax.erf(pre * root_half))
        act = (pre * half).astype(bf16)
        slope = half + pre * inv_root_two_pi * jnp.exp(-0.5 * pre * pre)
        grad_pre = dot(grad_mlp, w_fc22[side], ((1,), (1,))) * slope
        unit_sums[side] = jnp.sum(grad_pre, axis=0)
        grad_pre_low = grad_pre.astype(bf16)
        acts[side], grad_pres[side] = act, grad_pre_low
        mlp_out = mlp_out + dot(act, w_fc22[side], ((1,), (0,)))
        grad_second = grad_second + dot(grad_pre_low, w_fc12[side], ((1,), (1,)))
    act_par = other_core(acts[1])
    grad_pre_par = other_core(grad_pres[1])

    def both_rows(left, left_par, right, right_par):
        return dot(left, right, ((0,), (0,))) + dot(left_par, right_par, ((0,), (0,)))

    fc2_turned = both_rows(grad_mlp, grad_mlp_par, acts[0], act_par)
    fc1_local = both_rows(second, second_par, grad_pres[0], grad_pre_par)
    mlp_grads = reduce_rows(jnp.concatenate([fc2_turned, fc1_local], axis=1), dp_count, place)

    branch = attention + mlp_out
    output = (tokens.astype(f32) + put(scale_rows * branch)).astype(bf16)
    grad_logit = (
        scale_rows * (1.0 - router) * jnp.sum(grad_picked * branch, axis=-1, keepdims=True)
    )

    grad_hidden = norm_back(grad_second, ln2_gain, normed_two, inv_two)
    grad_attention = grad_branch + grad_hidden
    grad_attn_low = grad_attention.astype(bf16)
    grad_attn_par = other_core(grad_attn_low)
    grad_first = 0.0
    grad_qkvs = []
    for side in range(2):
        q, k, v, probs, probs_low, mixed = saved[side]
        grad_mixed = split_heads(dot(grad_attn_low, w_proj2[side], ((1,), (1,))).astype(bf16))
        grad_probs = jnp.einsum("bqhd,bkhd->bhqk", grad_mixed, v, preferred_element_type=f32)
        row_dot = jnp.sum(probs * grad_probs, axis=-1, keepdims=True)
        grad_scores = (probs * (grad_probs - row_dot)).astype(bf16)
        grad_q = jnp.einsum("bhqk,bkhd->bqhd", grad_scores, k, preferred_element_type=f32) * factor
        grad_k = jnp.einsum("bhqk,bqhd->bkhd", grad_scores, q, preferred_element_type=f32) * factor
        grad_v = jnp.einsum("bhqk,bqhd->bkhd", probs_low, grad_mixed, preferred_element_type=f32)
        flat = [g.reshape(rows, local).astype(bf16) for g in (grad_q, grad_k, grad_v)]
        grad_qkvs.append(jnp.concatenate(flat, axis=1))
        for t in range(3):
            grad_first = grad_first + dot(flat[t], w_qkv2[side][t], ((1,), (1,)))
    grad_qkv_par = other_core(grad_qkvs[1])
    qkv_local = both_rows(first, first_par, grad_qkvs[0], grad_qkv_par)
    proj_turned = both_rows(grad_attn_low, grad_attn_par, saved[0][5], mixed_par)
    attn_grads = reduce_rows(jnp.concatenate([qkv_local, proj_turned], axis=1), dp_count, place)

    grad_kept = (
        norm_back(grad_first, ln1_gain, normed_one, inv_one) + grad_hidden + grad_logit * w_router
    )
    input_grad = (cotangent.astype(f32) + put(grad_kept)).astype(bf16)

    def total(values):
        return jnp.sum(values, axis=0)

    shared = jnp.concatenate(
        [
            total(grad_first * normed_one),
            total(grad_first),
            total(grad_attention),
            total(grad_second * normed_two),
            total(grad_second),
            total(grad_branch),
            total(grad_logit * picked),
        ]
    )
    small = jnp.concatenate([shared, unit_sums[0]]) + other_core(
        jnp.concatenate([shared, unit_sums[1]])
    )
    for bit in range(dp_count.bit_length() - 1):
        small = small + lax.ppermute(small, "dp", partners(dp_count, bit))
    pieces = [small[i * width : (i + 1) * width] for i in range(7)]
    fc1_bias_grad = small[7 * width :]

    row_count = width // dp_count
    fc2_grad = mlp_grads[:, :units].T
    fc1_grad = mlp_grads[:, units:]
    qkv_grad = attn_grads[:, : 3 * local].reshape(row_count, 3, local).transpose(1, 0, 2)
    proj_grad = attn_grads[:, 3 * local :].T
    return (
        output,
        input_grad,
        pieces[0],
        pieces[1],
        qkv_grad,
        proj_grad,
        pieces[2],
        pieces[3],
        pieces[4],
        fc1_grad,
        fc1_bias_grad,
        fc2_grad,
        pieces[5],
        pieces[6],
    )


def solution(mesh):
    batch = ("dp", "head")
    return jax.shard_map(
        on_device,
        mesh=mesh,
        in_specs=(
            P(batch, None, None),
            P(batch, None),
            P(batch),
            P(),
            P(),
            P(None, None, "head"),
            P("head", None),
            P(),
            P(),
            P(),
            P(None, "head"),
            P("head"),
            P("head", None),
            P(),
            P(),
            P(batch, None, None),
        ),
        out_specs=(
            P(batch, None, None),
            P(batch, None, None),
            P(),
            P(),
            P(None, "dp", "head"),
            P("head", "dp"),
            P(),
            P(),
            P(),
            P("dp", "head"),
            P("head"),
            P("head", "dp"),
            P(),
            P(),
        ),
        check_vma=False,
    )
```

```python
import functools

import jax
import jax.numpy as jnp
from jax import lax
from jax.experimental import pallas as pl
from jax.experimental.pallas import tpu as pltpu
from jax.sharding import PartitionSpec as P

HEAD_DIM = 64
norm_eps = 1e-06
root_half = 0.7071067811865476
inv_root_two_pi = 0.3989422804014327
f32, bf16 = jnp.float32, jnp.bfloat16


MIB = 1024 * 1024
SIDES = 2
COST_RATE = 1_100_000_000
UNIT_BLOCK = 512


def rows_of(count):
    return -(-count // 16) * 16


def norm_stats(values):
    row_mean = jnp.mean(values, axis=-1, keepdims=True)
    centered = values - row_mean
    inv_std = lax.rsqrt(jnp.mean(centered * centered, axis=-1, keepdims=True) + norm_eps)
    return centered * inv_std, inv_std


def norm_back(grad_normed, gain, normed, inv_std):
    unit = grad_normed * gain
    return inv_std * (
        unit
        - jnp.mean(unit, axis=-1, keepdims=True)
        - normed * jnp.mean(unit * normed, axis=-1, keepdims=True)
    )


def dot(a, b, over=((1,), (0,))):
    return lax.dot_general(a, b, (over, ((), ())), preferred_element_type=f32)


def dot_turned(a, b):
    return dot(a, b, ((1,), (1,)))


def column_sum(values):
    return jnp.sum(values, axis=0, keepdims=True)


class Held:
    def __init__(self, ref, copy):
        self.ref, self.copy, self.shape = ref, copy, ref.shape

    def ready(self):
        if self.copy is not None:
            self.copy.wait()
            self.copy = None
        return self.ref

    def __getitem__(self, at):
        return self.ready()[at]


class Made:
    def __init__(self, ref, copy):
        self.ref, self.copy, self.shape, self.left = ref, copy, ref.shape, False

    def __getitem__(self, at):
        return self.ref[at]

    def __setitem__(self, at, value):
        self.ref[at] = value

    def leave(self):
        if not self.left:
            self.copy.start()
            self.left = True


class Far:
    def __init__(self, value):
        self.value = value


def call(kernel, out_shape, inputs, scalars=0, scratch=(), us=1, room=14):
    values = [x.value if isinstance(x, Far) else x for x in inputs]
    shapes = [x.value if isinstance(x, Far) else x for x in out_shape]
    far_in = [i for i, x in enumerate(inputs) if isinstance(x, Far)]
    far_out = [i for i, x in enumerate(out_shape) if isinstance(x, Far)]
    n_in, n_out = len(inputs), len(out_shape)
    near, away = pl.BlockSpec(memory_space=pltpu.VMEM), pl.BlockSpec(memory_space=pltpu.HBM)
    in_specs = [pl.BlockSpec(memory_space=pltpu.SMEM)] * scalars
    in_specs += [away if i in far_in else near for i in range(scalars, n_in)]

    def body(*refs):
        ins, outs, refs = list(refs[:n_in]), list(refs[n_in : n_in + n_out]), refs[n_in + n_out :]
        in_refs, refs = refs[: len(far_in)], refs[len(far_in) :]
        out_refs, refs = refs[: len(far_out)], refs[len(far_out) :]
        sems, extra = (refs[0], refs[1:]) if far_in or far_out else (None, refs)
        for n, i in enumerate(far_in):
            copy = pltpu.make_async_copy(ins[i], in_refs[n], sems.at[n])
            copy.start()
            ins[i] = Held(in_refs[n], copy)
        for n, i in enumerate(far_out):
            copy = pltpu.make_async_copy(out_refs[n], outs[i], sems.at[len(far_in) + n])
            outs[i] = Made(out_refs[n], copy)
        kernel(*ins, *outs, *extra)
        for i in far_in:
            ins[i].ready()
        for i in far_out:
            outs[i].leave()
        for i in far_out:
            outs[i].copy.wait()

    moved = sum(i.size * i.dtype.itemsize for i in values)
    moved += sum(o.size * o.dtype.itemsize for o in shapes)
    far_scratch = [pltpu.VMEM(values[i].shape, values[i].dtype) for i in far_in]
    far_scratch += [pltpu.VMEM(shapes[i].shape, shapes[i].dtype) for i in far_out]
    if far_scratch:
        far_scratch.append(pltpu.SemaphoreType.DMA((len(far_in) + len(far_out),)))
    values = [
        x if i < scalars else pltpu.with_memory_space_constraint(x, pltpu.HBM if i in far_in else pltpu.VMEM)
        for i, x in enumerate(values)
    ]
    return pl.pallas_call(
        body,
        out_shape=[
            (pltpu.HBM if i in far_out else pltpu.VMEM)(o.shape, o.dtype)
            for i, o in enumerate(shapes)
        ],
        in_specs=in_specs,
        out_specs=[away if i in far_out else near for i in range(n_out)],
        scratch_shapes=[*far_scratch, *scratch],
        compiler_params=pltpu.CompilerParams(vmem_limit_bytes=room * MIB),
        cost_estimate=pl.CostEstimate(flops=us * COST_RATE, bytes_accessed=moved, transcendentals=0),
    )(*values)


def line(ref):
    return ref[...].reshape(1, -1)


def shape(dims, kind):
    return jax.ShapeDtypeStruct(dims, kind)


def live_column(count_ref, images, padded):
    rows = lax.broadcasted_iota(jnp.int32, (padded, 1), 0)
    return jnp.concatenate(
        [jnp.where(rows < count_ref[b], 1.0, 0.0).astype(f32) for b in range(images)], axis=0
    )


def turned_hot(index_ref, padded_ref, image, slots, padded):
    wide = padded_ref[image : image + 1, :padded]
    place = lax.broadcasted_iota(jnp.int32, (slots, padded), 0)
    return jnp.where(place == wide, 1.0, 0.0).astype(bf16)


def fill_index(index_ref, padded_ref):
    padded_ref[...] = jnp.full(padded_ref.shape, -1, jnp.int32)
    padded_ref[: index_ref.shape[0], : index_ref.shape[1]] = index_ref[...]


def front_kernel(
    count_ref,
    index_ref,
    tokens_ref,
    cotangent_ref,
    router_w_ref,
    gain_ref,
    shift_ref,
    picked_ref,
    grad_picked_ref,
    first_ref,
    grad_mlp_ref,
    router_ref,
    fc2_bias_grad_ref,
    padded_ref,
):
    images, slots, _ = tokens_ref.shape
    padded = picked_ref.shape[0] // images
    fill_index(index_ref, padded_ref)
    for b in range(images):
        hot = turned_hot(index_ref, padded_ref, b, slots, padded)
        rows = slice(b * padded, (b + 1) * padded)
        picked_ref[rows, :] = dot(hot, tokens_ref[b], ((0,), (0,))).astype(bf16)
        grad_picked_ref[rows, :] = dot(hot, cotangent_ref[b], ((0,), (0,))).astype(bf16)
    picked = picked_ref[...].astype(f32)
    router = jax.nn.sigmoid(jnp.sum(picked * line(router_w_ref), axis=-1, keepdims=True))
    router_ref[...] = router
    normed, _ = norm_stats(picked)
    first_ref[...] = (normed * line(gain_ref) + line(shift_ref)).astype(bf16)
    scale = live_column(count_ref, images, padded) * router
    grad_branch = scale * grad_picked_ref[...].astype(f32)
    grad_mlp_ref[...] = grad_branch.astype(bf16)
    fc2_bias_grad_ref[...] = column_sum(grad_branch)


def stacked_heads(pair):
    lane = lax.broadcasted_iota(jnp.int32, pair.shape, 1)
    zero = jnp.zeros_like(pair)
    return jnp.concatenate(
        [jnp.where(lane < HEAD_DIM, pair, zero), jnp.where(lane < HEAD_DIM, zero, pair)], axis=0
    )


def joined_heads(stacked):
    half = stacked.shape[0] // 2
    lane = lax.broadcasted_iota(jnp.int32, (half, stacked.shape[1]), 1)
    return jnp.where(lane < HEAD_DIM, stacked[:half], stacked[half:])


def pair_probs(queries, keys, count):
    scores = dot_turned(queries, keys) * HEAD_DIM ** (-0.5)
    lane = lax.broadcasted_iota(jnp.int32, scores.shape, 1)
    scores = jnp.where(lane < count, scores, -1e30)
    raised = jnp.exp(scores - jnp.max(scores, axis=-1, keepdims=True))
    return raised * (1.0 / jnp.sum(raised, axis=-1, keepdims=True))


def attention_kernel(
    count_ref,
    first_ref,
    qkv_own_ref,
    qkv_other_ref,
    proj_own_ref,
    proj_other_ref,
    picked_ref,
    proj_bias_ref,
    gain_ref,
    shift_ref,
    made_own_ref,
    made_other_ref,
    mixed_own_ref,
    mixed_other_ref,
    attention_ref,
    second_ref,
):
    images = count_ref.shape[0]
    padded = first_ref.shape[0] // images
    local = qkv_own_ref.shape[2]
    total = line(proj_bias_ref)
    for side in range(SIDES):
        w_ref = (qkv_own_ref, qkv_other_ref)[side]
        made_ref = (made_own_ref, made_other_ref)[side]
        mixed_ref = (mixed_own_ref, mixed_other_ref)[side]
        for t in range(3):
            made_ref[:, t * local : (t + 1) * local] = dot(first_ref[...], w_ref[t]).astype(
                bf16
            )
        for b in range(images):
            rows = slice(b * padded, (b + 1) * padded)
            for at in range(0, local, 2 * HEAD_DIM):
                q, k, v = (
                    made_ref[rows, t * local + at : t * local + at + 2 * HEAD_DIM]
                    for t in range(3)
                )
                probs = pair_probs(stacked_heads(q), k, count_ref[b]).astype(bf16)
                mixed_ref[rows, at : at + 2 * HEAD_DIM] = joined_heads(dot(probs, v)).astype(bf16)
        total = total + dot(mixed_ref[...], (proj_own_ref, proj_other_ref)[side][...])
    attention_ref[...] = total
    normed, _ = norm_stats(picked_ref[...].astype(f32) + total)
    second_ref[...] = (normed * line(gain_ref) + line(shift_ref)).astype(bf16)


def mlp_kernel(second_ref, w_fc1_ref, bias_ref, grad_mlp_ref, w_fc2_ref, *refs):
    begin_refs, (both_ref, unit_sum_ref, mlp_ref, grad_second_ref) = refs[:-4], refs[-4:]
    units = w_fc1_ref.shape[1]
    for at in range(0, units, UNIT_BLOCK):
        block = slice(at, at + UNIT_BLOCK)
        pre = dot(second_ref[...], w_fc1_ref[:, block]) + bias_ref[block].reshape(1, -1)
        half = 0.5 * (1.0 + lax.erf(pre * root_half))
        act = (pre * half).astype(bf16)
        both_ref[0, :, block] = act
        slope = half + pre * inv_root_two_pi * jnp.exp(-0.5 * pre * pre)
        grad_pre = dot_turned(grad_mlp_ref[...], w_fc2_ref[block, :]) * slope
        unit_sum_ref[block] = column_sum(grad_pre).reshape(UNIT_BLOCK)
        both_ref[1, :, block] = grad_pre.astype(bf16)
    mlp_out = dot(both_ref[0], w_fc2_ref[...])
    grad_second = dot_turned(both_ref[1], w_fc1_ref[...])
    if len(begin_refs) == 1:
        mlp_ref[...] = mlp_out + line(begin_refs[0])
        grad_second_ref[...] = grad_second
    else:
        mlp_ref[...] = mlp_out + begin_refs[0][...]
        grad_second_ref[...] = grad_second + begin_refs[1][...]


def mlp(second, grad_mlp, w_fc1, bias, w_fc2, begin):
    rows, width = second.shape
    units = (w_fc1.value if isinstance(w_fc1, Far) else w_fc1).shape[1]
    return call(
        mlp_kernel,
        [
            shape((2, rows, units), bf16),
            shape((units,), f32),
            shape((rows, width), f32),
            shape((rows, width), f32),
        ],
        (second, w_fc1, bias, grad_mlp, w_fc2, *begin),
        us=6,
    )


TOP_BITS = 4
UNITS = 1 << TOP_BITS


def my_bits():
    place = lax.axis_index("dp") >> (lax.axis_size("dp").bit_length() - 1 - TOP_BITS)
    return [(place >> bit) & 1 for bit in range(TOP_BITS)]


def order_of(part):
    return [(part + j) % 3 for j in range(3)] + [3]


def bits_left(part, step):
    return [bit for bit in range(TOP_BITS - 1, -1, -1) if bit not in order_of(part)[:step]]


def unit_rows(ref, spread, chosen, unit):
    place = 0
    for bit in spread:
        place = place * 2 + chosen[bit]
    return ref[pl.ds(pl.multiple_of(place * unit, 16), unit), :]


def every_choice(bits):
    for j in range(1 << len(bits)):
        yield j, {bit: (j >> (len(bits) - 1 - i)) & 1 for i, bit in enumerate(bits)}


def arrange_rows(turned_ref, mine, part, arranged_ref):
    unit = turned_ref.shape[0] // UNITS
    bit = order_of(part)[0]
    for side, value in enumerate((1 - mine[bit], mine[bit])):
        for j, chosen in every_choice(bits_left(part, 1)):
            chosen[bit] = value
            to = (side * UNITS // 2 + j) * unit
            arranged_ref[to : to + unit, :] = unit_rows(
                turned_ref, bits_left(part, 0), chosen, unit
            )


def term_sum(terms, part, chosen, unit):
    total = 0.0
    for n, ref in enumerate(terms):
        total = total + unit_rows(ref, bits_left(part, max(n, 1)), chosen, unit).astype(f32)
    return total


def step_kernel(step, unit, *refs):
    mine = my_bits()
    for part in range(3):
        terms = refs[part * (step + 1) : (part + 1) * (step + 1)]
        outs = refs[3 * (step + 1) :]
        order = order_of(part)
        for j, chosen in every_choice(bits_left(part, step + 1)):
            for bit in order[1:step]:
                chosen[bit] = mine[bit]
            chosen[order[step]] = 1 - mine[order[step]]
            value = term_sum(terms, part, chosen, unit).astype(bf16)
            if len(outs) == 1:
                outs[0][part * unit : (part + 1) * unit, :] = value
            else:
                outs[part][j * unit : (j + 1) * unit, :] = value


def joined_sums(refs, unit):
    mine = my_bits()
    last = refs[3 * TOP_BITS]
    for part in range(3):
        terms = refs[part * TOP_BITS : (part + 1) * TOP_BITS]
        chosen = {bit: mine[bit] for bit in range(TOP_BITS)}
        total = term_sum(terms, part, chosen, unit)
        yield part, total + last[part * unit : (part + 1) * unit, :].astype(f32)


def mlp_finish_kernel(*refs):
    fc2_ref, fc1_ref = refs[-2:]
    for part, total in joined_sums(refs, fc1_ref.shape[0]):
        at = slice(part * UNIT_BLOCK, (part + 1) * UNIT_BLOCK)
        fc2_ref[:, at] = total[:, :UNIT_BLOCK]
        fc1_ref[:, at] = total[:, UNIT_BLOCK:]


def attn_finish_kernel(*refs):
    qkv_ref, proj_ref = refs[-2:]
    local = qkv_ref.shape[2]
    third = local // 3
    for part, total in joined_sums(refs, proj_ref.shape[0]):
        qkv_ref[part] = total[:, :local]
        proj_ref[:, part * third : (part + 1) * third] = total[:, local:]


def both_rows(own, other):
    return jnp.concatenate([own, other], axis=0)


def weight_tile(arranged_ref, right, away_ref, kept_ref, columns):
    half = away_ref.shape[0]
    away_ref[:, columns] = dot(arranged_ref[:half, :], right).astype(bf16)
    kept_ref[:, columns] = dot(arranged_ref[half:, :], right)


def mlp_weights_kernel(
    grad_mlp_own_ref,
    grad_mlp_par_ref,
    second_own_ref,
    second_par_ref,
    both_own_ref,
    both_par_ref,
    *outs,
):
    away_refs, kept_refs, (turned_ref, arranged_ref) = outs[:3], outs[3:6], outs[6:]
    mine = my_bits()
    for which, (own_ref, par_ref) in enumerate(
        ((grad_mlp_own_ref, grad_mlp_par_ref), (second_own_ref, second_par_ref))
    ):
        turned_ref[...] = both_rows(own_ref[...], par_ref[...]).T
        for part in range(3):
            at = slice(part * UNIT_BLOCK, (part + 1) * UNIT_BLOCK)
            right = both_rows(both_own_ref[which, :, at], both_par_ref[which, :, at])
            arrange_rows(turned_ref, mine, part, arranged_ref)
            columns = slice(which * UNIT_BLOCK, (which + 1) * UNIT_BLOCK)
            weight_tile(arranged_ref, right, away_refs[part], kept_refs[part], columns)


def attn_weights_kernel(
    first_own_ref,
    first_par_ref,
    grad_attn_own_ref,
    grad_attn_par_ref,
    qkv_own_ref,
    qkv_par_ref,
    mixed_own_ref,
    mixed_par_ref,
    *outs,
):
    away_refs, kept_refs, (turned_ref, arranged_ref) = outs[:3], outs[3:6], outs[6:]
    mine = my_bits()
    local = mixed_own_ref.shape[1]
    third = local // 3
    turned_ref[...] = both_rows(first_own_ref[...], first_par_ref[...]).T
    for part in range(3):
        at = slice(part * local, (part + 1) * local)
        right = both_rows(qkv_own_ref[:, at], qkv_par_ref[:, at])
        arrange_rows(turned_ref, mine, part, arranged_ref)
        weight_tile(arranged_ref, right, away_refs[part], kept_refs[part], slice(0, local))
    turned_ref[...] = both_rows(grad_attn_own_ref[...], grad_attn_par_ref[...]).T
    for part in range(3):
        at = slice(part * third, (part + 1) * third)
        right = both_rows(mixed_own_ref[:, at], mixed_par_ref[:, at])
        arrange_rows(turned_ref, mine, part, arranged_ref)
        weight_tile(
            arranged_ref, right, away_refs[part], kept_refs[part], slice(local, local + third)
        )


def weights(kernel, arrays, width, depth, columns, us):
    half = width // 2
    return call(
        kernel,
        [shape((half, columns), bf16)] * 3 + [shape((half, columns), f32)] * 3,
        arrays,
        scratch=[pltpu.VMEM((width, depth), bf16), pltpu.VMEM((width, depth), bf16)],
        us=us,
    )


def small_finish_kernel(left_ref, right_ref, *outs):
    total = left_ref[...] + right_ref[...]
    width = total.shape[1]
    for i, out_ref in enumerate(outs[:-1]):
        out_ref[...] = total[i : i + 1, :].reshape(width)
    for i in range(total.shape[0] - 7):
        outs[-1][i * width : (i + 1) * width] = total[7 + i : 8 + i, :].reshape(width)


def heads_back(count_ref, grad_attn_ref, proj_ref, made_ref, out_ref, mixed_scratch):
    images = count_ref.shape[0]
    padded = made_ref.shape[0] // images
    local = proj_ref.shape[0]
    factor = HEAD_DIM ** (-0.5)
    mixed_scratch[...] = dot_turned(grad_attn_ref[...], proj_ref[...]).astype(bf16)
    for b in range(images):
        rows = slice(b * padded, (b + 1) * padded)
        for at in range(0, local, 2 * HEAD_DIM):
            q, k, v = (
                made_ref[rows, t * local + at : t * local + at + 2 * HEAD_DIM] for t in range(3)
            )
            q = stacked_heads(q)
            grad_mixed = stacked_heads(mixed_scratch[rows, at : at + 2 * HEAD_DIM])
            probs = pair_probs(q, k, count_ref[b])
            grad_probs = dot_turned(grad_mixed, v)
            row_dot = jnp.sum(probs * grad_probs, axis=-1, keepdims=True)
            grad_scores = (probs * (grad_probs - row_dot)).astype(bf16)
            found = (
                joined_heads(dot(grad_scores, k)) * factor,
                dot(grad_scores, q, ((0,), (0,))) * factor,
                dot(probs.astype(bf16), grad_mixed, ((0,), (0,))),
            )
            for t in range(3):
                to = slice(t * local + at, t * local + at + 2 * HEAD_DIM)
                out_ref[rows, to] = found[t].astype(bf16)


def back_other_kernel(
    count_ref,
    grad_second_ref,
    picked_ref,
    attention_ref,
    grad_picked_ref,
    router_ref,
    gain_ref,
    made_ref,
    proj_ref,
    grad_attn_ref,
    grad_hidden_ref,
    out_ref,
    sums_ref,
    mixed_scratch,
):
    images = count_ref.shape[0]
    padded = picked_ref.shape[0] // images
    normed, inv_std = norm_stats(picked_ref[...].astype(f32) + attention_ref[...])
    grad_second = grad_second_ref[...]
    grad_hidden = norm_back(grad_second, line(gain_ref), normed, inv_std)
    grad_hidden_ref[...] = grad_hidden
    scale = live_column(count_ref, images, padded) * router_ref[...]
    grad_attention = scale * grad_picked_ref[...].astype(f32) + grad_hidden
    grad_attn_ref[...] = grad_attention.astype(bf16)
    sums_ref[0:1, :] = column_sum(grad_attention)
    sums_ref[1:2, :] = column_sum(grad_second * normed)
    sums_ref[2:3, :] = column_sum(grad_second)
    heads_back(count_ref, grad_attn_ref, proj_ref, made_ref, out_ref, mixed_scratch)


def last_kernel(
    count_ref,
    index_ref,
    tokens_ref,
    cotangent_ref,
    picked_ref,
    grad_picked_ref,
    router_ref,
    attention_ref,
    mlp_ref,
    grad_hidden_ref,
    grad_qkv_own_ref,
    grad_qkv_other_ref,
    qkv_own_ref,
    qkv_other_ref,
    gain_ref,
    router_w_ref,
    fc2_bias_grad_ref,
    back_sums_ref,
    unit_own_ref,
    unit_other_ref,
    output_ref,
    input_grad_ref,
    keep_ref,
    send_ref,
    padded_ref,
):
    images, slots, width = tokens_ref.shape
    padded = picked_ref.shape[0] // images
    local = qkv_own_ref.shape[2]
    fill_index(index_ref, padded_ref)
    grad_first = jnp.zeros(picked_ref.shape, f32)
    for side in range(SIDES):
        for t in range(3):
            grad_first = grad_first + dot_turned(
                (grad_qkv_own_ref, grad_qkv_other_ref)[side][:, t * local : (t + 1) * local],
                (qkv_own_ref, qkv_other_ref)[side][t],
            )
    picked = picked_ref[...].astype(f32)
    router = router_ref[...]
    scale = live_column(count_ref, images, padded) * router
    branch = attention_ref[...] + mlp_ref[...]
    grad_logit = (
        scale
        * (1.0 - router)
        * jnp.sum(grad_picked_ref[...].astype(f32) * branch, axis=-1, keepdims=True)
    )
    normed, inv_std = norm_stats(picked)
    grad_kept = (
        norm_back(grad_first, line(gain_ref), normed, inv_std)
        + grad_hidden_ref[...]
        + grad_logit * line(router_w_ref)
    )
    sums = (
        column_sum(grad_first * normed),
        column_sum(grad_first),
        back_sums_ref[0:1, :],
        back_sums_ref[1:2, :],
        back_sums_ref[2:3, :],
        fc2_bias_grad_ref[...],
        column_sum(grad_logit * picked),
    )
    for i, values in enumerate(sums):
        keep_ref[i : i + 1, :] = values
        send_ref[i : i + 1, :] = values
    for i in range(unit_own_ref.shape[0] // width):
        at = slice(i * width, (i + 1) * width)
        keep_ref[7 + i : 8 + i, :] = unit_own_ref[at].reshape(1, width)
        send_ref[7 + i : 8 + i, :] = unit_other_ref[at].reshape(1, width)
    for update, base_ref, out_ref in (
        (scale * branch, tokens_ref, output_ref),
        (grad_kept, cotangent_ref, input_grad_ref),
    ):
        high = update.astype(bf16)
        low = (update - high.astype(f32)).astype(bf16)
        for b in range(images):
            hot = turned_hot(index_ref, padded_ref, b, slots, padded)
            rows = slice(b * padded, (b + 1) * padded)
            updated = base_ref[b].astype(f32) + (dot(hot, high[rows]) + dot(hot, low[rows]))
            out_ref[b] = updated.astype(bf16)
        out_ref.leave()


def other_core(value):
    return lax.ppermute(value, "head", [(0, 1), (1, 0)])


def partners(count, bit):
    return [(i, i ^ (1 << bit)) for i in range(count)]


class Halving:
    def __init__(self, halves, count):
        self.shift, self.count = count.bit_length() - 1 - TOP_BITS, count
        self.unit = halves[0].shape[0] * 2 // UNITS
        self.columns = halves[0].shape[1]
        self.terms = [[kept] for kept in halves[3:]]
        self.away, self.step, self.last = list(halves[:3]), 0, None

    def swap(self, part):
        bit = order_of(part)[self.step] + self.shift
        return partners(self.count, bit)

    def send(self):
        if self.step == 3:
            self.last = lax.ppermute(self.away[0], "dp", self.swap(0))
        else:
            for part in range(3):
                got = lax.ppermute(self.away[part], "dp", self.swap(part))
                self.terms[part].append(got)
        self.step += 1

    def flat(self):
        return tuple(term for terms in self.terms for term in terms)

    def next(self, after):
        flat, after = lax.optimization_barrier((self.flat(), after))
        rows = self.unit * UNITS >> (self.step + 1)
        outs = [shape((rows, self.columns), bf16)] * 3
        if self.step == 3:
            outs = [shape((3 * self.unit, self.columns), bf16)]
        self.away = call(
            functools.partial(step_kernel, self.step, self.unit), outs, flat, us=1
        )
        self.away, after = lax.optimization_barrier((self.away, after))
        self.send()
        return after

    def finish(self, kernel, outs):
        return call(kernel, [Far(out) for out in outs], (*self.flat(), self.last), us=1)


def fewer_rows(grad, count, axis):
    place = lax.axis_index("dp")
    for bit in range(count.bit_length() - 2 - TOP_BITS, -1, -1):
        half = grad.shape[axis] // 2
        mine = (place >> bit) & 1
        away = lax.dynamic_slice_in_dim(grad, (1 - mine) * half, half, axis).astype(bf16)
        kept = lax.dynamic_slice_in_dim(grad, mine * half, half, axis)
        grad = kept + lax.ppermute(away, "dp", partners(count, bit)).astype(f32)
    return grad


def on_device(
    tokens,
    kept_index,
    kept_count,
    ln1_gain,
    ln1_bias,
    w_qkv,
    w_proj,
    proj_bias,
    ln2_gain,
    ln2_bias,
    w_fc1,
    fc1_bias,
    w_fc2,
    fc2_bias,
    w_router,
    cotangent,
):
    images, slots, width = tokens.shape
    padded = rows_of(kept_index.shape[1])
    rows = images * padded
    local = w_qkv.shape[2]
    units = w_fc1.shape[1]
    count = lax.axis_size("dp")

    w_qkv_other = other_core(w_qkv)
    w_proj_other = other_core(w_proj)
    w_fc1_other = other_core(w_fc1)
    bias_other = other_core(fc1_bias)
    w_fc2_other = other_core(w_fc2)
    index_scratch = pltpu.VMEM((8, 128), jnp.int32)

    picked, grad_picked, first, grad_mlp, router, fc2_bias_sum = call(
        front_kernel,
        [
            shape((rows, width), bf16),
            shape((rows, width), bf16),
            shape((rows, width), bf16),
            shape((rows, width), bf16),
            shape((rows, 1), f32),
            shape((1, width), f32),
        ],
        (kept_count, Far(kept_index), Far(tokens), Far(cotangent), Far(w_router), Far(ln1_gain), Far(ln1_bias)),
        scalars=1,
        scratch=[index_scratch],
        us=3,
    )
    first_par = other_core(first)
    grad_mlp_par = other_core(grad_mlp)

    made, made_other, mixed, mixed_other, attention, second = call(
        attention_kernel,
        [
            shape((rows, 3 * local), bf16),
            shape((rows, 3 * local), bf16),
            shape((rows, local), bf16),
            shape((rows, local), bf16),
            shape((rows, width), f32),
            shape((rows, width), bf16),
        ],
        (
            kept_count,
            first,
            Far(w_qkv),
            w_qkv_other,
            Far(w_proj),
            w_proj_other,
            picked,
            Far(proj_bias),
            Far(ln2_gain),
            Far(ln2_bias),
        ),
        scalars=1,
        us=7,
    )
    mixed_par = other_core(mixed_other)
    second_par = other_core(second)

    both_other, unit_other, mlp_out, grad_second = mlp(
        second, grad_mlp, w_fc1_other, bias_other, w_fc2_other, (Far(fc2_bias),)
    )
    both_par = other_core(both_other)
    both_own, unit_own, mlp_out, grad_second = mlp(
        second, grad_mlp, Far(w_fc1), Far(fc1_bias), Far(w_fc2), (mlp_out, grad_second)
    )
    mlp_halves = weights(
        mlp_weights_kernel,
        (grad_mlp, grad_mlp_par, second, second_par, both_own, both_par),
        width,
        2 * rows,
        2 * UNIT_BLOCK,
        8,
    )
    mlp_halves, grad_second = lax.optimization_barrier((mlp_halves, grad_second))
    mlp_sums = Halving(mlp_halves, count)
    mlp_sums.send()

    grad_attn, grad_hidden, grad_qkv_other, back_sums = call(
        back_other_kernel,
        [
            shape((rows, width), bf16),
            shape((rows, width), f32),
            shape((rows, 3 * local), bf16),
            shape((8, width), f32),
        ],
        (
            kept_count,
            grad_second,
            picked,
            attention,
            grad_picked,
            router,
            Far(ln2_gain),
            made_other,
            w_proj_other,
        ),
        scalars=1,
        scratch=[pltpu.VMEM((rows, local), bf16)],
        us=7,
    )
    grad_attn_par = other_core(grad_attn)
    grad_qkv_par = other_core(grad_qkv_other)
    (grad_qkv,) = call(
        heads_back,
        [shape((rows, 3 * local), bf16)],
        (kept_count, grad_attn, Far(w_proj), made),
        scalars=1,
        scratch=[pltpu.VMEM((rows, local), bf16)],
        us=6,
    )
    grad_qkv = mlp_sums.next(grad_qkv)
    attn_halves = weights(
        attn_weights_kernel,
        (first, first_par, grad_attn, grad_attn_par, grad_qkv, grad_qkv_par, mixed, mixed_par),
        width,
        2 * rows,
        local + local // 3,
        5,
    )
    attn_halves, grad_qkv = lax.optimization_barrier((attn_halves, grad_qkv))
    attn_sums = Halving(attn_halves, count)
    attn_sums.send()

    sum_rows = 7 + units // width
    output, input_grad, keep, send = call(
        last_kernel,
        [
            Far(shape(tokens.shape, bf16)),
            Far(shape(tokens.shape, bf16)),
            shape((sum_rows, width), f32),
            shape((sum_rows, width), f32),
        ],
        (
            kept_count,
            Far(kept_index),
            Far(tokens),
            Far(cotangent),
            picked,
            grad_picked,
            router,
            attention,
            mlp_out,
            grad_hidden,
            grad_qkv,
            grad_qkv_other,
            Far(w_qkv),
            w_qkv_other,
            Far(ln1_gain),
            Far(w_router),
            fc2_bias_sum,
            back_sums,
            unit_own,
            unit_other,
        ),
        scalars=1,
        scratch=[index_scratch],
        us=7,
    )
    keep = mlp_sums.next(keep)
    keep = attn_sums.next(keep)
    keep = mlp_sums.next(keep)
    keep = attn_sums.next(keep)
    keep = attn_sums.next(keep)
    small = keep + other_core(send)
    steps = count.bit_length() - 1
    for bit in range(steps - 1):
        small = small + lax.ppermute(small, "dp", partners(count, bit))
    sums = call(
        small_finish_kernel,
        [Far(shape((width,), f32))] * 7 + [Far(shape((units,), f32))],
        (small, lax.ppermute(small, "dp", partners(count, steps - 1))),
    )
    unit = width // UNITS
    fc2_turned, fc1_grad = mlp_sums.finish(
        mlp_finish_kernel, [shape((unit, units), f32), shape((unit, units), f32)]
    )
    qkv_grad, proj_turned = attn_sums.finish(
        attn_finish_kernel, [shape((3, unit, local), f32), shape((unit, local), f32)]
    )
    fc2_turned, fc1_grad, proj_turned = (
        fewer_rows(grad, count, 0) for grad in (fc2_turned, fc1_grad, proj_turned)
    )
    qkv_grad = fewer_rows(qkv_grad, count, 1)
    return (
        output,
        input_grad,
        sums[0],
        sums[1],
        qkv_grad,
        proj_turned.T,
        sums[2],
        sums[3],
        sums[4],
        fc1_grad,
        sums[7],
        fc2_turned.T,
        sums[5],
        sums[6],
    )


def solution(mesh):
    batch = ("dp", "head")
    return jax.shard_map(
        on_device,
        mesh=mesh,
        in_specs=(
            P(batch, None, None),
            P(batch, None),
            P(batch),
            P(),
            P(),
            P(None, None, "head"),
            P("head", None),
            P(),
            P(),
            P(),
            P(None, "head"),
            P("head"),
            P("head", None),
            P(),
            P(),
            P(batch, None, None),
        ),
        out_specs=(
            P(batch, None, None),
            P(batch, None, None),
            P(),
            P(),
            P(None, "dp", "head"),
            P("head", "dp"),
            P(),
            P(),
            P(),
            P("dp", "head"),
            P("head"),
            P("head", "dp"),
            P(),
            P(),
        ),
        check_vma=False,
    )
```

```python
import functools

import jax
import jax.numpy as jnp
from jax import lax
from jax.experimental import pallas as pl
from jax.experimental.pallas import tpu as pltpu
from jax.sharding import PartitionSpec as P

HEAD_DIM = 64
norm_eps = 1e-06
root_half = 0.7071067811865476
inv_root_two_pi = 0.3989422804014327
f32, bf16 = jnp.float32, jnp.bfloat16


MIB = 1024 * 1024
SIDES = 2
FLOPS = 1
UNIT_BLOCK = 512


def rows_of(count):
    return -(-count // 16) * 16


def norm_stats(values):
    row_mean = jnp.mean(values, axis=-1, keepdims=True)
    centered = values - row_mean
    inv_std = lax.rsqrt(jnp.mean(centered * centered, axis=-1, keepdims=True) + norm_eps)
    return centered * inv_std, inv_std


def norm_back(grad_normed, gain, normed, inv_std):
    unit = grad_normed * gain
    return inv_std * (
        unit
        - jnp.mean(unit, axis=-1, keepdims=True)
        - normed * jnp.mean(unit * normed, axis=-1, keepdims=True)
    )


def dot(a, b, over=((1,), (0,))):
    return lax.dot_general(a, b, (over, ((), ())), preferred_element_type=f32)


def dot_turned(a, b):
    return dot(a, b, ((1,), (1,)))


def column_sum(values):
    return jnp.sum(values, axis=0, keepdims=True)


class Held:
    def __init__(self, ref, copy):
        self.ref, self.copy, self.shape = ref, copy, ref.shape

    def ready(self):
        if self.copy is not None:
            self.copy.wait()
            self.copy = None
        return self.ref

    def __getitem__(self, at):
        return self.ready()[at]


class Made:
    def __init__(self, ref, copy):
        self.ref, self.copy, self.shape, self.left = ref, copy, ref.shape, False

    def __getitem__(self, at):
        return self.ref[at]

    def __setitem__(self, at, value):
        self.ref[at] = value

    def leave(self):
        if not self.left:
            self.copy.start()
            self.left = True


class Far:
    def __init__(self, value):
        self.value = value


def call(kernel, out_shape, inputs, scratch=(), fetch=(), room=14):
    inputs = [*inputs, *[Far(x) for x in fetch]]
    values = [x.value if isinstance(x, Far) else x for x in inputs]
    shapes = [x.value if isinstance(x, Far) else x for x in out_shape]
    shapes += [shape(x.shape, x.dtype) for x in fetch]
    n_fetch, n_in, n_out = len(fetch), len(inputs), len(shapes)
    far_in = [i for i in range(n_in - n_fetch) if isinstance(inputs[i], Far)]
    far_out = [i for i, x in enumerate(out_shape) if isinstance(x, Far)]
    near, away = pl.BlockSpec(memory_space=pltpu.VMEM), pl.BlockSpec(memory_space=pltpu.HBM)
    in_hbm = [isinstance(x, Far) for x in inputs]

    def body(*refs):
        ins, outs, refs = list(refs[:n_in]), list(refs[n_in : n_in + n_out]), refs[n_in + n_out :]
        in_refs, refs = refs[: len(far_in)], refs[len(far_in) :]
        out_refs, refs = refs[: len(far_out)], refs[len(far_out) :]
        sems, extra = (refs[0], refs[1:]) if n_sems else (None, refs)
        for n, i in enumerate(far_in):
            copy = pltpu.make_async_copy(ins[i], in_refs[n], sems.at[n])
            copy.start()
            ins[i] = Held(in_refs[n], copy)
        for n, i in enumerate(far_out):
            copy = pltpu.make_async_copy(out_refs[n], outs[i], sems.at[len(far_in) + n])
            outs[i] = Made(out_refs[n], copy)
        fetched = []
        for n in range(n_fetch):
            copy = pltpu.make_async_copy(
                ins[n_in - n_fetch + n],
                outs[n_out - n_fetch + n],
                sems.at[len(far_in) + len(far_out) + n],
            )
            copy.start()
            fetched.append(copy)
        kernel(*ins[: n_in - n_fetch], *outs[: n_out - n_fetch], *extra)
        for i in far_in:
            ins[i].ready()
        for i in far_out:
            outs[i].leave()
        for copy in fetched:
            copy.wait()
        for i in far_out:
            outs[i].copy.wait()

    def landing(x):
        return (pltpu.SMEM if x.dtype == jnp.int32 and x.ndim == 1 else pltpu.VMEM)(x.shape, x.dtype)

    far_scratch = [landing(values[i]) for i in far_in]
    far_scratch += [pltpu.VMEM(shapes[i].shape, shapes[i].dtype) for i in far_out]
    n_sems = len(far_in) + len(far_out) + n_fetch
    if n_sems:
        far_scratch.append(pltpu.SemaphoreType.DMA((n_sems,)))
    values = [
        pltpu.with_memory_space_constraint(x, pltpu.HBM if far else pltpu.VMEM)
        for x, far in zip(values, in_hbm)
    ]
    return pl.pallas_call(
        body,
        out_shape=[
            (pltpu.HBM if i in far_out else pltpu.VMEM)(o.shape, o.dtype)
            for i, o in enumerate(shapes)
        ],
        in_specs=[away if far else near for far in in_hbm],
        out_specs=[away if i in far_out else near for i in range(n_out)],
        scratch_shapes=[*far_scratch, *scratch],
        compiler_params=pltpu.CompilerParams(vmem_limit_bytes=room * MIB),
        cost_estimate=pl.CostEstimate(flops=FLOPS, bytes_accessed=1, transcendentals=0),
    )(*values)


def line(ref):
    return ref[...].reshape(1, -1)


def shape(dims, kind):
    return jax.ShapeDtypeStruct(dims, kind)


def live_column(count_ref, images, padded):
    rows = lax.broadcasted_iota(jnp.int32, (padded, 1), 0)
    return jnp.concatenate(
        [jnp.where(rows < count_ref[b], 1.0, 0.0).astype(f32) for b in range(images)], axis=0
    )


def turned_hot(index_ref, padded_ref, image, slots, padded):
    wide = padded_ref[image : image + 1, :padded]
    place = lax.broadcasted_iota(jnp.int32, (slots, padded), 0)
    return jnp.where(place == wide, 1.0, 0.0).astype(bf16)


def fill_index(index_ref, padded_ref):
    padded_ref[...] = jnp.full(padded_ref.shape, -1, jnp.int32)
    padded_ref[: index_ref.shape[0], : index_ref.shape[1]] = index_ref[...]


def pick_rows(index_ref, source_ref, rows_ref, padded_ref):
    images, slots, _ = source_ref.shape
    padded = rows_ref.shape[0] // images
    fill_index(index_ref, padded_ref)
    for b in range(images):
        hot = turned_hot(index_ref, padded_ref, b, slots, padded)
        rows = slice(b * padded, (b + 1) * padded)
        rows_ref[rows, :] = dot(hot, source_ref[b], ((0,), (0,))).astype(bf16)


def front_kernel(
    index_ref,
    tokens_ref,
    router_w_ref,
    gain_ref,
    shift_ref,
    picked_ref,
    first_ref,
    router_ref,
    padded_ref,
):
    pick_rows(index_ref, tokens_ref, picked_ref, padded_ref)
    picked = picked_ref[...].astype(f32)
    router_ref[...] = jax.nn.sigmoid(jnp.sum(picked * line(router_w_ref), axis=-1, keepdims=True))
    normed, _ = norm_stats(picked)
    first_ref[...] = (normed * line(gain_ref) + line(shift_ref)).astype(bf16)


def grad_front_kernel(
    count_ref,
    index_ref,
    cotangent_ref,
    router_ref,
    grad_picked_ref,
    grad_mlp_ref,
    fc2_bias_grad_ref,
    padded_ref,
):
    images = cotangent_ref.shape[0]
    pick_rows(index_ref, cotangent_ref, grad_picked_ref, padded_ref)
    scale = live_column(count_ref, images, router_ref.shape[0] // images) * router_ref[...]
    grad_branch = scale * grad_picked_ref[...].astype(f32)
    grad_mlp_ref[...] = grad_branch.astype(bf16)
    fc2_bias_grad_ref[...] = column_sum(grad_branch)


def stacked_heads(pair):
    lane = lax.broadcasted_iota(jnp.int32, pair.shape, 1)
    zero = jnp.zeros_like(pair)
    return jnp.concatenate(
        [jnp.where(lane < HEAD_DIM, pair, zero), jnp.where(lane < HEAD_DIM, zero, pair)], axis=0
    )


def joined_heads(stacked):
    half = stacked.shape[0] // 2
    lane = lax.broadcasted_iota(jnp.int32, (half, stacked.shape[1]), 1)
    return jnp.where(lane < HEAD_DIM, stacked[:half], stacked[half:])


def pair_probs(queries, keys, count):
    scores = dot_turned(queries, keys) * HEAD_DIM ** (-0.5)
    lane = lax.broadcasted_iota(jnp.int32, scores.shape, 1)
    scores = jnp.where(lane < count, scores, -1e30)
    raised = jnp.exp(scores - jnp.max(scores, axis=-1, keepdims=True))
    return raised * (1.0 / jnp.sum(raised, axis=-1, keepdims=True))


def attention_kernel(
    count_ref,
    first_ref,
    qkv_own_ref,
    qkv_other_ref,
    proj_own_ref,
    proj_other_ref,
    picked_ref,
    proj_bias_ref,
    gain_ref,
    shift_ref,
    made_own_ref,
    made_other_ref,
    mixed_own_ref,
    mixed_other_ref,
    attention_ref,
    second_ref,
):
    images = count_ref.shape[0]
    padded = first_ref.shape[0] // images
    local = qkv_own_ref.shape[2]
    total = line(proj_bias_ref)
    for side in range(SIDES):
        w_ref = (qkv_own_ref, qkv_other_ref)[side]
        made_ref = (made_own_ref, made_other_ref)[side]
        mixed_ref = (mixed_own_ref, mixed_other_ref)[side]
        for t in range(3):
            made_ref[:, t * local : (t + 1) * local] = dot(first_ref[...], w_ref[t]).astype(
                bf16
            )
        for b in range(images):
            rows = slice(b * padded, (b + 1) * padded)
            for at in range(0, local, 2 * HEAD_DIM):
                q, k, v = (
                    made_ref[rows, t * local + at : t * local + at + 2 * HEAD_DIM]
                    for t in range(3)
                )
                probs = pair_probs(stacked_heads(q), k, count_ref[b]).astype(bf16)
                mixed_ref[rows, at : at + 2 * HEAD_DIM] = joined_heads(dot(probs, v)).astype(bf16)
        total = total + dot(mixed_ref[...], (proj_own_ref, proj_other_ref)[side][...])
    attention_ref[...] = total
    normed, _ = norm_stats(picked_ref[...].astype(f32) + total)
    second_ref[...] = (normed * line(gain_ref) + line(shift_ref)).astype(bf16)


def hidden_kernel(second_ref, w_fc1_ref, bias_ref, act_ref, slope_ref):
    for at in range(0, act_ref.shape[1], UNIT_BLOCK):
        block = slice(at, at + UNIT_BLOCK)
        pre = dot(second_ref[...], w_fc1_ref[:, block]) + bias_ref[block].reshape(1, -1)
        half = 0.5 * (1.0 + lax.erf(pre * root_half))
        act_ref[:, block] = (pre * half).astype(bf16)
        slope_ref[:, block] = half + pre * inv_root_two_pi * jnp.exp(-0.5 * pre * pre)


def hidden_back_kernel(grad_mlp_ref, w_fc2_ref, slope_ref, grad_pre_ref, unit_sum_ref):
    for at in range(0, slope_ref.shape[1], UNIT_BLOCK):
        block = slice(at, at + UNIT_BLOCK)
        grad_pre = dot_turned(grad_mlp_ref[...], w_fc2_ref[block, :]) * slope_ref[:, block]
        unit_sum_ref[block] = column_sum(grad_pre).reshape(UNIT_BLOCK)
        grad_pre_ref[:, block] = grad_pre.astype(bf16)


TOP_BITS = 4
UNITS = 1 << TOP_BITS


def my_bits():
    place = lax.axis_index("dp") >> (lax.axis_size("dp").bit_length() - 1 - TOP_BITS)
    return [(place >> bit) & 1 for bit in range(TOP_BITS)]


def order_of(part):
    return [(part + j) % 3 for j in range(3)] + [3]


def bits_left(part, step):
    return [bit for bit in range(TOP_BITS - 1, -1, -1) if bit not in order_of(part)[:step]]


def every_choice(bits):
    for j in range(1 << len(bits)):
        yield j, {bit: (j >> (len(bits) - 1 - i)) & 1 for i, bit in enumerate(bits)}


def unit_rows(ref, spread, chosen, unit, base=0):
    place = 0
    for bit in spread:
        place = place * 2 + chosen[bit]
    return ref[pl.ds(pl.multiple_of(base + place * unit, 16), unit), :]


def arrange_rows(turned_ref, mine, part, arranged_ref):
    unit = turned_ref.shape[0] // UNITS
    bit = order_of(part)[0]
    for side, value in enumerate((1 - mine[bit], mine[bit])):
        for j, chosen in every_choice(bits_left(part, 1)):
            chosen[bit] = value
            to = (side * UNITS // 2 + j) * unit
            arranged_ref[to : to + unit, :] = unit_rows(
                turned_ref, bits_left(part, 0), chosen, unit
            )


class Stream:
    def __init__(self, part, away, kept):
        self.part, self.step, self.away, self.terms = part, 0, away, [(kept, 0, 1)]
        self.unit = kept.shape[0] * 2 // UNITS

    def bit(self):
        return order_of(self.part)[self.step]

    def rows(self):
        return self.unit * UNITS >> (self.step + 1)

    def sent(self, got, base):
        self.step += 1
        self.away = None
        self.terms.append((got, base, self.step))


def listed(streams):
    arrays, plans = [], []
    for stream in streams:
        terms = [(stream.away, 0, 0)] if stream.away is not None else stream.terms
        plan = []
        for array, base, step in terms:
            found = [n for n, x in enumerate(arrays) if x is array]
            if not found:
                found = [len(arrays)]
                arrays.append(array)
            plan.append((found[0], base, step))
        plans.append(plan)
    return arrays, plans


def plan_sum(refs, plan, part, chosen, unit):
    total = 0.0
    for n, base, step in plan:
        total = total + unit_rows(refs[n], bits_left(part, step), chosen, unit, base).astype(f32)
    return total


def step_kernel(n_arrays, n_small, plans, *refs):
    mine = my_bits()
    small, outs = refs[n_arrays : n_arrays + n_small], refs[n_arrays + n_small :]
    if n_small:
        outs[-1][...] = sum(ref[...] for ref in small)
    for part, step, made, unit, plan, out, base in plans:
        order = order_of(part)
        if made:
            ref = refs[plan[0][0]]
            outs[out][base : base + ref.shape[0], :] = ref[...]
            continue
        for j, chosen in every_choice(bits_left(part, step + 1)):
            for bit in order[:step]:
                chosen[bit] = mine[bit]
            chosen[order[step]] = 1 - mine[order[step]]
            to = base + j * unit
            outs[out][to : to + unit, :] = plan_sum(refs, plan, part, chosen, unit).astype(bf16)


def finish_kernel(n_arrays, n_small, plans, *refs):
    mine = my_bits()
    chosen = {bit: mine[bit] for bit in range(TOP_BITS)}
    small, refs_out = refs[n_arrays : n_arrays + n_small], refs[n_arrays + n_small :]
    fc2_ref, fc1_ref, qkv_ref, proj_ref, *outs = refs_out
    local = qkv_ref.shape[2]
    third = local // 3
    for i, (part, unit, plan) in enumerate(plans):
        total = plan_sum(refs, plan, part, chosen, unit)
        if i < 6:
            (fc2_ref, fc1_ref)[i // 3][:, part * UNIT_BLOCK : (part + 1) * UNIT_BLOCK] = total
        else:
            qkv_ref[part] = total[:, :local]
            proj_ref[:, part * third : (part + 1) * third] = total[:, local:]
        if i == 5:
            fc2_ref.leave()
            fc1_ref.leave()
    total = sum(ref[...] for ref in small)
    width = total.shape[1]
    for i, out_ref in enumerate(outs[:-1]):
        out_ref[...] = total[i : i + 1, :].reshape(width)
    for i in range(total.shape[0] - 7):
        outs[-1][i * width : (i + 1) * width] = total[7 + i : 8 + i, :].reshape(width)


def both_rows(own, other):
    return jnp.concatenate([own, other], axis=0)


def weight_tile(arranged_ref, right, away_ref, kept_ref, columns):
    half = away_ref.shape[0]
    away_ref[:, columns] = dot(arranged_ref[:half, :], right).astype(bf16)
    kept_ref[:, columns] = dot(arranged_ref[half:, :], right)


def mlp_weights_kernel(left_own_ref, left_par_ref, right_own_ref, right_par_ref, *outs):
    away_refs, kept_refs, (turned_ref, arranged_ref) = outs[:3], outs[3:6], outs[6:]
    mine = my_bits()
    turned_ref[...] = both_rows(left_own_ref[...], left_par_ref[...]).T
    columns = slice(0, UNIT_BLOCK)
    for part in range(3):
        at = slice(part * UNIT_BLOCK, (part + 1) * UNIT_BLOCK)
        right = both_rows(right_own_ref[:, at], right_par_ref[:, at])
        arrange_rows(turned_ref, mine, part, arranged_ref)
        weight_tile(arranged_ref, right, away_refs[part], kept_refs[part], columns)


def attn_weights_kernel(
    first_own_ref,
    first_par_ref,
    grad_attn_own_ref,
    grad_attn_par_ref,
    qkv_own_ref,
    qkv_par_ref,
    mixed_own_ref,
    mixed_par_ref,
    *outs,
):
    away_refs, kept_refs, (turned_ref, arranged_ref) = outs[:3], outs[3:6], outs[6:]
    mine = my_bits()
    local = mixed_own_ref.shape[1]
    third = local // 3
    turned_ref[...] = both_rows(first_own_ref[...], first_par_ref[...]).T
    for part in range(3):
        at = slice(part * local, (part + 1) * local)
        right = both_rows(qkv_own_ref[:, at], qkv_par_ref[:, at])
        arrange_rows(turned_ref, mine, part, arranged_ref)
        weight_tile(arranged_ref, right, away_refs[part], kept_refs[part], slice(0, local))
    turned_ref[...] = both_rows(grad_attn_own_ref[...], grad_attn_par_ref[...]).T
    for part in range(3):
        at = slice(part * third, (part + 1) * third)
        right = both_rows(mixed_own_ref[:, at], mixed_par_ref[:, at])
        arrange_rows(turned_ref, mine, part, arranged_ref)
        weight_tile(
            arranged_ref, right, away_refs[part], kept_refs[part], slice(local, local + third)
        )


def weights(kernel, arrays, width, depth, columns):
    half = width // 2
    return call(
        kernel,
        [shape((half, columns), bf16)] * 3 + [shape((half, columns), f32)] * 3,
        arrays,
        scratch=[pltpu.VMEM((width, depth), bf16), pltpu.VMEM((width, depth), bf16)],
    )


def heads_back(count_ref, grad_attn_ref, proj_ref, made_ref, out_ref, mixed_scratch):
    images = count_ref.shape[0]
    padded = made_ref.shape[0] // images
    local = proj_ref.shape[0]
    factor = HEAD_DIM ** (-0.5)
    mixed_scratch[...] = dot_turned(grad_attn_ref[...], proj_ref[...]).astype(bf16)
    for b in range(images):
        rows = slice(b * padded, (b + 1) * padded)
        for at in range(0, local, 2 * HEAD_DIM):
            q, k, v = (
                made_ref[rows, t * local + at : t * local + at + 2 * HEAD_DIM] for t in range(3)
            )
            q = stacked_heads(q)
            grad_mixed = stacked_heads(mixed_scratch[rows, at : at + 2 * HEAD_DIM])
            probs = pair_probs(q, k, count_ref[b])
            grad_probs = dot_turned(grad_mixed, v)
            row_dot = jnp.sum(probs * grad_probs, axis=-1, keepdims=True)
            grad_scores = (probs * (grad_probs - row_dot)).astype(bf16)
            found = (
                joined_heads(dot(grad_scores, k)) * factor,
                dot(grad_scores, q, ((0,), (0,))) * factor,
                dot(probs.astype(bf16), grad_mixed, ((0,), (0,))),
            )
            for t in range(3):
                to = slice(t * local + at, t * local + at + 2 * HEAD_DIM)
                out_ref[rows, to] = found[t].astype(bf16)


def back_kernel(
    count_ref,
    grad_pre_other_ref,
    w_fc1_other_ref,
    grad_pre_ref,
    w_fc1_ref,
    picked_ref,
    attention_ref,
    grad_picked_ref,
    router_ref,
    gain_ref,
    made_ref,
    proj_ref,
    grad_attn_ref,
    grad_hidden_ref,
    out_ref,
    sums_ref,
    mixed_scratch,
):
    images = count_ref.shape[0]
    padded = picked_ref.shape[0] // images
    grad_second = dot_turned(grad_pre_other_ref[...], w_fc1_other_ref[...])
    grad_second = grad_second + dot_turned(grad_pre_ref[...], w_fc1_ref[...])
    normed, inv_std = norm_stats(picked_ref[...].astype(f32) + attention_ref[...])
    grad_hidden = norm_back(grad_second, line(gain_ref), normed, inv_std)
    grad_hidden_ref[...] = grad_hidden
    scale = live_column(count_ref, images, padded) * router_ref[...]
    grad_attention = scale * grad_picked_ref[...].astype(f32) + grad_hidden
    grad_attn_ref[...] = grad_attention.astype(bf16)
    sums_ref[0:1, :] = column_sum(grad_attention)
    sums_ref[1:2, :] = column_sum(grad_second * normed)
    sums_ref[2:3, :] = column_sum(grad_second)
    heads_back(count_ref, grad_attn_ref, proj_ref, made_ref, out_ref, mixed_scratch)


def branch_kernel(
    count_ref,
    picked_ref,
    grad_picked_ref,
    router_ref,
    attention_ref,
    act_own_ref,
    act_other_ref,
    w_fc2_ref,
    w_fc2_other_ref,
    fc2_bias_ref,
    update_ref,
    grad_logit_ref,
    router_grad_ref,
):
    images = count_ref.shape[0]
    padded = picked_ref.shape[0] // images
    router = router_ref[...]
    scale = live_column(count_ref, images, padded) * router
    mlp_out = dot(act_own_ref[...], w_fc2_ref[...]) + dot(act_other_ref[...], w_fc2_other_ref[...])
    branch = attention_ref[...] + (mlp_out + line(fc2_bias_ref))
    update_ref[...] = scale * branch
    grad_logit = (
        scale
        * (1.0 - router)
        * jnp.sum(grad_picked_ref[...].astype(f32) * branch, axis=-1, keepdims=True)
    )
    grad_logit_ref[...] = grad_logit
    router_grad_ref[...] = column_sum(grad_logit * picked_ref[...].astype(f32))


def first_back_kernel(
    qkv_own_ref,
    gain_ref,
    router_w_ref,
    picked_ref,
    grad_hidden_ref,
    grad_logit_ref,
    grad_qkv_own_ref,
    grad_qkv_other_ref,
    qkv_other_ref,
    fc2_bias_grad_ref,
    router_grad_ref,
    back_sums_ref,
    unit_own_ref,
    unit_other_ref,
    grad_kept_ref,
    keep_ref,
    send_ref,
):
    width = picked_ref.shape[1]
    local = qkv_other_ref.shape[2]
    grad_first = jnp.zeros(picked_ref.shape, f32)
    for side in range(SIDES):
        for t in range(3):
            grad_first = grad_first + dot_turned(
                (grad_qkv_own_ref, grad_qkv_other_ref)[side][:, t * local : (t + 1) * local],
                (qkv_own_ref, qkv_other_ref)[side][t],
            )
    normed, inv_std = norm_stats(picked_ref[...].astype(f32))
    grad_kept_ref[...] = (
        norm_back(grad_first, line(gain_ref), normed, inv_std)
        + grad_hidden_ref[...]
        + grad_logit_ref[...] * line(router_w_ref)
    )
    sums = (
        column_sum(grad_first * normed),
        column_sum(grad_first),
        back_sums_ref[0:1, :],
        back_sums_ref[1:2, :],
        back_sums_ref[2:3, :],
        fc2_bias_grad_ref[...],
        router_grad_ref[...],
    )
    for i, values in enumerate(sums):
        keep_ref[i : i + 1, :] = values
        send_ref[i : i + 1, :] = values
    for i in range(unit_own_ref.shape[0] // width):
        at = slice(i * width, (i + 1) * width)
        keep_ref[7 + i : 8 + i, :] = unit_own_ref[at].reshape(1, width)
        send_ref[7 + i : 8 + i, :] = unit_other_ref[at].reshape(1, width)


def put_back_kernel(n_small, index_ref, base_ref, change_ref, *refs):
    small_refs, outs, padded_ref = refs[:n_small], refs[n_small:-1], refs[-1]
    out_ref = outs[0]
    if n_small:
        outs[1][...] = sum(ref[...] for ref in small_refs)
    images, slots, _ = base_ref.shape
    padded = change_ref.shape[0] // images
    fill_index(index_ref, padded_ref)
    for b in range(images):
        hot = turned_hot(index_ref, padded_ref, b, slots, padded)
        change = change_ref[b * padded : (b + 1) * padded, :]
        high = change.astype(bf16)
        low = (change - high.astype(f32)).astype(bf16)
        updated = base_ref[b].astype(f32) + (dot(hot, high) + dot(hot, low))
        out_ref[b] = updated.astype(bf16)


def other_core(value):
    return lax.ppermute(value, "head", [(0, 1), (1, 0)])


def partners(count, bit):
    return [(i, i ^ (1 << bit)) for i in range(count)]


def swap(value, bit, count):
    return lax.ppermute(value, "dp", partners(count, bit + count.bit_length() - 1 - TOP_BITS))


def begin(halves, count):
    streams = [Stream(part, None, halves[3 + part]) for part in range(3)]
    for part, stream in enumerate(streams):
        stream.sent(swap(halves[part], stream.bit(), count), 0)
    return streams


def exchange(streams, count, after, small=()):
    arrays, plans = listed(streams)
    tied, after = lax.optimization_barrier((tuple(arrays), after))
    bits = []
    for stream in streams:
        if stream.bit() not in bits:
            bits.append(stream.bit())
    sizes, full, bases = [0] * len(bits), [], []
    for stream, plan in zip(streams, plans):
        out = bits.index(stream.bit())
        made = stream.away is not None
        full.append((stream.part, stream.step, made, stream.unit, plan, out, sizes[out]))
        bases.append(sizes[out])
        sizes[out] += stream.rows()
    columns = arrays[0].shape[1]
    outs = [shape((size, columns), bf16) for size in sizes]
    outs += [shape(array.shape, array.dtype) for array in small[:1]]
    made = call(
        functools.partial(step_kernel, len(arrays), len(small), full), outs, (*tied, *small)
    )
    made, after = lax.optimization_barrier((made, after))
    got = [swap(made[n], bit, count) for n, bit in enumerate(bits)]
    for stream, base in zip(streams, bases):
        stream.sent(got[bits.index(stream.bit())], base)
    return (after, made[-1]) if small else after


def fewer_rows(grad, count, axis):
    place = lax.axis_index("dp")
    for bit in range(count.bit_length() - 2 - TOP_BITS, -1, -1):
        half = grad.shape[axis] // 2
        mine = (place >> bit) & 1
        away = lax.dynamic_slice_in_dim(grad, (1 - mine) * half, half, axis).astype(bf16)
        kept = lax.dynamic_slice_in_dim(grad, mine * half, half, axis)
        grad = kept + lax.ppermute(away, "dp", partners(count, bit)).astype(f32)
    return grad


def on_device(
    tokens,
    kept_index,
    kept_count,
    ln1_gain,
    ln1_bias,
    w_qkv,
    w_proj,
    proj_bias,
    ln2_gain,
    ln2_bias,
    w_fc1,
    fc1_bias,
    w_fc2,
    fc2_bias,
    w_router,
    cotangent,
):
    images, slots, width = tokens.shape
    padded = rows_of(kept_index.shape[1])
    rows = images * padded
    local = w_qkv.shape[2]
    units = w_fc1.shape[1]
    count = lax.axis_size("dp")

    top = count.bit_length() - 1 - TOP_BITS
    w_qkv_other = other_core(w_qkv)
    w_proj_other = other_core(w_proj)
    index_scratch = pltpu.VMEM((8, 128), jnp.int32)
    heads_scratch = pltpu.VMEM((rows, local), bf16)
    tie = lax.optimization_barrier
    picked, first, router, *near = call(
        front_kernel,
        [shape((rows, width), bf16), shape((rows, width), bf16), shape((rows, 1), f32)],
        (Far(kept_index), Far(tokens), Far(w_router), Far(ln1_gain), Far(ln1_bias)),
        scratch=[index_scratch],
        fetch=(w_qkv, w_proj, proj_bias, ln2_gain, ln2_bias, fc1_bias, fc2_bias, ln1_gain, w_router),
    )
    w_qkv, w_proj, proj_bias, ln2_gain, ln2_bias, bias_own, fc2_bias, ln1_gain, w_router = near
    w_fc1_late, w_fc2_late, bias_late, first, w_qkv_other, w_proj_other = tie(
        (w_fc1, w_fc2, fc1_bias, first, w_qkv_other, w_proj_other)
    )
    w_fc1_other = other_core(w_fc1_late)
    bias_other = other_core(bias_late)
    w_fc2_other = other_core(w_fc2_late)
    first_par = other_core(first)

    made, made_other, mixed, mixed_other, attention, second, w_fc1, w_fc2 = call(
        attention_kernel,
        [
            shape((rows, 3 * local), bf16),
            shape((rows, 3 * local), bf16),
            shape((rows, local), bf16),
            shape((rows, local), bf16),
            shape((rows, width), f32),
            shape((rows, width), bf16),
        ],
        (
            Far(kept_count),
            first,
            w_qkv,
            w_qkv_other,
            w_proj,
            w_proj_other,
            picked,
            proj_bias,
            ln2_gain,
            ln2_bias,
        ),
        fetch=(w_fc1, w_fc2),
    )
    second, first_par = tie((second, first_par))
    mixed_par = other_core(mixed_other)
    second_par = other_core(second)

    def hidden(w, bias):
        return call(
            hidden_kernel,
            [shape((rows, units), bf16), shape((rows, units), f32)],
            (second, w, bias),
        )

    def hidden_back(w, slope):
        return call(
            hidden_back_kernel,
            [shape((rows, units), bf16), shape((units,), f32)],
            (grad_mlp, w, slope),
        )

    def mlp_weights(left, left_par, right, right_par):
        return weights(
            mlp_weights_kernel, (left, left_par, right, right_par), width, 2 * rows, UNIT_BLOCK
        )

    act_other, slope_other = hidden(w_fc1_other, bias_other)
    act_par = other_core(act_other)
    router, act_other = tie((router, act_other))
    grad_picked, grad_mlp, fc2_bias_sum, cotangent = call(
        grad_front_kernel,
        [shape((rows, width), bf16), shape((rows, width), bf16), shape((1, width), f32)],
        (Far(kept_count), Far(kept_index), Far(cotangent), router),
        scratch=[index_scratch],
        fetch=(cotangent,),
    )
    grad_mlp_par = other_core(grad_mlp)
    second, grad_mlp, mixed_par, second_par = tie((second, grad_mlp, mixed_par, second_par))
    act, slope = hidden(w_fc1, bias_own)
    halves = mlp_weights(grad_mlp, grad_mlp_par, act, act_par)
    halves, slope_other = tie((halves, slope_other))
    mlp_sums = begin(halves, count)
    grad_pre_other, unit_other = hidden_back(w_fc2_other, slope_other)
    grad_pre_par = other_core(grad_pre_other)
    grad_pre, unit_own = hidden_back(w_fc2, slope)
    halves = mlp_weights(second, second_par, grad_pre, grad_pre_par)
    halves, grad_pre = tie((halves, grad_pre))
    mlp_sums += begin(halves, count)

    grad_attn, grad_hidden, grad_qkv_other, back_sums = call(
        back_kernel,
        [
            shape((rows, width), bf16),
            shape((rows, width), f32),
            shape((rows, 3 * local), bf16),
            shape((8, width), f32),
        ],
        (
            Far(kept_count),
            grad_pre_other,
            w_fc1_other,
            grad_pre,
            w_fc1,
            picked,
            attention,
            grad_picked,
            router,
            ln2_gain,
            made_other,
            w_proj_other,
        ),
        scratch=[heads_scratch],
    )
    grad_attn_par = other_core(grad_attn)
    grad_qkv_par = other_core(grad_qkv_other)
    grad_attn = exchange(mlp_sums, count, grad_attn)
    grad_attn, grad_attn_par, grad_qkv_par = tie((grad_attn, grad_attn_par, grad_qkv_par))
    (grad_qkv,) = call(
        heads_back,
        [shape((rows, 3 * local), bf16)],
        (Far(kept_count), grad_attn, w_proj, made),
        scratch=[heads_scratch],
    )
    halves = weights(
        attn_weights_kernel,
        (first, first_par, grad_attn, grad_attn_par, grad_qkv, grad_qkv_par, mixed, mixed_par),
        width,
        2 * rows,
        local + local // 3,
    )
    attn_sums = [Stream(part, halves[part], halves[3 + part]) for part in range(3)]
    act = exchange((*mlp_sums, *attn_sums), count, act)
    update, grad_logit, router_sum = call(
        branch_kernel,
        [shape((rows, width), f32), shape((rows, 1), f32), shape((1, width), f32)],
        (
            Far(kept_count),
            picked,
            grad_picked,
            router,
            attention,
            act,
            act_other,
            w_fc2,
            w_fc2_other,
            fc2_bias,
        ),
    )

    sum_rows = 7 + units // width
    grad_kept, keep, send = call(
        first_back_kernel,
        [
            shape((rows, width), f32),
            shape((sum_rows, width), f32),
            shape((sum_rows, width), f32),
        ],
        (
            w_qkv,
            ln1_gain,
            w_router,
            picked,
            grad_hidden,
            grad_logit,
            grad_qkv,
            grad_qkv_other,
            w_qkv_other,
            fc2_bias_sum,
            router_sum,
            back_sums,
            unit_own,
            unit_other,
        ),
    )

    def put_back(base, change, *small):
        return call(
            functools.partial(put_back_kernel, len(small)),
            [Far(shape(base.shape, bf16)), *[shape(x.shape, x.dtype) for x in small[:1]]],
            (Far(kept_index), base, change, *small),
            scratch=[index_scratch],
        )

    got = other_core(send)
    update, keep = tie((update, keep))
    output, small = put_back(tokens, update, keep, got)
    got = swap(small, 0, count)
    grad_kept, output = tie((grad_kept, output))
    grad_kept, small = exchange((*mlp_sums, *attn_sums), count, grad_kept, (small, got))
    got = swap(small, 1, count)
    (input_grad,) = put_back(cotangent, grad_kept)
    input_grad, small = exchange(attn_sums, count, input_grad, (small, got))
    got = swap(small, 2, count)
    input_grad, small = exchange(attn_sums, count, input_grad, (small, got))
    for low in range(top):
        small = small + lax.ppermute(small, "dp", partners(count, low))
    got = swap(small, 3, count)
    sums = (*mlp_sums, *attn_sums)
    arrays, plans = listed(sums)
    plans = [(stream.part, stream.unit, plan) for stream, plan in zip(sums, plans)]
    unit = width // UNITS
    fc2_turned, fc1_grad, qkv_grad, proj_turned, *sums = call(
        functools.partial(finish_kernel, len(arrays), 2, plans),
        [
            Far(shape((unit, units), f32)),
            Far(shape((unit, units), f32)),
            Far(shape((3, unit, local), f32)),
            Far(shape((unit, local), f32)),
            *[Far(shape((width,), f32))] * 7,
            Far(shape((units,), f32)),
        ],
        (*arrays, small, got),
    )
    fc2_turned, fc1_grad, proj_turned = (
        fewer_rows(grad, count, 0) for grad in (fc2_turned, fc1_grad, proj_turned)
    )
    qkv_grad = fewer_rows(qkv_grad, count, 1)
    return (
        output,
        input_grad,
        sums[0],
        sums[1],
        qkv_grad,
        proj_turned.T,
        sums[2],
        sums[3],
        sums[4],
        fc1_grad,
        sums[7],
        fc2_turned.T,
        sums[5],
        sums[6],
    )


def solution(mesh):
    batch = ("dp", "head")
    return jax.shard_map(
        on_device,
        mesh=mesh,
        in_specs=(
            P(batch, None, None),
            P(batch, None),
            P(batch),
            P(),
            P(),
            P(None, None, "head"),
            P("head", None),
            P(),
            P(),
            P(),
            P(None, "head"),
            P("head"),
            P("head", None),
            P(),
            P(),
            P(batch, None, None),
        ),
        out_specs=(
            P(batch, None, None),
            P(batch, None, None),
            P(),
            P(),
            P(None, "dp", "head"),
            P("head", "dp"),
            P(),
            P(),
            P(),
            P("dp", "head"),
            P("head"),
            P("head", "dp"),
            P(),
            P(),
        ),
        check_vma=False,
    )
```

```python
import functools

import jax
import jax.numpy as jnp
from jax import lax
from jax.experimental import pallas as pl
from jax.experimental.pallas import tpu as pltpu
from jax.sharding import PartitionSpec as P

HEAD_DIM = 64
norm_eps = 1e-06
root_half = 0.7071067811865476
inv_root_two_pi = 0.3989422804014327
f32, bf16 = jnp.float32, jnp.bfloat16


MIB = 1024 * 1024
SIDES = 2
FLOPS = 1
UNIT_BLOCK = 512


def rows_of(count):
    return -(-count // 16) * 16


def norm_stats(values):
    row_mean = jnp.mean(values, axis=-1, keepdims=True)
    centered = values - row_mean
    inv_std = lax.rsqrt(jnp.mean(centered * centered, axis=-1, keepdims=True) + norm_eps)
    return centered * inv_std, inv_std


def norm_back(grad_normed, gain, normed, inv_std):
    unit = grad_normed * gain
    return inv_std * (
        unit
        - jnp.mean(unit, axis=-1, keepdims=True)
        - normed * jnp.mean(unit * normed, axis=-1, keepdims=True)
    )


def dot(a, b, over=((1,), (0,))):
    return lax.dot_general(a, b, (over, ((), ())), preferred_element_type=f32)


def dot_turned(a, b):
    return dot(a, b, ((1,), (1,)))


def column_sum(values):
    return jnp.sum(values, axis=0, keepdims=True)


class Held:
    def __init__(self, ref, copy):
        self.ref, self.copy, self.shape = ref, copy, ref.shape

    def ready(self):
        if self.copy is not None:
            self.copy.wait()
            self.copy = None
        return self.ref

    def __getitem__(self, at):
        return self.ready()[at]


class Made:
    def __init__(self, ref, copy):
        self.ref, self.copy, self.shape, self.left = ref, copy, ref.shape, False

    def __getitem__(self, at):
        return self.ref[at]

    def __setitem__(self, at, value):
        self.ref[at] = value

    def leave(self):
        if not self.left:
            self.copy.start()
            self.left = True


class Far:
    def __init__(self, value):
        self.value = value


def call(kernel, out_shape, inputs, scratch=(), fetch=(), room=14):
    inputs = [*inputs, *[Far(x) for x in fetch]]
    values = [x.value if isinstance(x, Far) else x for x in inputs]
    shapes = [x.value if isinstance(x, Far) else x for x in out_shape]
    shapes += [shape(x.shape, x.dtype) for x in fetch]
    n_fetch, n_in, n_out = len(fetch), len(inputs), len(shapes)
    far_in = [i for i in range(n_in - n_fetch) if isinstance(inputs[i], Far)]
    far_out = [i for i, x in enumerate(out_shape) if isinstance(x, Far)]
    near, away = pl.BlockSpec(memory_space=pltpu.VMEM), pl.BlockSpec(memory_space=pltpu.HBM)
    in_hbm = [isinstance(x, Far) for x in inputs]

    def body(*refs):
        ins, outs, refs = list(refs[:n_in]), list(refs[n_in : n_in + n_out]), refs[n_in + n_out :]
        in_refs, refs = refs[: len(far_in)], refs[len(far_in) :]
        out_refs, refs = refs[: len(far_out)], refs[len(far_out) :]
        sems, extra = (refs[0], refs[1:]) if n_sems else (None, refs)
        for n, i in enumerate(far_in):
            copy = pltpu.make_async_copy(ins[i], in_refs[n], sems.at[n])
            copy.start()
            ins[i] = Held(in_refs[n], copy)
        for n, i in enumerate(far_out):
            copy = pltpu.make_async_copy(out_refs[n], outs[i], sems.at[len(far_in) + n])
            outs[i] = Made(out_refs[n], copy)
        fetched = []
        for n in range(n_fetch):
            copy = pltpu.make_async_copy(
                ins[n_in - n_fetch + n],
                outs[n_out - n_fetch + n],
                sems.at[len(far_in) + len(far_out) + n],
            )
            copy.start()
            fetched.append(copy)
        kernel(*ins[: n_in - n_fetch], *outs[: n_out - n_fetch], *extra)
        for i in far_in:
            ins[i].ready()
        for i in far_out:
            outs[i].leave()
        for copy in fetched:
            copy.wait()
        for i in far_out:
            outs[i].copy.wait()

    def landing(x):
        return (pltpu.SMEM if x.dtype == jnp.int32 and x.ndim == 1 else pltpu.VMEM)(x.shape, x.dtype)

    far_scratch = [landing(values[i]) for i in far_in]
    far_scratch += [pltpu.VMEM(shapes[i].shape, shapes[i].dtype) for i in far_out]
    n_sems = len(far_in) + len(far_out) + n_fetch
    if n_sems:
        far_scratch.append(pltpu.SemaphoreType.DMA((n_sems,)))
    values = [
        pltpu.with_memory_space_constraint(x, pltpu.HBM if far else pltpu.VMEM)
        for x, far in zip(values, in_hbm)
    ]
    return pl.pallas_call(
        body,
        out_shape=[
            (pltpu.HBM if i in far_out else pltpu.VMEM)(o.shape, o.dtype)
            for i, o in enumerate(shapes)
        ],
        in_specs=[away if far else near for far in in_hbm],
        out_specs=[away if i in far_out else near for i in range(n_out)],
        scratch_shapes=[*far_scratch, *scratch],
        compiler_params=pltpu.CompilerParams(vmem_limit_bytes=room * MIB),
        cost_estimate=pl.CostEstimate(flops=FLOPS, bytes_accessed=1, transcendentals=0),
    )(*values)


def line(ref):
    return ref[...].reshape(1, -1)


def shape(dims, kind):
    return jax.ShapeDtypeStruct(dims, kind)


def turned_hot(index_ref, image, slots, padded):
    place = lax.broadcasted_iota(jnp.int32, (slots, padded), 0)
    return jnp.where(place == index_ref[image : image + 1, :padded], 1.0, 0.0).astype(bf16)


def front_kernel(
    index_in_ref,
    tokens_ref,
    count_in_ref,
    router_w_ref,
    gain_ref,
    shift_ref,
    cotangent_ref,
    index_ref,
    count_ref,
    picked_ref,
    grad_picked_ref,
    first_ref,
    grad_mlp_ref,
    router_ref,
    scale_ref,
    fc2_bias_grad_ref,
):
    images, slots, _ = tokens_ref.shape
    padded = picked_ref.shape[0] // images
    index_ref[...] = jnp.full(index_ref.shape, -1, jnp.int32)
    index_ref[:images, : index_in_ref.shape[1]] = index_in_ref[...]
    for b in range(images):
        hot = turned_hot(index_ref, b, slots, padded)
        picked_ref[b * padded : (b + 1) * padded, :] = dot(hot, tokens_ref[b], ((0,), (0,))).astype(
            bf16
        )
    picked = picked_ref[...].astype(f32)
    router = jax.nn.sigmoid(jnp.sum(picked * line(router_w_ref), axis=-1, keepdims=True))
    router_ref[...] = router
    normed, _ = norm_stats(picked)
    first_ref[...] = (normed * line(gain_ref) + line(shift_ref)).astype(bf16)
    rows = lax.broadcasted_iota(jnp.int32, (padded, 1), 0)
    for b in range(images):
        count_ref[b : b + 1, :] = jnp.full((1, count_ref.shape[1]), count_in_ref[b], jnp.int32)
        at = slice(b * padded, (b + 1) * padded)
        live = jnp.where(rows < count_in_ref[b], 1.0, 0.0).astype(f32)
        scale_ref[at, :] = live * router_ref[at, :]
        hot = turned_hot(index_ref, b, slots, padded)
        grad_picked_ref[at, :] = dot(hot, cotangent_ref[b], ((0,), (0,))).astype(bf16)
    grad_branch = scale_ref[...] * grad_picked_ref[...].astype(f32)
    grad_mlp_ref[...] = grad_branch.astype(bf16)
    fc2_bias_grad_ref[...] = column_sum(grad_branch)


def stacked_heads(pair):
    lane = lax.broadcasted_iota(jnp.int32, pair.shape, 1)
    zero = jnp.zeros_like(pair)
    return jnp.concatenate(
        [jnp.where(lane < HEAD_DIM, pair, zero), jnp.where(lane < HEAD_DIM, zero, pair)], axis=0
    )


def joined_heads(stacked):
    half = stacked.shape[0] // 2
    lane = lax.broadcasted_iota(jnp.int32, (half, stacked.shape[1]), 1)
    return jnp.where(lane < HEAD_DIM, stacked[:half], stacked[half:])


def pairs_of_heads(images, padded, local):
    return [
        (b, slice(b * padded, (b + 1) * padded), at)
        for b in range(images)
        for at in range(0, local, 2 * HEAD_DIM)
    ]


def saved_qkv(made_ref, rows, at):
    local = made_ref.shape[1] // 3
    return [made_ref[rows, t * local + at : t * local + at + 2 * HEAD_DIM] for t in range(3)]


def probabilities(scores, count, axis):
    key = lax.broadcasted_iota(jnp.int32, scores.shape, axis)
    scores = jnp.where(key < count, scores, -1e30)
    raised = jnp.exp(scores - jnp.max(scores, axis=axis, keepdims=True))
    return raised * (1.0 / jnp.sum(raised, axis=axis, keepdims=True))


def project(first_ref, w_ref, made_ref):
    local = w_ref.shape[2]
    for t in range(3):
        made_ref[:, t * local : (t + 1) * local] = dot(first_ref[...], w_ref[t]).astype(bf16)


def attend(images, count_ref, made_ref, mixed_ref):
    padded, local = made_ref.shape[0] // images, mixed_ref.shape[1]
    units = pairs_of_heads(images, padded, local)
    qkv = [saved_qkv(made_ref, rows, at) for _, rows, at in units]
    scores = [dot_turned(stacked_heads(q), k) * HEAD_DIM ** (-0.5) for q, k, _ in qkv]
    probs = [
        probabilities(x, count_ref[b : b + 1, 0:1], 1).astype(bf16)
        for x, (b, _, _) in zip(scores, units)
    ]
    mixed = [joined_heads(dot(x, v)) for x, (_, _, v) in zip(probs, qkv)]
    for x, (_, rows, at) in zip(mixed, units):
        mixed_ref[rows, at : at + 2 * HEAD_DIM] = x.astype(bf16)


def attention_kernel(
    images,
    count_ref,
    first_ref,
    w_own_ref,
    w_other_ref,
    proj_own_ref,
    proj_other_ref,
    picked_ref,
    proj_bias_ref,
    gain_ref,
    shift_ref,
    made_own_ref,
    made_other_ref,
    mixed_own_ref,
    mixed_other_ref,
    attention_ref,
    second_ref,
    pack_ref,
):
    width = first_ref.shape[1]
    pack_ref[:, :width] = first_ref[...]
    project(first_ref, w_own_ref, made_own_ref)
    project(first_ref, w_other_ref, made_other_ref)
    attend(images, count_ref, made_own_ref, mixed_own_ref)
    attend(images, count_ref, made_other_ref, mixed_other_ref)
    total = line(proj_bias_ref) + dot(mixed_own_ref[...], proj_own_ref[...])
    total = total + dot(mixed_other_ref[...], proj_other_ref[...])
    attention_ref[...] = total
    normed, _ = norm_stats(picked_ref[...].astype(f32) + total)
    second = (normed * line(gain_ref) + line(shift_ref)).astype(bf16)
    second_ref[...] = second
    pack_ref[:, width : 2 * width] = second
    pack_ref[:, 2 * width :] = mixed_other_ref[...]


def hidden_kernel(second_ref, w_fc1_ref, bias_ref, act_ref, slope_ref):
    for at in range(0, act_ref.shape[1], UNIT_BLOCK):
        block = slice(at, at + UNIT_BLOCK)
        pre = dot(second_ref[...], w_fc1_ref[:, block]) + bias_ref[block].reshape(1, -1)
        half = 0.5 * (1.0 + lax.erf(pre * root_half))
        act_ref[:, block] = (pre * half).astype(bf16)
        slope_ref[:, block] = half + pre * inv_root_two_pi * jnp.exp(-0.5 * pre * pre)


def hidden_back_kernel(grad_mlp_ref, w_fc2_ref, slope_ref, grad_pre_ref, unit_sum_ref):
    for at in range(0, slope_ref.shape[1], UNIT_BLOCK):
        block = slice(at, at + UNIT_BLOCK)
        grad_pre = dot_turned(grad_mlp_ref[...], w_fc2_ref[block, :]) * slope_ref[:, block]
        unit_sum_ref[block] = column_sum(grad_pre).reshape(UNIT_BLOCK)
        grad_pre_ref[:, block] = grad_pre.astype(bf16)


TOP_BITS = 4
FC2_EARLY, FC1_EARLY, ATTN_EARLY = 1, 0, 0
UNITS = 1 << TOP_BITS


def my_bits():
    place = lax.axis_index("dp") >> (lax.axis_size("dp").bit_length() - 1 - TOP_BITS)
    return [(place >> bit) & 1 for bit in range(TOP_BITS)]


def order_of(part, early=0):
    order = [(part + j) % 3 for j in range(3)] + [3]
    return order[:2] + [3, order[2]] if part < early else order


def bits_left(order, step):
    return [bit for bit in range(TOP_BITS - 1, -1, -1) if bit not in order[:step]]


def every_choice(bits):
    for j in range(1 << len(bits)):
        yield j, {bit: (j >> (len(bits) - 1 - i)) & 1 for i, bit in enumerate(bits)}


def unit_rows(ref, spread, chosen, unit, base=0):
    place = 0
    for bit in spread:
        place = place * 2 + chosen[bit]
    return ref[pl.ds(pl.multiple_of(base + place * unit, 16), unit), :]


def arrange_rows(turned_ref, mine, part, arranged_ref):
    unit = turned_ref.shape[0] // UNITS
    order = order_of(part)
    bit = order[0]
    for side, value in enumerate((1 - mine[bit], mine[bit])):
        for j, chosen in every_choice(bits_left(order, 1)):
            chosen[bit] = value
            to = (side * UNITS // 2 + j) * unit
            arranged_ref[to : to + unit, :] = unit_rows(
                turned_ref, bits_left(order, 0), chosen, unit
            )


class Stream:
    def __init__(self, part, away, kept, early):
        self.part, self.step, self.away, self.terms = part, 0, away, [(kept, 0, 1)]
        self.order = order_of(part, early)
        self.unit = kept.shape[0] * 2 // UNITS

    def bit(self):
        return self.order[self.step]

    def rows(self):
        return self.unit * UNITS >> (self.step + 1)

    def sent(self, got, base):
        self.step += 1
        self.away = None
        self.terms.append((got, base, self.step))


def listed(streams):
    arrays, plans = [], []
    for stream in streams:
        terms = [(stream.away, 0, 0)] if stream.away is not None else stream.terms
        plan = []
        for array, base, step in terms:
            found = [n for n, x in enumerate(arrays) if x is array]
            if not found:
                found = [len(arrays)]
                arrays.append(array)
            plan.append((found[0], base, step))
        plans.append(plan)
    return arrays, plans


def plan_sum(refs, plan, order, chosen, unit):
    total = 0.0
    for n, base, step in plan:
        total = total + unit_rows(refs[n], bits_left(order, step), chosen, unit, base).astype(f32)
    return total


def step_kernel(n_arrays, n_small, plans, *refs):
    mine = my_bits()
    small, outs = refs[n_arrays : n_arrays + n_small], refs[n_arrays + n_small :]
    if n_small:
        outs[-1][...] = sum(ref[...] for ref in small)
    for order, step, made, unit, plan, out, base in plans:
        if made:
            ref = refs[plan[0][0]]
            outs[out][base : base + ref.shape[0], :] = ref[...]
            continue
        for j, chosen in every_choice(bits_left(order, step + 1)):
            for bit in order[:step]:
                chosen[bit] = mine[bit]
            chosen[order[step]] = 1 - mine[order[step]]
            to = base + j * unit
            outs[out][to : to + unit, :] = plan_sum(refs, plan, order, chosen, unit).astype(bf16)


def finish_kernel(n_arrays, n_small, plans, *refs):
    mine = my_bits()
    chosen = {bit: mine[bit] for bit in range(TOP_BITS)}
    small, refs_out = refs[n_arrays : n_arrays + n_small], refs[n_arrays + n_small :]
    fc2_ref, fc1_ref, qkv_ref, proj_ref, *outs = refs_out
    local = qkv_ref.shape[2]
    third = local // 3
    for i, (part, order, unit, plan) in enumerate(plans):
        total = plan_sum(refs, plan, order, chosen, unit)
        if i < 6:
            (fc2_ref, fc1_ref)[i // 3][:, part * UNIT_BLOCK : (part + 1) * UNIT_BLOCK] = total
        else:
            qkv_ref[part] = total[:, :local]
            proj_ref[:, part * third : (part + 1) * third] = total[:, local:]
        if i == 5:
            fc2_ref.leave()
            fc1_ref.leave()
    total = sum(ref[...] for ref in small)
    width = total.shape[1]
    for i, out_ref in enumerate(outs[:-1]):
        out_ref[...] = total[i : i + 1, :].reshape(width)
    for i in range(total.shape[0] - 7):
        outs[-1][i * width : (i + 1) * width] = total[7 + i : 8 + i, :].reshape(width)


def both_rows(own, other):
    return jnp.concatenate([own, other], axis=0)


def weight_tile(arranged_ref, right, away_ref, kept_ref, columns):
    half = away_ref.shape[0]
    away_ref[:, columns] = dot(arranged_ref[:half, :], right).astype(bf16)
    kept_ref[:, columns] = dot(arranged_ref[half:, :], right)


def mlp_weights_kernel(at_left, left_own_ref, left_par_ref, right_own_ref, right_par_ref, *outs):
    away_refs, kept_refs, (turned_ref, arranged_ref) = outs[:3], outs[3:6], outs[6:]
    mine = my_bits()
    left_par = left_par_ref[:, at_left : at_left + left_own_ref.shape[1]]
    turned_ref[...] = both_rows(left_own_ref[...], left_par).T
    columns = slice(0, UNIT_BLOCK)
    for part in range(3):
        at = slice(part * UNIT_BLOCK, (part + 1) * UNIT_BLOCK)
        right = both_rows(right_own_ref[:, at], right_par_ref[:, at])
        arrange_rows(turned_ref, mine, part, arranged_ref)
        weight_tile(arranged_ref, right, away_refs[part], kept_refs[part], columns)


def attn_weights_kernel(
    first_own_ref,
    pack_par_ref,
    grad_attn_own_ref,
    grad_attn_par_ref,
    qkv_own_ref,
    qkv_par_ref,
    mixed_own_ref,
    *outs,
):
    away_refs, kept_refs, (turned_ref, arranged_ref) = outs[:3], outs[3:6], outs[6:]
    mine = my_bits()
    width, local = first_own_ref.shape[1], mixed_own_ref.shape[1]
    third = local // 3
    turned_ref[...] = both_rows(first_own_ref[...], pack_par_ref[:, :width]).T
    for part in range(3):
        at = slice(part * local, (part + 1) * local)
        right = both_rows(qkv_own_ref[:, at], qkv_par_ref[:, at])
        arrange_rows(turned_ref, mine, part, arranged_ref)
        weight_tile(arranged_ref, right, away_refs[part], kept_refs[part], slice(0, local))
    turned_ref[...] = both_rows(grad_attn_own_ref[...], grad_attn_par_ref[...]).T
    for part in range(3):
        at = slice(part * third, (part + 1) * third)
        right = both_rows(mixed_own_ref[:, at], pack_par_ref[:, 2 * width + at.start : 2 * width + at.stop])
        arrange_rows(turned_ref, mine, part, arranged_ref)
        weight_tile(
            arranged_ref, right, away_refs[part], kept_refs[part], slice(local, local + third)
        )


def weights(kernel, arrays, width, depth, columns):
    half = width // 2
    return call(
        kernel,
        [shape((half, columns), bf16)] * 3 + [shape((half, columns), f32)] * 3,
        arrays,
        scratch=[pltpu.VMEM((width, depth), bf16), pltpu.VMEM((width, depth), bf16)],
    )


def heads_back(images, count_ref, grad_attn_ref, proj_ref, made_ref, out_ref, mixed_scratch):
    padded, local = made_ref.shape[0] // images, proj_ref.shape[0]
    factor = HEAD_DIM ** (-0.5)
    mixed_scratch[...] = dot_turned(grad_attn_ref[...], proj_ref[...]).astype(bf16)
    units = pairs_of_heads(images, padded, local)
    for first in range(0, len(units), 3):
        some = units[first : first + 3]
        q, k, v = zip(*[saved_qkv(made_ref, rows, at) for _, rows, at in some])
        q = [stacked_heads(x) for x in q]
        grad_mixed = [
            stacked_heads(mixed_scratch[rows, at : at + 2 * HEAD_DIM]) for _, rows, at in some
        ]
        scores = [dot_turned(x, y) * factor for x, y in zip(k, q)]
        grad_probs = [dot_turned(x, y) for x, y in zip(v, grad_mixed)]
        probs = [
            probabilities(x, count_ref[b : b + 1, 0:1], 0) for x, (b, _, _) in zip(scores, some)
        ]
        grad_scores = [
            (p * (g - jnp.sum(p * g, axis=0, keepdims=True))).astype(bf16)
            for p, g in zip(probs, grad_probs)
        ]
        grad_k = [dot(x, y) * factor for x, y in zip(grad_scores, q)]
        grad_v = [dot(x.astype(bf16), y) for x, y in zip(probs, grad_mixed)]
        grad_q = [joined_heads(dot(x, y, ((0,), (0,)))) * factor for x, y in zip(grad_scores, k)]
        for (_, rows, at), *found in zip(some, grad_q, grad_k, grad_v):
            for t in range(3):
                to = slice(t * local + at, t * local + at + 2 * HEAD_DIM)
                out_ref[rows, to] = found[t].astype(bf16)


def back_kernel(
    grad_pre_other_ref,
    w_fc1_other_ref,
    grad_pre_ref,
    w_fc1_ref,
    picked_ref,
    attention_ref,
    grad_picked_ref,
    scale_ref,
    gain_ref,
    grad_attn_ref,
    grad_hidden_ref,
    sums_ref,
):
    grad_second = dot_turned(grad_pre_other_ref[...], w_fc1_other_ref[...])
    grad_second = grad_second + dot_turned(grad_pre_ref[...], w_fc1_ref[...])
    normed, inv_std = norm_stats(picked_ref[...].astype(f32) + attention_ref[...])
    grad_hidden = norm_back(grad_second, line(gain_ref), normed, inv_std)
    grad_hidden_ref[...] = grad_hidden
    grad_attention = scale_ref[...] * grad_picked_ref[...].astype(f32) + grad_hidden
    grad_attn_ref[...] = grad_attention.astype(bf16)
    sums_ref[0:1, :] = column_sum(grad_attention)
    sums_ref[1:2, :] = column_sum(grad_second * normed)
    sums_ref[2:3, :] = column_sum(grad_second)


def branch_kernel(
    picked_ref,
    grad_picked_ref,
    router_ref,
    scale_ref,
    attention_ref,
    act_own_ref,
    act_other_ref,
    w_fc2_ref,
    w_fc2_other_ref,
    fc2_bias_ref,
    update_ref,
    grad_logit_ref,
    router_grad_ref,
):
    scale = scale_ref[...]
    mlp_out = dot(act_own_ref[...], w_fc2_ref[...]) + dot(act_other_ref[...], w_fc2_other_ref[...])
    branch = attention_ref[...] + (mlp_out + line(fc2_bias_ref))
    update_ref[...] = scale * branch
    grad_logit = (
        scale
        * (1.0 - router_ref[...])
        * jnp.sum(grad_picked_ref[...].astype(f32) * branch, axis=-1, keepdims=True)
    )
    grad_logit_ref[...] = grad_logit
    router_grad_ref[...] = column_sum(grad_logit * picked_ref[...].astype(f32))


def first_back_kernel(
    qkv_own_ref,
    gain_ref,
    router_w_ref,
    picked_ref,
    grad_hidden_ref,
    grad_logit_ref,
    grad_qkv_own_ref,
    grad_qkv_other_ref,
    qkv_other_ref,
    fc2_bias_grad_ref,
    router_grad_ref,
    back_sums_ref,
    unit_own_ref,
    unit_other_ref,
    grad_kept_ref,
    keep_ref,
    send_ref,
):
    width = picked_ref.shape[1]
    local = qkv_other_ref.shape[2]
    grad_first = jnp.zeros(picked_ref.shape, f32)
    for side in range(SIDES):
        for t in range(3):
            grad_first = grad_first + dot_turned(
                (grad_qkv_own_ref, grad_qkv_other_ref)[side][:, t * local : (t + 1) * local],
                (qkv_own_ref, qkv_other_ref)[side][t],
            )
    normed, inv_std = norm_stats(picked_ref[...].astype(f32))
    grad_kept_ref[...] = (
        norm_back(grad_first, line(gain_ref), normed, inv_std)
        + grad_hidden_ref[...]
        + grad_logit_ref[...] * line(router_w_ref)
    )
    sums = (
        column_sum(grad_first * normed),
        column_sum(grad_first),
        back_sums_ref[0:1, :],
        back_sums_ref[1:2, :],
        back_sums_ref[2:3, :],
        fc2_bias_grad_ref[...],
        router_grad_ref[...],
    )
    for i, values in enumerate(sums):
        keep_ref[i : i + 1, :] = values
        send_ref[i : i + 1, :] = values
    for i in range(unit_own_ref.shape[0] // width):
        at = slice(i * width, (i + 1) * width)
        keep_ref[7 + i : 8 + i, :] = unit_own_ref[at].reshape(1, width)
        send_ref[7 + i : 8 + i, :] = unit_other_ref[at].reshape(1, width)


def put_back_kernel(n_small, index_ref, base_ref, change_ref, *refs):
    small_refs, outs = refs[:n_small], refs[n_small:]
    if n_small:
        outs[1][...] = sum(ref[...] for ref in small_refs)
    images, slots, _ = base_ref.shape
    padded = change_ref.shape[0] // images
    for b in range(images):
        hot = turned_hot(index_ref, b, slots, padded)
        change = change_ref[b * padded : (b + 1) * padded, :]
        high = change.astype(bf16)
        low = (change - high.astype(f32)).astype(bf16)
        updated = base_ref[b].astype(f32) + (dot(hot, high) + dot(hot, low))
        outs[0][b] = updated.astype(bf16)


def other_core(value):
    return lax.ppermute(value, "head", [(0, 1), (1, 0)])


def partners(count, bit):
    return [(i, i ^ (1 << bit)) for i in range(count)]


def swap(value, bit, count):
    return lax.ppermute(value, "dp", partners(count, bit + count.bit_length() - 1 - TOP_BITS))


def waiting(halves, early=0):
    return [Stream(part, halves[part], halves[3 + part], early) for part in range(3)]


def begin(halves, count, early=0):
    streams = waiting(halves, early)
    for stream in streams:
        stream.sent(swap(stream.away, stream.bit(), count), 0)
    return streams


def exchange(streams, count, after, small=()):
    arrays, plans = listed(streams)
    tied, after = lax.optimization_barrier((tuple(arrays), after))
    bits = []
    for stream in streams:
        if stream.bit() not in bits:
            bits.append(stream.bit())
    sizes, full, bases = [0] * len(bits), [], []
    for stream, plan in zip(streams, plans):
        out = bits.index(stream.bit())
        made = stream.away is not None
        full.append((stream.order, stream.step, made, stream.unit, plan, out, sizes[out]))
        bases.append(sizes[out])
        sizes[out] += stream.rows()
    columns = arrays[0].shape[1]
    outs = [shape((size, columns), bf16) for size in sizes]
    outs += [shape(array.shape, array.dtype) for array in small[:1]]
    made = call(
        functools.partial(step_kernel, len(arrays), len(small), full), outs, (*tied, *small)
    )
    made, after = lax.optimization_barrier((made, after))
    got = [swap(made[n], bit, count) for n, bit in enumerate(bits)]
    for stream, base in zip(streams, bases):
        stream.sent(got[bits.index(stream.bit())], base)
    return (after, made[-1]) if small else after


def arrived(streams, after):
    arrays = []
    for stream in streams:
        if all(stream.terms[-1][0] is not x for x in arrays):
            arrays.append(stream.terms[-1][0])
    tied, after = lax.optimization_barrier((arrays, after))
    for stream in streams:
        array, base, step = stream.terms[-1]
        place = [x is array for x in arrays].index(True)
        stream.terms[-1] = (tied[place], base, step)
    return after


def fewer_rows(grad, count, axis):
    place = lax.axis_index("dp")
    for bit in range(count.bit_length() - 2 - TOP_BITS, -1, -1):
        half = grad.shape[axis] // 2
        mine = (place >> bit) & 1
        away = lax.dynamic_slice_in_dim(grad, (1 - mine) * half, half, axis).astype(bf16)
        kept = lax.dynamic_slice_in_dim(grad, mine * half, half, axis)
        grad = kept + lax.ppermute(away, "dp", partners(count, bit)).astype(f32)
    return grad


def on_device(
    tokens,
    kept_index,
    kept_count,
    ln1_gain,
    ln1_bias,
    w_qkv,
    w_proj,
    proj_bias,
    ln2_gain,
    ln2_bias,
    w_fc1,
    fc1_bias,
    w_fc2,
    fc2_bias,
    w_router,
    cotangent,
):
    images, slots, width = tokens.shape
    padded = rows_of(kept_index.shape[1])
    rows = images * padded
    local = w_qkv.shape[2]
    units = w_fc1.shape[1]
    count = lax.axis_size("dp")

    top = count.bit_length() - 1 - TOP_BITS
    w_qkv_other = other_core(w_qkv)
    w_proj_other = other_core(w_proj)
    bias_other = other_core(fc1_bias)
    tie = lax.optimization_barrier
    table = shape((8, 128), jnp.int32)
    (
        index,
        counts,
        picked,
        grad_picked,
        first,
        grad_mlp,
        router,
        scale,
        fc2_bias_sum,
        w_qkv,
        w_proj,
        proj_bias,
        ln2_gain,
        ln2_bias,
        bias_own,
        fc2_bias,
        ln1_gain,
        w_router,
    ) = call(
        front_kernel,
        [table, table]
        + [shape((rows, width), bf16)] * 4
        + [shape((rows, 1), f32)] * 2
        + [shape((1, width), f32)],
        (
            Far(kept_index),
            Far(tokens),
            Far(kept_count),
            Far(w_router),
            Far(ln1_gain),
            Far(ln1_bias),
            Far(cotangent),
        ),
        fetch=(
            w_qkv,
            w_proj,
            proj_bias,
            ln2_gain,
            ln2_bias,
            fc1_bias,
            fc2_bias,
            ln1_gain,
            w_router,
        ),
    )
    w_fc1_late, bias_other, first, w_qkv_other, w_proj_other = tie(
        (w_fc1, bias_other, first, w_qkv_other, w_proj_other)
    )
    w_fc1_other = other_core(w_fc1_late)

    made, made_other, mixed, mixed_other, attention, second, pack = call(
        functools.partial(attention_kernel, images),
        [
            shape((rows, 3 * local), bf16),
            shape((rows, 3 * local), bf16),
            shape((rows, local), bf16),
            shape((rows, local), bf16),
            shape((rows, width), f32),
            shape((rows, width), bf16),
            shape((rows, 2 * width + local), bf16),
        ],
        (
            counts,
            first,
            w_qkv,
            w_qkv_other,
            w_proj,
            w_proj_other,
            picked,
            proj_bias,
            ln2_gain,
            ln2_bias,
        ),
    )
    second, grad_mlp = tie((second, grad_mlp))
    grad_mlp_par = other_core(grad_mlp)

    def hidden(w, bias):
        return call(
            hidden_kernel,
            [shape((rows, units), bf16), shape((rows, units), f32)],
            (second, w, bias),
        )

    def hidden_back(w, slope):
        return call(
            hidden_back_kernel,
            [shape((rows, units), bf16), shape((units,), f32)],
            (grad_mlp, w, slope),
        )

    def mlp_weights(left, left_par, at_left, right, right_par):
        return weights(
            functools.partial(mlp_weights_kernel, at_left),
            (left, left_par, right, right_par),
            width,
            2 * rows,
            UNIT_BLOCK,
        )

    act_other, slope_other = hidden(w_fc1_other, bias_other)
    act_par = other_core(act_other)
    bias_own, act_other = tie((bias_own, act_other))
    act, slope = hidden(w_fc1, bias_own)
    w_fc2_late, act_par, grad_mlp_par, pack, slope = tie(
        (w_fc2, act_par, grad_mlp_par, pack, slope)
    )
    w_fc2_other = other_core(w_fc2_late)
    pack_par = other_core(pack)
    grad_pre, unit_own = hidden_back(w_fc2, slope)
    act, grad_pre = tie((act, grad_pre))
    halves = mlp_weights(grad_mlp, grad_mlp_par, 0, act, act_par)
    halves, slope_other = tie((halves, slope_other))
    fc2_sums = begin(halves, count, FC2_EARLY)
    grad_pre_other, unit_other = hidden_back(w_fc2_other, slope_other)
    grad_pre_par = other_core(grad_pre_other)
    grad_attn, grad_hidden, back_sums = call(
        back_kernel,
        [shape((rows, width), bf16), shape((rows, width), f32), shape((8, width), f32)],
        (
            grad_pre_other,
            w_fc1_other,
            grad_pre,
            w_fc1,
            picked,
            attention,
            grad_picked,
            scale,
            ln2_gain,
        ),
    )
    grad_pre, grad_attn = tie((grad_pre, grad_attn))
    halves = mlp_weights(second, pack_par, width, grad_pre, grad_pre_par)

    def attention_back(w, saved, grad):
        return call(
            functools.partial(heads_back, images),
            [shape((rows, 3 * local), bf16)],
            (counts, grad, w, saved),
            scratch=[pltpu.VMEM((rows, local), bf16)],
        )[0]

    halves, grad_attn = tie((halves, grad_attn))
    grad_qkv_other = attention_back(w_proj_other, made_other, grad_attn)
    fc1_sums = waiting(halves, FC1_EARLY)
    grad_attn, grad_qkv_other = exchange(
        (*fc2_sums, *fc1_sums), count, (grad_attn, grad_qkv_other)
    )
    grad_attn_par = other_core(grad_attn)
    grad_qkv_par = other_core(grad_qkv_other)
    grad_qkv = attention_back(w_proj, made, grad_attn)
    halves = weights(
        attn_weights_kernel,
        (first, pack_par, grad_attn, grad_attn_par, grad_qkv, grad_qkv_par, mixed),
        width,
        2 * rows,
        local + local // 3,
    )
    attn_sums = waiting(halves, ATTN_EARLY)
    act = exchange((*fc2_sums, *fc1_sums, *attn_sums), count, act)
    update, grad_logit, router_sum = call(
        branch_kernel,
        [shape((rows, width), f32), shape((rows, 1), f32), shape((1, width), f32)],
        (
            picked,
            grad_picked,
            router,
            scale,
            attention,
            act,
            act_other,
            w_fc2,
            w_fc2_other,
            fc2_bias,
        ),
    )

    sum_rows = 7 + units // width
    grad_kept, keep, send = call(
        first_back_kernel,
        [
            shape((rows, width), f32),
            shape((sum_rows, width), f32),
            shape((sum_rows, width), f32),
        ],
        (
            w_qkv,
            ln1_gain,
            w_router,
            picked,
            grad_hidden,
            grad_logit,
            grad_qkv,
            grad_qkv_other,
            w_qkv_other,
            fc2_bias_sum,
            router_sum,
            back_sums,
            unit_own,
            unit_other,
        ),
    )

    def put_back(base, change, *small):
        return call(
            functools.partial(put_back_kernel, len(small)),
            [Far(shape(base.shape, bf16)), *[shape(x.shape, x.dtype) for x in small[:1]]],
            (index, base, change, *small),
        )

    got = other_core(send)
    update, keep = tie((update, keep))
    output, small = put_back(tokens, update, keep, got)
    got = swap(small, 0, count)
    grad_kept, output = tie((grad_kept, output))
    (input_grad,) = put_back(cotangent, grad_kept)
    input_grad, small = exchange(
        (*fc2_sums, *fc1_sums, *attn_sums), count, input_grad, (small, got)
    )
    got = swap(small, 1, count)
    input_grad = arrived(fc2_sums, input_grad)
    input_grad, small = exchange((*fc1_sums, *attn_sums), count, input_grad, (small, got))
    got = swap(small, 2, count)
    input_grad = arrived(fc1_sums, input_grad)
    input_grad, small = exchange(attn_sums, count, input_grad, (small, got))
    for low in range(top):
        small = small + lax.ppermute(small, "dp", partners(count, low))
    got = swap(small, 3, count)
    sums = (*fc2_sums, *fc1_sums, *attn_sums)
    arrays, plans = listed(sums)
    plans = [(stream.part, stream.order, stream.unit, plan) for stream, plan in zip(sums, plans)]
    unit = width // UNITS
    fc2_turned, fc1_grad, qkv_grad, proj_turned, *sums = call(
        functools.partial(finish_kernel, len(arrays), 2, plans),
        [
            Far(shape((unit, units), f32)),
            Far(shape((unit, units), f32)),
            Far(shape((3, unit, local), f32)),
            Far(shape((unit, local), f32)),
            *[Far(shape((width,), f32))] * 7,
            Far(shape((units,), f32)),
        ],
        (*arrays, small, got),
    )
    fc2_turned, fc1_grad, proj_turned = (
        fewer_rows(grad, count, 0) for grad in (fc2_turned, fc1_grad, proj_turned)
    )
    qkv_grad = fewer_rows(qkv_grad, count, 1)
    return (
        output,
        input_grad,
        sums[0],
        sums[1],
        qkv_grad,
        proj_turned.T,
        sums[2],
        sums[3],
        sums[4],
        fc1_grad,
        sums[7],
        fc2_turned.T,
        sums[5],
        sums[6],
    )


def solution(mesh):
    batch = ("dp", "head")
    return jax.shard_map(
        on_device,
        mesh=mesh,
        in_specs=(
            P(batch, None, None),
            P(batch, None),
            P(batch),
            P(),
            P(),
            P(None, None, "head"),
            P("head", None),
            P(),
            P(),
            P(),
            P(None, "head"),
            P("head"),
            P("head", None),
            P(),
            P(),
            P(batch, None, None),
        ),
        out_specs=(
            P(batch, None, None),
            P(batch, None, None),
            P(),
            P(),
            P(None, "dp", "head"),
            P("head", "dp"),
            P(),
            P(),
            P(),
            P("dp", "head"),
            P("head"),
            P("head", "dp"),
            P(),
            P(),
        ),
        check_vma=False,
    )
```

```python
import functools

import jax
import jax.numpy as jnp
from jax import lax
from jax.experimental import pallas as pl
from jax.experimental.pallas import tpu as pltpu
from jax.sharding import PartitionSpec as P

HEAD_DIM = 64
norm_eps = 1e-06
root_half = 0.7071067811865476
inv_root_two_pi = 0.3989422804014327
f32, bf16 = jnp.float32, jnp.bfloat16


MIB = 1024 * 1024
SIDES = 2
FLOPS = 1
UNIT_BLOCK = 512


def rows_of(count):
    return -(-count // 16) * 16


def norm_stats(values):
    row_mean = jnp.mean(values, axis=-1, keepdims=True)
    centered = values - row_mean
    inv_std = lax.rsqrt(jnp.mean(centered * centered, axis=-1, keepdims=True) + norm_eps)
    return centered * inv_std, inv_std


def norm_back(grad_normed, gain, normed, inv_std):
    unit = grad_normed * gain
    return inv_std * (
        unit
        - jnp.mean(unit, axis=-1, keepdims=True)
        - normed * jnp.mean(unit * normed, axis=-1, keepdims=True)
    )


def dot(a, b, over=((1,), (0,))):
    return lax.dot_general(a, b, (over, ((), ())), preferred_element_type=f32)


def dot_turned(a, b):
    return dot(a, b, ((1,), (1,)))


def column_sum(values):
    return jnp.sum(values, axis=0, keepdims=True)


class Held:
    def __init__(self, ref, copy):
        self.ref, self.copy, self.shape = ref, copy, ref.shape

    def ready(self):
        if self.copy is not None:
            self.copy.wait()
            self.copy = None
        return self.ref

    def __getitem__(self, at):
        return self.ready()[at]


class Made:
    def __init__(self, ref, copy):
        self.ref, self.copy, self.shape, self.left = ref, copy, ref.shape, False

    def __getitem__(self, at):
        return self.ref[at]

    def __setitem__(self, at, value):
        self.ref[at] = value

    def leave(self):
        if not self.left:
            self.copy.start()
            self.left = True


class Far:
    def __init__(self, value):
        self.value = value


def call(kernel, out_shape, inputs, scratch=(), fetch=(), room=14):
    inputs = [*inputs, *[Far(x) for x in fetch]]
    values = [x.value if isinstance(x, Far) else x for x in inputs]
    shapes = [x.value if isinstance(x, Far) else x for x in out_shape]
    shapes += [shape(x.shape, x.dtype) for x in fetch]
    n_fetch, n_in, n_out = len(fetch), len(inputs), len(shapes)
    far_in = [i for i in range(n_in - n_fetch) if isinstance(inputs[i], Far)]
    far_out = [i for i, x in enumerate(out_shape) if isinstance(x, Far)]
    near, away = pl.BlockSpec(memory_space=pltpu.VMEM), pl.BlockSpec(memory_space=pltpu.HBM)
    in_hbm = [isinstance(x, Far) for x in inputs]

    def body(*refs):
        ins, outs, refs = list(refs[:n_in]), list(refs[n_in : n_in + n_out]), refs[n_in + n_out :]
        in_refs, refs = refs[: len(far_in)], refs[len(far_in) :]
        out_refs, refs = refs[: len(far_out)], refs[len(far_out) :]
        sems, extra = (refs[0], refs[1:]) if n_sems else (None, refs)
        for n, i in enumerate(far_in):
            copy = pltpu.make_async_copy(ins[i], in_refs[n], sems.at[n])
            copy.start()
            ins[i] = Held(in_refs[n], copy)
        for n, i in enumerate(far_out):
            copy = pltpu.make_async_copy(out_refs[n], outs[i], sems.at[len(far_in) + n])
            outs[i] = Made(out_refs[n], copy)
        fetched = []
        for n in range(n_fetch):
            copy = pltpu.make_async_copy(
                ins[n_in - n_fetch + n],
                outs[n_out - n_fetch + n],
                sems.at[len(far_in) + len(far_out) + n],
            )
            copy.start()
            fetched.append(copy)
        kernel(*ins[: n_in - n_fetch], *outs[: n_out - n_fetch], *extra)
        for i in far_in:
            ins[i].ready()
        for i in far_out:
            outs[i].leave()
        for copy in fetched:
            copy.wait()
        for i in far_out:
            outs[i].copy.wait()

    def landing(x):
        return (pltpu.SMEM if x.dtype == jnp.int32 and x.ndim == 1 else pltpu.VMEM)(x.shape, x.dtype)

    far_scratch = [landing(values[i]) for i in far_in]
    far_scratch += [pltpu.VMEM(shapes[i].shape, shapes[i].dtype) for i in far_out]
    n_sems = len(far_in) + len(far_out) + n_fetch
    if n_sems:
        far_scratch.append(pltpu.SemaphoreType.DMA((n_sems,)))
    values = [
        pltpu.with_memory_space_constraint(x, pltpu.HBM if far else pltpu.VMEM)
        for x, far in zip(values, in_hbm)
    ]
    return pl.pallas_call(
        body,
        out_shape=[
            (pltpu.HBM if i in far_out else pltpu.VMEM)(o.shape, o.dtype)
            for i, o in enumerate(shapes)
        ],
        in_specs=[away if far else near for far in in_hbm],
        out_specs=[away if i in far_out else near for i in range(n_out)],
        scratch_shapes=[*far_scratch, *scratch],
        compiler_params=pltpu.CompilerParams(vmem_limit_bytes=room * MIB),
        cost_estimate=pl.CostEstimate(flops=FLOPS, bytes_accessed=1, transcendentals=0),
    )(*values)


def line(ref):
    return ref[...].reshape(1, -1)


def shape(dims, kind):
    return jax.ShapeDtypeStruct(dims, kind)


def turned_hot(index_ref, image, slots, padded):
    place = lax.broadcasted_iota(jnp.int32, (slots, padded), 0)
    return jnp.where(place == index_ref[image : image + 1, :padded], 1.0, 0.0).astype(bf16)


def front_kernel(
    index_in_ref,
    tokens_ref,
    count_in_ref,
    router_w_ref,
    gain_ref,
    shift_ref,
    cotangent_ref,
    index_ref,
    count_ref,
    picked_ref,
    grad_picked_ref,
    first_ref,
    grad_mlp_ref,
    router_ref,
    scale_ref,
    fc2_bias_grad_ref,
):
    images, slots, _ = tokens_ref.shape
    padded = picked_ref.shape[0] // images
    index_ref[...] = jnp.full(index_ref.shape, -1, jnp.int32)
    index_ref[:images, : index_in_ref.shape[1]] = index_in_ref[...]
    for b in range(images):
        hot = turned_hot(index_ref, b, slots, padded)
        picked_ref[b * padded : (b + 1) * padded, :] = dot(hot, tokens_ref[b], ((0,), (0,))).astype(
            bf16
        )
    picked = picked_ref[...].astype(f32)
    router = jax.nn.sigmoid(jnp.sum(picked * line(router_w_ref), axis=-1, keepdims=True))
    router_ref[...] = router
    normed, _ = norm_stats(picked)
    first_ref[...] = (normed * line(gain_ref) + line(shift_ref)).astype(bf16)
    rows = lax.broadcasted_iota(jnp.int32, (padded, 1), 0)
    for b in range(images):
        count_ref[b : b + 1, :] = jnp.full((1, count_ref.shape[1]), count_in_ref[b], jnp.int32)
        at = slice(b * padded, (b + 1) * padded)
        live = jnp.where(rows < count_in_ref[b], 1.0, 0.0).astype(f32)
        scale_ref[at, :] = live * router_ref[at, :]
        hot = turned_hot(index_ref, b, slots, padded)
        grad_picked_ref[at, :] = dot(hot, cotangent_ref[b], ((0,), (0,))).astype(bf16)
    grad_branch = scale_ref[...] * grad_picked_ref[...].astype(f32)
    grad_mlp_ref[...] = grad_branch.astype(bf16)
    fc2_bias_grad_ref[...] = column_sum(grad_branch)


def stacked_heads(pair):
    lane = lax.broadcasted_iota(jnp.int32, pair.shape, 1)
    zero = jnp.zeros_like(pair)
    return jnp.concatenate(
        [jnp.where(lane < HEAD_DIM, pair, zero), jnp.where(lane < HEAD_DIM, zero, pair)], axis=0
    )


def joined_heads(stacked):
    half = stacked.shape[0] // 2
    lane = lax.broadcasted_iota(jnp.int32, (half, stacked.shape[1]), 1)
    return jnp.where(lane < HEAD_DIM, stacked[:half], stacked[half:])


def pairs_of_heads(images, padded, local):
    return [
        (b, slice(b * padded, (b + 1) * padded), at)
        for b in range(images)
        for at in range(0, local, 2 * HEAD_DIM)
    ]


def saved_qkv(made_ref, rows, at):
    local = made_ref.shape[1] // 3
    return [made_ref[rows, t * local + at : t * local + at + 2 * HEAD_DIM] for t in range(3)]


def probabilities(scores, count, axis):
    key = lax.broadcasted_iota(jnp.int32, scores.shape, axis)
    scores = jnp.where(key < count, scores, -1e30)
    raised = jnp.exp(scores - jnp.max(scores, axis=axis, keepdims=True))
    return raised * (1.0 / jnp.sum(raised, axis=axis, keepdims=True))


def project(first_ref, w_ref, made_ref):
    local = w_ref.shape[2]
    for t in range(3):
        made_ref[:, t * local : (t + 1) * local] = dot(first_ref[...], w_ref[t]).astype(bf16)


def attend(images, count_ref, made_ref, mixed_ref):
    padded, local = made_ref.shape[0] // images, mixed_ref.shape[1]
    units = pairs_of_heads(images, padded, local)
    qkv = [saved_qkv(made_ref, rows, at) for _, rows, at in units]
    scores = [dot_turned(stacked_heads(q), k) * HEAD_DIM ** (-0.5) for q, k, _ in qkv]
    probs = [
        probabilities(x, count_ref[b : b + 1, 0:1], 1).astype(bf16)
        for x, (b, _, _) in zip(scores, units)
    ]
    mixed = [joined_heads(dot(x, v)) for x, (_, _, v) in zip(probs, qkv)]
    for x, (_, rows, at) in zip(mixed, units):
        mixed_ref[rows, at : at + 2 * HEAD_DIM] = x.astype(bf16)


def attention_kernel(
    images,
    count_ref,
    first_ref,
    w_own_ref,
    w_other_ref,
    proj_own_ref,
    proj_other_ref,
    picked_ref,
    proj_bias_ref,
    gain_ref,
    shift_ref,
    made_own_ref,
    made_other_ref,
    mixed_own_ref,
    mixed_other_ref,
    attention_ref,
    second_ref,
    pack_ref,
):
    width = first_ref.shape[1]
    pack_ref[:, :width] = first_ref[...]
    project(first_ref, w_own_ref, made_own_ref)
    project(first_ref, w_other_ref, made_other_ref)
    attend(images, count_ref, made_own_ref, mixed_own_ref)
    attend(images, count_ref, made_other_ref, mixed_other_ref)
    total = line(proj_bias_ref) + dot(mixed_own_ref[...], proj_own_ref[...])
    total = total + dot(mixed_other_ref[...], proj_other_ref[...])
    attention_ref[...] = total
    normed, _ = norm_stats(picked_ref[...].astype(f32) + total)
    second = (normed * line(gain_ref) + line(shift_ref)).astype(bf16)
    second_ref[...] = second
    pack_ref[:, width : 2 * width] = second
    pack_ref[:, 2 * width :] = mixed_other_ref[...]


def hidden_kernel(second_ref, w_fc1_ref, bias_ref, act_ref, slope_ref):
    for at in range(0, act_ref.shape[1], UNIT_BLOCK):
        block = slice(at, at + UNIT_BLOCK)
        pre = dot(second_ref[...], w_fc1_ref[:, block]) + bias_ref[block].reshape(1, -1)
        half = 0.5 * (1.0 + lax.erf(pre * root_half))
        act_ref[:, block] = (pre * half).astype(bf16)
        slope_ref[:, block] = half + pre * inv_root_two_pi * jnp.exp(-0.5 * pre * pre)


def hidden_back_kernel(grad_mlp_ref, w_fc2_ref, slope_ref, grad_pre_ref, unit_sum_ref):
    for at in range(0, slope_ref.shape[1], UNIT_BLOCK):
        block = slice(at, at + UNIT_BLOCK)
        grad_pre = dot_turned(grad_mlp_ref[...], w_fc2_ref[block, :]) * slope_ref[:, block]
        unit_sum_ref[block] = column_sum(grad_pre).reshape(UNIT_BLOCK)
        grad_pre_ref[:, block] = grad_pre.astype(bf16)


TOP_BITS = 4
FC2_EARLY, FC1_EARLY, ATTN_EARLY = 1, 0, 0
UNITS = 1 << TOP_BITS


def my_bits():
    place = lax.axis_index("dp") >> (lax.axis_size("dp").bit_length() - 1 - TOP_BITS)
    return [(place >> bit) & 1 for bit in range(TOP_BITS)]


def order_of(part, early=0):
    order = [(part + j) % 3 for j in range(3)] + [3]
    return order[:2] + [3, order[2]] if part < early else order


def bits_left(order, step):
    return [bit for bit in range(TOP_BITS - 1, -1, -1) if bit not in order[:step]]


def every_choice(bits):
    for j in range(1 << len(bits)):
        yield j, {bit: (j >> (len(bits) - 1 - i)) & 1 for i, bit in enumerate(bits)}


def unit_rows(ref, spread, chosen, unit, base=0):
    place = 0
    for bit in spread:
        place = place * 2 + chosen[bit]
    return ref[pl.ds(pl.multiple_of(base + place * unit, 16), unit), :]


def arrange_rows(turned_ref, mine, part, arranged_ref):
    unit = turned_ref.shape[0] // UNITS
    order = order_of(part)
    bit = order[0]
    for side, value in enumerate((1 - mine[bit], mine[bit])):
        for j, chosen in every_choice(bits_left(order, 1)):
            chosen[bit] = value
            to = (side * UNITS // 2 + j) * unit
            arranged_ref[to : to + unit, :] = unit_rows(
                turned_ref, bits_left(order, 0), chosen, unit
            )


class Stream:
    def __init__(self, part, away, kept, early):
        self.part, self.step, self.away, self.terms = part, 0, away, [(kept, 0, 1)]
        self.order = order_of(part, early)
        self.unit = kept.shape[0] * 2 // UNITS

    def bit(self):
        return self.order[self.step]

    def rows(self):
        return self.unit * UNITS >> (self.step + 1)

    def sent(self, got, base):
        self.step += 1
        self.away = None
        self.terms.append((got, base, self.step))


def listed(streams):
    arrays, plans = [], []
    for stream in streams:
        terms = [(stream.away, 0, 0)] if stream.away is not None else stream.terms
        plan = []
        for array, base, step in terms:
            found = [n for n, x in enumerate(arrays) if x is array]
            if not found:
                found = [len(arrays)]
                arrays.append(array)
            plan.append((found[0], base, step))
        plans.append(plan)
    return arrays, plans


def plan_sum(refs, plan, order, chosen, unit):
    total = 0.0
    for n, base, step in plan:
        total = total + unit_rows(refs[n], bits_left(order, step), chosen, unit, base).astype(f32)
    return total


def step_kernel(n_arrays, n_small, plans, *refs):
    mine = my_bits()
    small, outs = refs[n_arrays : n_arrays + n_small], refs[n_arrays + n_small :]
    if n_small:
        outs[-1][...] = sum(ref[...] for ref in small)
    for order, step, made, unit, plan, out, base in plans:
        if made:
            ref = refs[plan[0][0]]
            outs[out][base : base + ref.shape[0], :] = ref[...]
            continue
        for j, chosen in every_choice(bits_left(order, step + 1)):
            for bit in order[:step]:
                chosen[bit] = mine[bit]
            chosen[order[step]] = 1 - mine[order[step]]
            to = base + j * unit
            outs[out][to : to + unit, :] = plan_sum(refs, plan, order, chosen, unit).astype(bf16)


def mlp_finish_kernel(n_arrays, plans, *refs):
    mine = my_bits()
    chosen = {bit: mine[bit] for bit in range(TOP_BITS)}
    outs = refs[n_arrays:]
    for i, (part, order, unit, plan) in enumerate(plans):
        total = plan_sum(refs, plan, order, chosen, unit)
        outs[i // 3][:, part * UNIT_BLOCK : (part + 1) * UNIT_BLOCK] = total


def attn_finish_kernel(n_arrays, n_small, plans, *refs):
    mine = my_bits()
    chosen = {bit: mine[bit] for bit in range(TOP_BITS)}
    small, (qkv_ref, proj_ref, *outs) = (
        refs[n_arrays : n_arrays + n_small],
        refs[n_arrays + n_small :],
    )
    local = qkv_ref.shape[2]
    third = local // 3
    for part, order, unit, plan in plans:
        total = plan_sum(refs, plan, order, chosen, unit)
        qkv_ref[part] = total[:, :local]
        proj_ref[:, part * third : (part + 1) * third] = total[:, local:]
    total = sum(ref[...] for ref in small)
    width = total.shape[1]
    for i, out_ref in enumerate(outs[:-1]):
        out_ref[...] = total[i : i + 1, :].reshape(width)
    for i in range(total.shape[0] - 7):
        outs[-1][i * width : (i + 1) * width] = total[7 + i : 8 + i, :].reshape(width)


def both_rows(own, other):
    return jnp.concatenate([own, other], axis=0)


def weight_tile(arranged_ref, right, away_ref, kept_ref, columns):
    half = away_ref.shape[0]
    away_ref[:, columns] = dot(arranged_ref[:half, :], right).astype(bf16)
    kept_ref[:, columns] = dot(arranged_ref[half:, :], right)


def mlp_weights_kernel(at_left, left_own_ref, left_par_ref, right_own_ref, right_par_ref, *outs):
    away_refs, kept_refs, (turned_ref, arranged_ref) = outs[:3], outs[3:6], outs[6:]
    mine = my_bits()
    left_par = left_par_ref[:, at_left : at_left + left_own_ref.shape[1]]
    turned_ref[...] = both_rows(left_own_ref[...], left_par).T
    columns = slice(0, UNIT_BLOCK)
    for part in range(3):
        at = slice(part * UNIT_BLOCK, (part + 1) * UNIT_BLOCK)
        right = both_rows(right_own_ref[:, at], right_par_ref[:, at])
        arrange_rows(turned_ref, mine, part, arranged_ref)
        weight_tile(arranged_ref, right, away_refs[part], kept_refs[part], columns)


def attn_weights_kernel(
    first_own_ref,
    pack_par_ref,
    grad_attn_own_ref,
    grad_attn_par_ref,
    qkv_own_ref,
    qkv_par_ref,
    mixed_own_ref,
    *outs,
):
    away_refs, kept_refs, (turned_ref, arranged_ref) = outs[:3], outs[3:6], outs[6:]
    mine = my_bits()
    width, local = first_own_ref.shape[1], mixed_own_ref.shape[1]
    third = local // 3
    turned_ref[...] = both_rows(first_own_ref[...], pack_par_ref[:, :width]).T
    for part in range(3):
        at = slice(part * local, (part + 1) * local)
        right = both_rows(qkv_own_ref[:, at], qkv_par_ref[:, at])
        arrange_rows(turned_ref, mine, part, arranged_ref)
        weight_tile(arranged_ref, right, away_refs[part], kept_refs[part], slice(0, local))
    turned_ref[...] = both_rows(grad_attn_own_ref[...], grad_attn_par_ref[...]).T
    for part in range(3):
        at = slice(part * third, (part + 1) * third)
        right = both_rows(mixed_own_ref[:, at], pack_par_ref[:, 2 * width + at.start : 2 * width + at.stop])
        arrange_rows(turned_ref, mine, part, arranged_ref)
        weight_tile(
            arranged_ref, right, away_refs[part], kept_refs[part], slice(local, local + third)
        )


def weights(kernel, arrays, width, depth, columns):
    half = width // 2
    return call(
        kernel,
        [shape((half, columns), bf16)] * 3 + [shape((half, columns), f32)] * 3,
        arrays,
        scratch=[pltpu.VMEM((width, depth), bf16), pltpu.VMEM((width, depth), bf16)],
    )


def heads_back(images, count_ref, grad_attn_ref, proj_ref, made_ref, out_ref, mixed_scratch):
    padded, local = made_ref.shape[0] // images, proj_ref.shape[0]
    factor = HEAD_DIM ** (-0.5)
    mixed_scratch[...] = dot_turned(grad_attn_ref[...], proj_ref[...]).astype(bf16)
    units = pairs_of_heads(images, padded, local)
    for first in range(0, len(units), 3):
        some = units[first : first + 3]
        q, k, v = zip(*[saved_qkv(made_ref, rows, at) for _, rows, at in some])
        q = [stacked_heads(x) for x in q]
        grad_mixed = [
            stacked_heads(mixed_scratch[rows, at : at + 2 * HEAD_DIM]) for _, rows, at in some
        ]
        scores = [dot_turned(x, y) * factor for x, y in zip(k, q)]
        grad_probs = [dot_turned(x, y) for x, y in zip(v, grad_mixed)]
        probs = [
            probabilities(x, count_ref[b : b + 1, 0:1], 0) for x, (b, _, _) in zip(scores, some)
        ]
        grad_scores = [
            (p * (g - jnp.sum(p * g, axis=0, keepdims=True))).astype(bf16)
            for p, g in zip(probs, grad_probs)
        ]
        grad_k = [dot(x, y) * factor for x, y in zip(grad_scores, q)]
        grad_v = [dot(x.astype(bf16), y) for x, y in zip(probs, grad_mixed)]
        grad_q = [joined_heads(dot(x, y, ((0,), (0,)))) * factor for x, y in zip(grad_scores, k)]
        for (_, rows, at), *found in zip(some, grad_q, grad_k, grad_v):
            for t in range(3):
                to = slice(t * local + at, t * local + at + 2 * HEAD_DIM)
                out_ref[rows, to] = found[t].astype(bf16)


def back_kernel(
    grad_pre_other_ref,
    w_fc1_other_ref,
    grad_pre_ref,
    w_fc1_ref,
    picked_ref,
    attention_ref,
    grad_picked_ref,
    scale_ref,
    gain_ref,
    grad_attn_ref,
    grad_hidden_ref,
    sums_ref,
):
    grad_second = dot_turned(grad_pre_other_ref[...], w_fc1_other_ref[...])
    grad_second = grad_second + dot_turned(grad_pre_ref[...], w_fc1_ref[...])
    normed, inv_std = norm_stats(picked_ref[...].astype(f32) + attention_ref[...])
    grad_hidden = norm_back(grad_second, line(gain_ref), normed, inv_std)
    grad_hidden_ref[...] = grad_hidden
    grad_attention = scale_ref[...] * grad_picked_ref[...].astype(f32) + grad_hidden
    grad_attn_ref[...] = grad_attention.astype(bf16)
    sums_ref[0:1, :] = column_sum(grad_attention)
    sums_ref[1:2, :] = column_sum(grad_second * normed)
    sums_ref[2:3, :] = column_sum(grad_second)


def branch_kernel(
    picked_ref,
    grad_picked_ref,
    router_ref,
    scale_ref,
    attention_ref,
    act_own_ref,
    act_other_ref,
    w_fc2_ref,
    w_fc2_other_ref,
    fc2_bias_ref,
    update_ref,
    grad_logit_ref,
    router_grad_ref,
):
    scale = scale_ref[...]
    mlp_out = dot(act_own_ref[...], w_fc2_ref[...]) + dot(act_other_ref[...], w_fc2_other_ref[...])
    branch = attention_ref[...] + (mlp_out + line(fc2_bias_ref))
    update_ref[...] = scale * branch
    grad_logit = (
        scale
        * (1.0 - router_ref[...])
        * jnp.sum(grad_picked_ref[...].astype(f32) * branch, axis=-1, keepdims=True)
    )
    grad_logit_ref[...] = grad_logit
    router_grad_ref[...] = column_sum(grad_logit * picked_ref[...].astype(f32))


def first_back_kernel(
    qkv_own_ref,
    gain_ref,
    router_w_ref,
    picked_ref,
    grad_hidden_ref,
    grad_logit_ref,
    grad_qkv_own_ref,
    grad_qkv_other_ref,
    qkv_other_ref,
    fc2_bias_grad_ref,
    router_grad_ref,
    back_sums_ref,
    unit_own_ref,
    unit_other_ref,
    grad_kept_ref,
    keep_ref,
    send_ref,
):
    width = picked_ref.shape[1]
    local = qkv_other_ref.shape[2]
    grad_first = jnp.zeros(picked_ref.shape, f32)
    for side in range(SIDES):
        for t in range(3):
            grad_first = grad_first + dot_turned(
                (grad_qkv_own_ref, grad_qkv_other_ref)[side][:, t * local : (t + 1) * local],
                (qkv_own_ref, qkv_other_ref)[side][t],
            )
    normed, inv_std = norm_stats(picked_ref[...].astype(f32))
    grad_kept_ref[...] = (
        norm_back(grad_first, line(gain_ref), normed, inv_std)
        + grad_hidden_ref[...]
        + grad_logit_ref[...] * line(router_w_ref)
    )
    sums = (
        column_sum(grad_first * normed),
        column_sum(grad_first),
        back_sums_ref[0:1, :],
        back_sums_ref[1:2, :],
        back_sums_ref[2:3, :],
        fc2_bias_grad_ref[...],
        router_grad_ref[...],
    )
    for i, values in enumerate(sums):
        keep_ref[i : i + 1, :] = values
        send_ref[i : i + 1, :] = values
    for i in range(unit_own_ref.shape[0] // width):
        at = slice(i * width, (i + 1) * width)
        keep_ref[7 + i : 8 + i, :] = unit_own_ref[at].reshape(1, width)
        send_ref[7 + i : 8 + i, :] = unit_other_ref[at].reshape(1, width)


def put_back_kernel(n_small, index_ref, base_ref, change_ref, *refs):
    small_refs, outs = refs[:n_small], refs[n_small:]
    if n_small:
        outs[1][...] = sum(ref[...] for ref in small_refs)
    images, slots, _ = base_ref.shape
    padded = change_ref.shape[0] // images
    for b in range(images):
        hot = turned_hot(index_ref, b, slots, padded)
        change = change_ref[b * padded : (b + 1) * padded, :]
        high = change.astype(bf16)
        low = (change - high.astype(f32)).astype(bf16)
        updated = base_ref[b].astype(f32) + (dot(hot, high) + dot(hot, low))
        outs[0][b] = updated.astype(bf16)


def other_core(value):
    return lax.ppermute(value, "head", [(0, 1), (1, 0)])


def partners(count, bit):
    return [(i, i ^ (1 << bit)) for i in range(count)]


def swap(value, bit, count):
    return lax.ppermute(value, "dp", partners(count, bit + count.bit_length() - 1 - TOP_BITS))


def waiting(halves, early=0):
    return [Stream(part, halves[part], halves[3 + part], early) for part in range(3)]


def begin(halves, count, early=0):
    streams = waiting(halves, early)
    for stream in streams:
        stream.sent(swap(stream.away, stream.bit(), count), 0)
    return streams


def exchange(streams, count, after, small=()):
    arrays, plans = listed(streams)
    tied, after = lax.optimization_barrier((tuple(arrays), after))
    bits = []
    for stream in streams:
        if stream.bit() not in bits:
            bits.append(stream.bit())
    sizes, full, bases = [0] * len(bits), [], []
    for stream, plan in zip(streams, plans):
        out = bits.index(stream.bit())
        made = stream.away is not None
        full.append((stream.order, stream.step, made, stream.unit, plan, out, sizes[out]))
        bases.append(sizes[out])
        sizes[out] += stream.rows()
    columns = arrays[0].shape[1]
    outs = [shape((size, columns), bf16) for size in sizes]
    outs += [shape(array.shape, array.dtype) for array in small[:1]]
    made = call(
        functools.partial(step_kernel, len(arrays), len(small), full), outs, (*tied, *small)
    )
    made, after = lax.optimization_barrier((made, after))
    got = [swap(made[n], bit, count) for n, bit in enumerate(bits)]
    for stream, base in zip(streams, bases):
        stream.sent(got[bits.index(stream.bit())], base)
    return (after, made[-1]) if small else after


def arrived(streams, after):
    arrays = []
    for stream in streams:
        if all(stream.terms[-1][0] is not x for x in arrays):
            arrays.append(stream.terms[-1][0])
    tied, after = lax.optimization_barrier((arrays, after))
    for stream in streams:
        array, base, step = stream.terms[-1]
        place = [x is array for x in arrays].index(True)
        stream.terms[-1] = (tied[place], base, step)
    return after


def fewer_rows(grad, count, axis):
    place = lax.axis_index("dp")
    for bit in range(count.bit_length() - 2 - TOP_BITS, -1, -1):
        half = grad.shape[axis] // 2
        mine = (place >> bit) & 1
        away = lax.dynamic_slice_in_dim(grad, (1 - mine) * half, half, axis).astype(bf16)
        kept = lax.dynamic_slice_in_dim(grad, mine * half, half, axis)
        grad = kept + lax.ppermute(away, "dp", partners(count, bit)).astype(f32)
    return grad


def on_device(
    tokens,
    kept_index,
    kept_count,
    ln1_gain,
    ln1_bias,
    w_qkv,
    w_proj,
    proj_bias,
    ln2_gain,
    ln2_bias,
    w_fc1,
    fc1_bias,
    w_fc2,
    fc2_bias,
    w_router,
    cotangent,
):
    images, slots, width = tokens.shape
    padded = rows_of(kept_index.shape[1])
    rows = images * padded
    local = w_qkv.shape[2]
    units = w_fc1.shape[1]
    count = lax.axis_size("dp")

    top = count.bit_length() - 1 - TOP_BITS
    w_qkv_other = other_core(w_qkv)
    w_proj_other = other_core(w_proj)
    bias_other = other_core(fc1_bias)
    tie = lax.optimization_barrier
    table = shape((8, 128), jnp.int32)
    (
        index,
        counts,
        picked,
        grad_picked,
        first,
        grad_mlp,
        router,
        scale,
        fc2_bias_sum,
        w_qkv,
        w_proj,
        proj_bias,
        ln2_gain,
        ln2_bias,
        bias_own,
        fc2_bias,
        ln1_gain,
        w_router,
    ) = call(
        front_kernel,
        [table, table]
        + [shape((rows, width), bf16)] * 4
        + [shape((rows, 1), f32)] * 2
        + [shape((1, width), f32)],
        (
            Far(kept_index),
            Far(tokens),
            Far(kept_count),
            Far(w_router),
            Far(ln1_gain),
            Far(ln1_bias),
            Far(cotangent),
        ),
        fetch=(
            w_qkv,
            w_proj,
            proj_bias,
            ln2_gain,
            ln2_bias,
            fc1_bias,
            fc2_bias,
            ln1_gain,
            w_router,
        ),
    )
    grad_mlp_par = other_core(grad_mlp)
    w_fc1_late, bias_other, first, w_qkv_other, w_proj_other = tie(
        (w_fc1, bias_other, first, w_qkv_other, w_proj_other)
    )
    w_fc1_other = other_core(w_fc1_late)

    made, made_other, mixed, mixed_other, attention, second, pack = call(
        functools.partial(attention_kernel, images),
        [
            shape((rows, 3 * local), bf16),
            shape((rows, 3 * local), bf16),
            shape((rows, local), bf16),
            shape((rows, local), bf16),
            shape((rows, width), f32),
            shape((rows, width), bf16),
            shape((rows, 2 * width + local), bf16),
        ],
        (
            counts,
            first,
            w_qkv,
            w_qkv_other,
            w_proj,
            w_proj_other,
            picked,
            proj_bias,
            ln2_gain,
            ln2_bias,
        ),
    )
    second, grad_mlp_par, w_fc2_late = tie((second, grad_mlp_par, w_fc2))
    w_fc2_other = other_core(w_fc2_late)

    def hidden(w, bias):
        return call(
            hidden_kernel,
            [shape((rows, units), bf16), shape((rows, units), f32)],
            (second, w, bias),
        )

    def hidden_back(w, slope):
        return call(
            hidden_back_kernel,
            [shape((rows, units), bf16), shape((units,), f32)],
            (grad_mlp, w, slope),
        )

    def mlp_weights(left, left_par, at_left, right, right_par):
        return weights(
            functools.partial(mlp_weights_kernel, at_left),
            (left, left_par, right, right_par),
            width,
            2 * rows,
            UNIT_BLOCK,
        )

    act_other, slope_other = hidden(w_fc1_other, bias_other)
    act_par = other_core(act_other)
    bias_own, act_other = tie((bias_own, act_other))
    act, slope = hidden(w_fc1, bias_own)
    grad_pre, unit_own = hidden_back(w_fc2, slope)
    slope_other, grad_pre = tie((slope_other, grad_pre))
    grad_pre_other, unit_other = hidden_back(w_fc2_other, slope_other)
    act, grad_pre, grad_pre_other, pack = tie((act, grad_pre, grad_pre_other, pack))
    halves = mlp_weights(grad_mlp, grad_mlp_par, 0, act, act_par)
    grad_pre_par = other_core(grad_pre_other)
    pack_par = other_core(pack)
    halves, grad_pre_other = tie((halves, grad_pre_other))
    fc2_sums = begin(halves, count, FC2_EARLY)
    grad_attn, grad_hidden, back_sums = call(
        back_kernel,
        [shape((rows, width), bf16), shape((rows, width), f32), shape((8, width), f32)],
        (
            grad_pre_other,
            w_fc1_other,
            grad_pre,
            w_fc1,
            picked,
            attention,
            grad_picked,
            scale,
            ln2_gain,
        ),
    )
    grad_pre, grad_attn = tie((grad_pre, grad_attn))
    halves = mlp_weights(second, pack_par, width, grad_pre, grad_pre_par)

    def attention_back(w, saved, grad):
        return call(
            functools.partial(heads_back, images),
            [shape((rows, 3 * local), bf16)],
            (counts, grad, w, saved),
            scratch=[pltpu.VMEM((rows, local), bf16)],
        )[0]

    halves, grad_attn = tie((halves, grad_attn))
    grad_qkv_other = attention_back(w_proj_other, made_other, grad_attn)
    fc1_sums = waiting(halves, FC1_EARLY)
    grad_attn, grad_qkv_other = exchange(
        (*fc2_sums, *fc1_sums), count, (grad_attn, grad_qkv_other)
    )
    grad_attn_par = other_core(grad_attn)
    grad_qkv_par = other_core(grad_qkv_other)
    grad_qkv = attention_back(w_proj, made, grad_attn)
    halves = weights(
        attn_weights_kernel,
        (first, pack_par, grad_attn, grad_attn_par, grad_qkv, grad_qkv_par, mixed),
        width,
        2 * rows,
        local + local // 3,
    )
    attn_sums = waiting(halves, ATTN_EARLY)
    act = exchange((*fc2_sums, *fc1_sums, *attn_sums), count, act)
    update, grad_logit, router_sum = call(
        branch_kernel,
        [shape((rows, width), f32), shape((rows, 1), f32), shape((1, width), f32)],
        (
            picked,
            grad_picked,
            router,
            scale,
            attention,
            act,
            act_other,
            w_fc2,
            w_fc2_other,
            fc2_bias,
        ),
    )

    sum_rows = 7 + units // width
    grad_kept, keep, send = call(
        first_back_kernel,
        [
            shape((rows, width), f32),
            shape((sum_rows, width), f32),
            shape((sum_rows, width), f32),
        ],
        (
            w_qkv,
            ln1_gain,
            w_router,
            picked,
            grad_hidden,
            grad_logit,
            grad_qkv,
            grad_qkv_other,
            w_qkv_other,
            fc2_bias_sum,
            router_sum,
            back_sums,
            unit_own,
            unit_other,
        ),
    )

    def put_back(base, change, *small):
        return call(
            functools.partial(put_back_kernel, len(small)),
            [Far(shape(base.shape, bf16)), *[shape(x.shape, x.dtype) for x in small[:1]]],
            (index, base, change, *small),
        )

    got = other_core(send)
    update, keep = tie((update, keep))
    output, small = put_back(tokens, update, keep, got)
    got = swap(small, 0, count)
    grad_kept, output = tie((grad_kept, output))
    (input_grad,) = put_back(cotangent, grad_kept)
    input_grad, small = exchange(
        (*fc2_sums, *fc1_sums, *attn_sums), count, input_grad, (small, got)
    )
    got = swap(small, 1, count)
    input_grad, small = exchange((*fc1_sums, *attn_sums), count, input_grad, (small, got))
    small = arrived(fc2_sums, small)
    got = swap(small, 2, count)
    input_grad, small = exchange(attn_sums, count, input_grad, (small, got))
    for low in range(top):
        small = small + lax.ppermute(small, "dp", partners(count, low))
    got = swap(small, 3, count)
    unit = width // UNITS

    def final(streams):
        arrays, plans = listed(streams)
        return arrays, [
            (stream.part, stream.order, stream.unit, plan) for stream, plan in zip(streams, plans)
        ]

    arrays, plans = final((*fc2_sums, *fc1_sums))
    fc2_turned, fc1_grad = call(
        functools.partial(mlp_finish_kernel, len(arrays), plans),
        [Far(shape((unit, units), f32)), Far(shape((unit, units), f32))],
        tuple(arrays),
    )
    small, fc2_turned, fc1_grad = tie((small, fc2_turned, fc1_grad))
    arrays, plans = final(attn_sums)
    qkv_grad, proj_turned, *sums = call(
        functools.partial(attn_finish_kernel, len(arrays), 2, plans),
        [
            Far(shape((3, unit, local), f32)),
            Far(shape((unit, local), f32)),
            *[Far(shape((width,), f32))] * 7,
            Far(shape((units,), f32)),
        ],
        (*arrays, small, got),
    )
    fc2_turned, fc1_grad, proj_turned = (
        fewer_rows(grad, count, 0) for grad in (fc2_turned, fc1_grad, proj_turned)
    )
    qkv_grad = fewer_rows(qkv_grad, count, 1)
    return (
        output,
        input_grad,
        sums[0],
        sums[1],
        qkv_grad,
        proj_turned.T,
        sums[2],
        sums[3],
        sums[4],
        fc1_grad,
        sums[7],
        fc2_turned.T,
        sums[5],
        sums[6],
    )


def solution(mesh):
    batch = ("dp", "head")
    return jax.shard_map(
        on_device,
        mesh=mesh,
        in_specs=(
            P(batch, None, None),
            P(batch, None),
            P(batch),
            P(),
            P(),
            P(None, None, "head"),
            P("head", None),
            P(),
            P(),
            P(),
            P(None, "head"),
            P("head"),
            P("head", None),
            P(),
            P(),
            P(batch, None, None),
        ),
        out_specs=(
            P(batch, None, None),
            P(batch, None, None),
            P(),
            P(),
            P(None, "dp", "head"),
            P("head", "dp"),
            P(),
            P(),
            P(),
            P("dp", "head"),
            P("head"),
            P("head", "dp"),
            P(),
            P(),
        ),
        check_vma=False,
    )
```

```python
import functools

import jax
import jax.numpy as jnp
from jax import lax
from jax.experimental import pallas as pl
from jax.experimental.pallas import tpu as pltpu
from jax.sharding import PartitionSpec as P

HEAD_DIM = 64
norm_eps = 1e-06
root_half = 0.7071067811865476
inv_root_two_pi = 0.3989422804014327
f32, bf16 = jnp.float32, jnp.bfloat16


MIB = 1024 * 1024
SIDES = 2
FLOPS = 1
UNIT_BLOCK = 512


def rows_of(count):
    return -(-count // 16) * 16


def norm_stats(values):
    row_mean = jnp.mean(values, axis=-1, keepdims=True)
    centered = values - row_mean
    inv_std = lax.rsqrt(jnp.mean(centered * centered, axis=-1, keepdims=True) + norm_eps)
    return centered * inv_std, inv_std


def norm_back(grad_normed, gain, normed, inv_std):
    unit = grad_normed * gain
    return inv_std * (
        unit
        - jnp.mean(unit, axis=-1, keepdims=True)
        - normed * jnp.mean(unit * normed, axis=-1, keepdims=True)
    )


def dot(a, b, over=((1,), (0,))):
    return lax.dot_general(a, b, (over, ((), ())), preferred_element_type=f32)


def dot_turned(a, b):
    return dot(a, b, ((1,), (1,)))


def column_sum(values):
    return jnp.sum(values, axis=0, keepdims=True)


class Held:
    def __init__(self, ref, copy):
        self.ref, self.copy, self.shape = ref, copy, ref.shape

    def ready(self):
        if self.copy is not None:
            self.copy.wait()
            self.copy = None
        return self.ref

    def __getitem__(self, at):
        return self.ready()[at]


class Made:
    def __init__(self, ref, copy):
        self.ref, self.copy, self.shape, self.left = ref, copy, ref.shape, False

    def __getitem__(self, at):
        return self.ref[at]

    def __setitem__(self, at, value):
        self.ref[at] = value

    def leave(self):
        if not self.left:
            self.copy.start()
            self.left = True


class Far:
    def __init__(self, value):
        self.value = value


def call(kernel, out_shape, inputs, scratch=(), fetch=(), room=14):
    inputs = [*inputs, *[Far(x) for x in fetch]]
    values = [x.value if isinstance(x, Far) else x for x in inputs]
    shapes = [x.value if isinstance(x, Far) else x for x in out_shape]
    shapes += [shape(x.shape, x.dtype) for x in fetch]
    n_fetch, n_in, n_out = len(fetch), len(inputs), len(shapes)
    far_in = [i for i in range(n_in - n_fetch) if isinstance(inputs[i], Far)]
    far_out = [i for i, x in enumerate(out_shape) if isinstance(x, Far)]
    near, away = pl.BlockSpec(memory_space=pltpu.VMEM), pl.BlockSpec(memory_space=pltpu.HBM)
    in_hbm = [isinstance(x, Far) for x in inputs]

    def body(*refs):
        ins, outs, refs = list(refs[:n_in]), list(refs[n_in : n_in + n_out]), refs[n_in + n_out :]
        in_refs, refs = refs[: len(far_in)], refs[len(far_in) :]
        out_refs, refs = refs[: len(far_out)], refs[len(far_out) :]
        sems, extra = (refs[0], refs[1:]) if n_sems else (None, refs)
        for n, i in enumerate(far_in):
            copy = pltpu.make_async_copy(ins[i], in_refs[n], sems.at[n])
            copy.start()
            ins[i] = Held(in_refs[n], copy)
        for n, i in enumerate(far_out):
            copy = pltpu.make_async_copy(out_refs[n], outs[i], sems.at[len(far_in) + n])
            outs[i] = Made(out_refs[n], copy)
        fetched = []
        for n in range(n_fetch):
            copy = pltpu.make_async_copy(
                ins[n_in - n_fetch + n],
                outs[n_out - n_fetch + n],
                sems.at[len(far_in) + len(far_out) + n],
            )
            copy.start()
            fetched.append(copy)
        kernel(*ins[: n_in - n_fetch], *outs[: n_out - n_fetch], *extra)
        for i in far_in:
            ins[i].ready()
        for i in far_out:
            outs[i].leave()
        for copy in fetched:
            copy.wait()
        for i in far_out:
            outs[i].copy.wait()

    def landing(x):
        return (pltpu.SMEM if x.dtype == jnp.int32 and x.ndim == 1 else pltpu.VMEM)(x.shape, x.dtype)

    far_scratch = [landing(values[i]) for i in far_in]
    far_scratch += [pltpu.VMEM(shapes[i].shape, shapes[i].dtype) for i in far_out]
    n_sems = len(far_in) + len(far_out) + n_fetch
    if n_sems:
        far_scratch.append(pltpu.SemaphoreType.DMA((n_sems,)))
    values = [
        pltpu.with_memory_space_constraint(x, pltpu.HBM if far else pltpu.VMEM)
        for x, far in zip(values, in_hbm)
    ]
    return pl.pallas_call(
        body,
        out_shape=[
            (pltpu.HBM if i in far_out else pltpu.VMEM)(o.shape, o.dtype)
            for i, o in enumerate(shapes)
        ],
        in_specs=[away if far else near for far in in_hbm],
        out_specs=[away if i in far_out else near for i in range(n_out)],
        scratch_shapes=[*far_scratch, *scratch],
        compiler_params=pltpu.CompilerParams(vmem_limit_bytes=room * MIB),
        cost_estimate=pl.CostEstimate(flops=FLOPS, bytes_accessed=1, transcendentals=0),
    )(*values)


def line(ref):
    return ref[...].reshape(1, -1)


def shape(dims, kind):
    return jax.ShapeDtypeStruct(dims, kind)


def turned_hot(index_ref, image, slots, padded):
    place = lax.broadcasted_iota(jnp.int32, (slots, padded), 0)
    return jnp.where(place == index_ref[image : image + 1, :padded], 1.0, 0.0).astype(bf16)


def front_kernel(
    index_in_ref,
    tokens_ref,
    count_in_ref,
    router_w_ref,
    gain_ref,
    shift_ref,
    cotangent_ref,
    index_ref,
    count_ref,
    picked_ref,
    grad_picked_ref,
    first_ref,
    grad_mlp_ref,
    router_ref,
    scale_ref,
    fc2_bias_grad_ref,
):
    images, slots, _ = tokens_ref.shape
    padded = picked_ref.shape[0] // images
    index_ref[...] = jnp.full(index_ref.shape, -1, jnp.int32)
    index_ref[:images, : index_in_ref.shape[1]] = index_in_ref[...]
    for b in range(images):
        hot = turned_hot(index_ref, b, slots, padded)
        picked_ref[b * padded : (b + 1) * padded, :] = dot(hot, tokens_ref[b], ((0,), (0,))).astype(
            bf16
        )
    picked = picked_ref[...].astype(f32)
    router = jax.nn.sigmoid(jnp.sum(picked * line(router_w_ref), axis=-1, keepdims=True))
    router_ref[...] = router
    normed, _ = norm_stats(picked)
    first_ref[...] = (normed * line(gain_ref) + line(shift_ref)).astype(bf16)
    rows = lax.broadcasted_iota(jnp.int32, (padded, 1), 0)
    for b in range(images):
        count_ref[b : b + 1, :] = jnp.full((1, count_ref.shape[1]), count_in_ref[b], jnp.int32)
        at = slice(b * padded, (b + 1) * padded)
        live = jnp.where(rows < count_in_ref[b], 1.0, 0.0).astype(f32)
        scale_ref[at, :] = live * router_ref[at, :]
        hot = turned_hot(index_ref, b, slots, padded)
        grad_picked_ref[at, :] = dot(hot, cotangent_ref[b], ((0,), (0,))).astype(bf16)
    grad_branch = scale_ref[...] * grad_picked_ref[...].astype(f32)
    grad_mlp_ref[...] = grad_branch.astype(bf16)
    fc2_bias_grad_ref[...] = column_sum(grad_branch)


def stacked_heads(pair):
    lane = lax.broadcasted_iota(jnp.int32, pair.shape, 1)
    zero = jnp.zeros_like(pair)
    return jnp.concatenate(
        [jnp.where(lane < HEAD_DIM, pair, zero), jnp.where(lane < HEAD_DIM, zero, pair)], axis=0
    )


def joined_heads(stacked):
    half = stacked.shape[0] // 2
    lane = lax.broadcasted_iota(jnp.int32, (half, stacked.shape[1]), 1)
    return jnp.where(lane < HEAD_DIM, stacked[:half], stacked[half:])


def pairs_of_heads(images, padded, local):
    return [
        (b, slice(b * padded, (b + 1) * padded), at)
        for b in range(images)
        for at in range(0, local, 2 * HEAD_DIM)
    ]


def saved_qkv(made_ref, rows, at):
    local = made_ref.shape[1] // 3
    return [made_ref[rows, t * local + at : t * local + at + 2 * HEAD_DIM] for t in range(3)]


def probabilities(scores, count, axis):
    key = lax.broadcasted_iota(jnp.int32, scores.shape, axis)
    scores = jnp.where(key < count, scores, -1e30)
    raised = jnp.exp(scores - jnp.max(scores, axis=axis, keepdims=True))
    return raised * (1.0 / jnp.sum(raised, axis=axis, keepdims=True))


def project(first_ref, w_ref, made_ref):
    local = w_ref.shape[2]
    for t in range(3):
        made_ref[:, t * local : (t + 1) * local] = dot(first_ref[...], w_ref[t]).astype(bf16)


def attend(images, count_ref, made_ref, mixed_ref):
    padded, local = made_ref.shape[0] // images, mixed_ref.shape[1]
    units = pairs_of_heads(images, padded, local)
    qkv = [saved_qkv(made_ref, rows, at) for _, rows, at in units]
    scores = [dot_turned(stacked_heads(q), k) * HEAD_DIM ** (-0.5) for q, k, _ in qkv]
    probs = [
        probabilities(x, count_ref[b : b + 1, 0:1], 1).astype(bf16)
        for x, (b, _, _) in zip(scores, units)
    ]
    mixed = [joined_heads(dot(x, v)) for x, (_, _, v) in zip(probs, qkv)]
    for x, (_, rows, at) in zip(mixed, units):
        mixed_ref[rows, at : at + 2 * HEAD_DIM] = x.astype(bf16)


def attention_kernel(
    images,
    count_ref,
    first_ref,
    w_own_ref,
    w_other_ref,
    proj_own_ref,
    proj_other_ref,
    picked_ref,
    proj_bias_ref,
    gain_ref,
    shift_ref,
    made_own_ref,
    made_other_ref,
    mixed_own_ref,
    mixed_other_ref,
    attention_ref,
    second_ref,
    pack_ref,
):
    width = first_ref.shape[1]
    pack_ref[:, :width] = first_ref[...]
    project(first_ref, w_own_ref, made_own_ref)
    project(first_ref, w_other_ref, made_other_ref)
    attend(images, count_ref, made_own_ref, mixed_own_ref)
    attend(images, count_ref, made_other_ref, mixed_other_ref)
    total = line(proj_bias_ref) + dot(mixed_own_ref[...], proj_own_ref[...])
    total = total + dot(mixed_other_ref[...], proj_other_ref[...])
    attention_ref[...] = total
    normed, _ = norm_stats(picked_ref[...].astype(f32) + total)
    second = (normed * line(gain_ref) + line(shift_ref)).astype(bf16)
    second_ref[...] = second
    pack_ref[:, width : 2 * width] = second
    pack_ref[:, 2 * width :] = mixed_other_ref[...]


def hidden_kernel(second_ref, w_fc1_ref, bias_ref, act_ref, slope_ref):
    for at in range(0, act_ref.shape[1], UNIT_BLOCK):
        block = slice(at, at + UNIT_BLOCK)
        pre = dot(second_ref[...], w_fc1_ref[:, block]) + bias_ref[block].reshape(1, -1)
        half = 0.5 * (1.0 + lax.erf(pre * root_half))
        act_ref[:, block] = (pre * half).astype(bf16)
        slope_ref[:, block] = half + pre * inv_root_two_pi * jnp.exp(-0.5 * pre * pre)


def hidden_back_kernel(grad_mlp_ref, w_fc2_ref, slope_ref, grad_pre_ref, unit_sum_ref):
    for at in range(0, slope_ref.shape[1], UNIT_BLOCK):
        block = slice(at, at + UNIT_BLOCK)
        grad_pre = dot_turned(grad_mlp_ref[...], w_fc2_ref[block, :]) * slope_ref[:, block]
        unit_sum_ref[block] = column_sum(grad_pre).reshape(UNIT_BLOCK)
        grad_pre_ref[:, block] = grad_pre.astype(bf16)


TOP_BITS = 4
FC2_EARLY, FC1_EARLY, ATTN_EARLY = 0, 0, 0
UNITS = 1 << TOP_BITS


def my_bits():
    place = lax.axis_index("dp") >> (lax.axis_size("dp").bit_length() - 1 - TOP_BITS)
    return [(place >> bit) & 1 for bit in range(TOP_BITS)]


def order_of(part, early=0):
    order = [(part - j) % 3 for j in range(3)] + [3]
    return order[:2] + [3, order[2]] if part < early else order


def bits_left(order, step):
    return [bit for bit in range(TOP_BITS - 1, -1, -1) if bit not in order[:step]]


def every_choice(bits):
    for j in range(1 << len(bits)):
        yield j, {bit: (j >> (len(bits) - 1 - i)) & 1 for i, bit in enumerate(bits)}


def unit_rows(ref, spread, chosen, unit, base=0):
    place = 0
    for bit in spread:
        place = place * 2 + chosen[bit]
    return ref[pl.ds(pl.multiple_of(base + place * unit, 16), unit), :]


def arrange_rows(turned_ref, mine, part, arranged_ref):
    unit = turned_ref.shape[0] // UNITS
    order = order_of(part)
    bit = order[0]
    for side, value in enumerate((1 - mine[bit], mine[bit])):
        for j, chosen in every_choice(bits_left(order, 1)):
            chosen[bit] = value
            to = (side * UNITS // 2 + j) * unit
            arranged_ref[to : to + unit, :] = unit_rows(
                turned_ref, bits_left(order, 0), chosen, unit
            )


class Stream:
    def __init__(self, part, away, kept, early):
        self.part, self.step, self.away, self.terms = part, 0, away, [(kept, 0, 1)]
        self.order = order_of(part, early)
        self.unit = kept.shape[0] * 2 // UNITS

    def bit(self):
        return self.order[self.step]

    def rows(self):
        return self.unit * UNITS >> (self.step + 1)

    def sent(self, got, base):
        self.step += 1
        self.away = None
        self.terms.append((got, base, self.step))


def listed(streams):
    arrays, plans = [], []
    for stream in streams:
        terms = [(stream.away, 0, 0)] if stream.away is not None else stream.terms
        plan = []
        for array, base, step in terms:
            found = [n for n, x in enumerate(arrays) if x is array]
            if not found:
                found = [len(arrays)]
                arrays.append(array)
            plan.append((found[0], base, step))
        plans.append(plan)
    return arrays, plans


def plan_sum(refs, plan, order, chosen, unit):
    total = 0.0
    for n, base, step in plan:
        total = total + unit_rows(refs[n], bits_left(order, step), chosen, unit, base).astype(f32)
    return total


def step_kernel(n_arrays, n_small, plans, *refs):
    mine = my_bits()
    small, outs = refs[n_arrays : n_arrays + n_small], refs[n_arrays + n_small :]
    if n_small:
        outs[-1][...] = sum(ref[...] for ref in small)
    for order, step, made, unit, plan, out, base in plans:
        if made:
            ref = refs[plan[0][0]]
            outs[out][base : base + ref.shape[0], :] = ref[...]
            continue
        for j, chosen in every_choice(bits_left(order, step + 1)):
            for bit in order[:step]:
                chosen[bit] = mine[bit]
            chosen[order[step]] = 1 - mine[order[step]]
            to = base + j * unit
            outs[out][to : to + unit, :] = plan_sum(refs, plan, order, chosen, unit).astype(bf16)


def mlp_finish_kernel(n_arrays, plans, *refs):
    mine = my_bits()
    chosen = {bit: mine[bit] for bit in range(TOP_BITS)}
    outs = refs[n_arrays:]
    for i, (part, order, unit, plan) in enumerate(plans):
        total = plan_sum(refs, plan, order, chosen, unit)
        outs[i // 3][:, part * UNIT_BLOCK : (part + 1) * UNIT_BLOCK] = total


def attn_finish_kernel(n_arrays, n_small, plans, *refs):
    mine = my_bits()
    chosen = {bit: mine[bit] for bit in range(TOP_BITS)}
    small, (qkv_ref, proj_ref, *outs) = (
        refs[n_arrays : n_arrays + n_small],
        refs[n_arrays + n_small :],
    )
    local = qkv_ref.shape[2]
    third = local // 3
    for part, order, unit, plan in plans:
        total = plan_sum(refs, plan, order, chosen, unit)
        qkv_ref[part] = total[:, :local]
        proj_ref[:, part * third : (part + 1) * third] = total[:, local:]
    total = sum(ref[...] for ref in small)
    width = total.shape[1]
    for i, out_ref in enumerate(outs[:-1]):
        out_ref[...] = total[i : i + 1, :].reshape(width)
    for i in range(total.shape[0] - 7):
        outs[-1][i * width : (i + 1) * width] = total[7 + i : 8 + i, :].reshape(width)


def both_rows(own, other):
    return jnp.concatenate([own, other], axis=0)


def weight_tile(arranged_ref, right, away_ref, kept_ref, columns):
    half = away_ref.shape[0]
    away_ref[:, columns] = dot(arranged_ref[:half, :], right).astype(bf16)
    kept_ref[:, columns] = dot(arranged_ref[half:, :], right)


def mlp_weights_kernel(at_left, left_own_ref, left_par_ref, right_own_ref, right_par_ref, *outs):
    away_refs, kept_refs, (turned_ref, arranged_ref) = outs[:3], outs[3:6], outs[6:]
    mine = my_bits()
    left_par = left_par_ref[:, at_left : at_left + left_own_ref.shape[1]]
    turned_ref[...] = both_rows(left_own_ref[...], left_par).T
    columns = slice(0, UNIT_BLOCK)
    for part in range(3):
        at = slice(part * UNIT_BLOCK, (part + 1) * UNIT_BLOCK)
        right = both_rows(right_own_ref[:, at], right_par_ref[:, at])
        arrange_rows(turned_ref, mine, part, arranged_ref)
        weight_tile(arranged_ref, right, away_refs[part], kept_refs[part], columns)


def attn_weights_kernel(
    first_own_ref,
    pack_par_ref,
    grad_attn_own_ref,
    grad_attn_par_ref,
    qkv_own_ref,
    qkv_par_ref,
    mixed_own_ref,
    *outs,
):
    away_refs, kept_refs, (turned_ref, arranged_ref) = outs[:3], outs[3:6], outs[6:]
    mine = my_bits()
    width, local = first_own_ref.shape[1], mixed_own_ref.shape[1]
    third = local // 3
    turned_ref[...] = both_rows(first_own_ref[...], pack_par_ref[:, :width]).T
    for part in range(3):
        at = slice(part * local, (part + 1) * local)
        right = both_rows(qkv_own_ref[:, at], qkv_par_ref[:, at])
        arrange_rows(turned_ref, mine, part, arranged_ref)
        weight_tile(arranged_ref, right, away_refs[part], kept_refs[part], slice(0, local))
    turned_ref[...] = both_rows(grad_attn_own_ref[...], grad_attn_par_ref[...]).T
    for part in range(3):
        at = slice(part * third, (part + 1) * third)
        right = both_rows(mixed_own_ref[:, at], pack_par_ref[:, 2 * width + at.start : 2 * width + at.stop])
        arrange_rows(turned_ref, mine, part, arranged_ref)
        weight_tile(
            arranged_ref, right, away_refs[part], kept_refs[part], slice(local, local + third)
        )


def weights(kernel, arrays, width, depth, columns):
    half = width // 2
    return call(
        kernel,
        [shape((half, columns), bf16)] * 3 + [shape((half, columns), f32)] * 3,
        arrays,
        scratch=[pltpu.VMEM((width, depth), bf16), pltpu.VMEM((width, depth), bf16)],
    )


def heads_back(images, count_ref, grad_attn_ref, proj_ref, made_ref, out_ref, mixed_scratch):
    padded, local = made_ref.shape[0] // images, proj_ref.shape[0]
    factor = HEAD_DIM ** (-0.5)
    mixed_scratch[...] = dot_turned(grad_attn_ref[...], proj_ref[...]).astype(bf16)
    units = pairs_of_heads(images, padded, local)
    for first in range(0, len(units), 3):
        some = units[first : first + 3]
        q, k, v = zip(*[saved_qkv(made_ref, rows, at) for _, rows, at in some])
        q = [stacked_heads(x) for x in q]
        grad_mixed = [
            stacked_heads(mixed_scratch[rows, at : at + 2 * HEAD_DIM]) for _, rows, at in some
        ]
        scores = [dot_turned(x, y) * factor for x, y in zip(k, q)]
        grad_probs = [dot_turned(x, y) for x, y in zip(v, grad_mixed)]
        probs = [
            probabilities(x, count_ref[b : b + 1, 0:1], 0) for x, (b, _, _) in zip(scores, some)
        ]
        grad_scores = [
            (p * (g - jnp.sum(p * g, axis=0, keepdims=True))).astype(bf16)
            for p, g in zip(probs, grad_probs)
        ]
        grad_k = [dot(x, y) * factor for x, y in zip(grad_scores, q)]
        grad_v = [dot(x.astype(bf16), y) for x, y in zip(probs, grad_mixed)]
        grad_q = [joined_heads(dot(x, y, ((0,), (0,)))) * factor for x, y in zip(grad_scores, k)]
        for (_, rows, at), *found in zip(some, grad_q, grad_k, grad_v):
            for t in range(3):
                to = slice(t * local + at, t * local + at + 2 * HEAD_DIM)
                out_ref[rows, to] = found[t].astype(bf16)


def back_kernel(
    grad_pre_other_ref,
    w_fc1_other_ref,
    grad_pre_ref,
    w_fc1_ref,
    picked_ref,
    attention_ref,
    grad_picked_ref,
    scale_ref,
    gain_ref,
    grad_attn_ref,
    grad_hidden_ref,
    sums_ref,
):
    grad_second = dot_turned(grad_pre_other_ref[...], w_fc1_other_ref[...])
    grad_second = grad_second + dot_turned(grad_pre_ref[...], w_fc1_ref[...])
    normed, inv_std = norm_stats(picked_ref[...].astype(f32) + attention_ref[...])
    grad_hidden = norm_back(grad_second, line(gain_ref), normed, inv_std)
    grad_hidden_ref[...] = grad_hidden
    grad_attention = scale_ref[...] * grad_picked_ref[...].astype(f32) + grad_hidden
    grad_attn_ref[...] = grad_attention.astype(bf16)
    sums_ref[0:1, :] = column_sum(grad_attention)
    sums_ref[1:2, :] = column_sum(grad_second * normed)
    sums_ref[2:3, :] = column_sum(grad_second)


def branch_kernel(
    picked_ref,
    grad_picked_ref,
    router_ref,
    scale_ref,
    attention_ref,
    act_own_ref,
    act_other_ref,
    w_fc2_ref,
    w_fc2_other_ref,
    fc2_bias_ref,
    update_ref,
    grad_logit_ref,
    router_grad_ref,
):
    scale = scale_ref[...]
    mlp_out = dot(act_own_ref[...], w_fc2_ref[...]) + dot(act_other_ref[...], w_fc2_other_ref[...])
    branch = attention_ref[...] + (mlp_out + line(fc2_bias_ref))
    update_ref[...] = scale * branch
    grad_logit = (
        scale
        * (1.0 - router_ref[...])
        * jnp.sum(grad_picked_ref[...].astype(f32) * branch, axis=-1, keepdims=True)
    )
    grad_logit_ref[...] = grad_logit
    router_grad_ref[...] = column_sum(grad_logit * picked_ref[...].astype(f32))


def first_back_kernel(
    qkv_own_ref,
    gain_ref,
    router_w_ref,
    picked_ref,
    grad_hidden_ref,
    grad_logit_ref,
    grad_qkv_own_ref,
    grad_qkv_other_ref,
    qkv_other_ref,
    fc2_bias_grad_ref,
    router_grad_ref,
    back_sums_ref,
    unit_own_ref,
    unit_other_ref,
    grad_kept_ref,
    keep_ref,
    send_ref,
):
    width = picked_ref.shape[1]
    local = qkv_other_ref.shape[2]
    grad_first = jnp.zeros(picked_ref.shape, f32)
    for side in range(SIDES):
        for t in range(3):
            grad_first = grad_first + dot_turned(
                (grad_qkv_own_ref, grad_qkv_other_ref)[side][:, t * local : (t + 1) * local],
                (qkv_own_ref, qkv_other_ref)[side][t],
            )
    normed, inv_std = norm_stats(picked_ref[...].astype(f32))
    grad_kept_ref[...] = (
        norm_back(grad_first, line(gain_ref), normed, inv_std)
        + grad_hidden_ref[...]
        + grad_logit_ref[...] * line(router_w_ref)
    )
    sums = (
        column_sum(grad_first * normed),
        column_sum(grad_first),
        back_sums_ref[0:1, :],
        back_sums_ref[1:2, :],
        back_sums_ref[2:3, :],
        fc2_bias_grad_ref[...],
        router_grad_ref[...],
    )
    for i, values in enumerate(sums):
        keep_ref[i : i + 1, :] = values
        send_ref[i : i + 1, :] = values
    for i in range(unit_own_ref.shape[0] // width):
        at = slice(i * width, (i + 1) * width)
        keep_ref[7 + i : 8 + i, :] = unit_own_ref[at].reshape(1, width)
        send_ref[7 + i : 8 + i, :] = unit_other_ref[at].reshape(1, width)


def put_back_kernel(n_small, index_ref, base_ref, change_ref, *refs):
    small_refs, outs = refs[:n_small], refs[n_small:]
    if n_small:
        outs[1][...] = sum(ref[...] for ref in small_refs)
    images, slots, _ = base_ref.shape
    padded = change_ref.shape[0] // images
    for b in range(images):
        hot = turned_hot(index_ref, b, slots, padded)
        change = change_ref[b * padded : (b + 1) * padded, :]
        high = change.astype(bf16)
        low = (change - high.astype(f32)).astype(bf16)
        updated = base_ref[b].astype(f32) + (dot(hot, high) + dot(hot, low))
        outs[0][b] = updated.astype(bf16)


def other_core(value):
    return lax.ppermute(value, "head", [(0, 1), (1, 0)])


def partners(count, bit):
    return [(i, i ^ (1 << bit)) for i in range(count)]


def swap(value, bit, count):
    return lax.ppermute(value, "dp", partners(count, bit + count.bit_length() - 1 - TOP_BITS))


def waiting(halves, early=0):
    return [Stream(part, halves[part], halves[3 + part], early) for part in range(3)]


def begin(halves, count, early=0):
    streams = waiting(halves, early)
    for stream in streams:
        stream.sent(swap(stream.away, stream.bit(), count), 0)
    return streams


def exchange(streams, count, after, small=()):
    arrays, plans = listed(streams)
    tied, after = lax.optimization_barrier((tuple(arrays), after))
    bits = []
    for stream in streams:
        if stream.bit() not in bits:
            bits.append(stream.bit())
    sizes, full, bases = [0] * len(bits), [], []
    for stream, plan in zip(streams, plans):
        out = bits.index(stream.bit())
        made = stream.away is not None
        full.append((stream.order, stream.step, made, stream.unit, plan, out, sizes[out]))
        bases.append(sizes[out])
        sizes[out] += stream.rows()
    columns = arrays[0].shape[1]
    outs = [shape((size, columns), bf16) for size in sizes]
    outs += [shape(array.shape, array.dtype) for array in small[:1]]
    made = call(
        functools.partial(step_kernel, len(arrays), len(small), full), outs, (*tied, *small)
    )
    made, after = lax.optimization_barrier((made, after))
    got = [swap(made[n], bit, count) for n, bit in enumerate(bits)]
    for stream, base in zip(streams, bases):
        stream.sent(got[bits.index(stream.bit())], base)
    return (after, made[-1]) if small else after


def arrived(streams, after):
    arrays = []
    for stream in streams:
        if all(stream.terms[-1][0] is not x for x in arrays):
            arrays.append(stream.terms[-1][0])
    tied, after = lax.optimization_barrier((arrays, after))
    for stream in streams:
        array, base, step = stream.terms[-1]
        place = [x is array for x in arrays].index(True)
        stream.terms[-1] = (tied[place], base, step)
    return after


def fewer_rows(grad, count, axis):
    place = lax.axis_index("dp")
    for bit in range(count.bit_length() - 2 - TOP_BITS, -1, -1):
        half = grad.shape[axis] // 2
        mine = (place >> bit) & 1
        away = lax.dynamic_slice_in_dim(grad, (1 - mine) * half, half, axis).astype(bf16)
        kept = lax.dynamic_slice_in_dim(grad, mine * half, half, axis)
        grad = kept + lax.ppermute(away, "dp", partners(count, bit)).astype(f32)
    return grad


def on_device(
    tokens,
    kept_index,
    kept_count,
    ln1_gain,
    ln1_bias,
    w_qkv,
    w_proj,
    proj_bias,
    ln2_gain,
    ln2_bias,
    w_fc1,
    fc1_bias,
    w_fc2,
    fc2_bias,
    w_router,
    cotangent,
):
    images, slots, width = tokens.shape
    padded = rows_of(kept_index.shape[1])
    rows = images * padded
    local = w_qkv.shape[2]
    units = w_fc1.shape[1]
    count = lax.axis_size("dp")

    top = count.bit_length() - 1 - TOP_BITS
    w_qkv_other = other_core(w_qkv)
    w_proj_other = other_core(w_proj)
    bias_other = other_core(fc1_bias)
    tie = lax.optimization_barrier
    table = shape((8, 128), jnp.int32)
    (
        index,
        counts,
        picked,
        grad_picked,
        first,
        grad_mlp,
        router,
        scale,
        fc2_bias_sum,
        w_qkv,
        w_proj,
        proj_bias,
        ln2_gain,
        ln2_bias,
        bias_own,
        fc2_bias,
        ln1_gain,
        w_router,
    ) = call(
        front_kernel,
        [table, table]
        + [shape((rows, width), bf16)] * 4
        + [shape((rows, 1), f32)] * 2
        + [shape((1, width), f32)],
        (
            Far(kept_index),
            Far(tokens),
            Far(kept_count),
            Far(w_router),
            Far(ln1_gain),
            Far(ln1_bias),
            Far(cotangent),
        ),
        fetch=(
            w_qkv,
            w_proj,
            proj_bias,
            ln2_gain,
            ln2_bias,
            fc1_bias,
            fc2_bias,
            ln1_gain,
            w_router,
        ),
    )
    grad_mlp_par = other_core(grad_mlp)
    w_fc1_late, bias_other, first, w_qkv_other, w_proj_other = tie(
        (w_fc1, bias_other, first, w_qkv_other, w_proj_other)
    )
    w_fc1_other = other_core(w_fc1_late)

    made, made_other, mixed, mixed_other, attention, second, pack = call(
        functools.partial(attention_kernel, images),
        [
            shape((rows, 3 * local), bf16),
            shape((rows, 3 * local), bf16),
            shape((rows, local), bf16),
            shape((rows, local), bf16),
            shape((rows, width), f32),
            shape((rows, width), bf16),
            shape((rows, 2 * width + local), bf16),
        ],
        (
            counts,
            first,
            w_qkv,
            w_qkv_other,
            w_proj,
            w_proj_other,
            picked,
            proj_bias,
            ln2_gain,
            ln2_bias,
        ),
    )
    second, grad_mlp_par, w_fc2_late = tie((second, grad_mlp_par, w_fc2))
    w_fc2_other = other_core(w_fc2_late)

    def hidden(w, bias):
        return call(
            hidden_kernel,
            [shape((rows, units), bf16), shape((rows, units), f32)],
            (second, w, bias),
        )

    def hidden_back(w, slope):
        return call(
            hidden_back_kernel,
            [shape((rows, units), bf16), shape((units,), f32)],
            (grad_mlp, w, slope),
        )

    def mlp_weights(left, left_par, at_left, right, right_par):
        return weights(
            functools.partial(mlp_weights_kernel, at_left),
            (left, left_par, right, right_par),
            width,
            2 * rows,
            UNIT_BLOCK,
        )

    act_other, slope_other = hidden(w_fc1_other, bias_other)
    act_par = other_core(act_other)
    bias_own, act_other = tie((bias_own, act_other))
    act, slope = hidden(w_fc1, bias_own)
    grad_pre, unit_own = hidden_back(w_fc2, slope)
    slope_other, grad_pre = tie((slope_other, grad_pre))
    grad_pre_other, unit_other = hidden_back(w_fc2_other, slope_other)
    act, grad_pre, grad_pre_other, pack = tie((act, grad_pre, grad_pre_other, pack))
    halves = mlp_weights(grad_mlp, grad_mlp_par, 0, act, act_par)
    grad_pre_par = other_core(grad_pre_other)
    pack_par = other_core(pack)
    halves, grad_pre_other = tie((halves, grad_pre_other))
    fc2_sums = begin(halves, count, FC2_EARLY)
    grad_attn, grad_hidden, back_sums = call(
        back_kernel,
        [shape((rows, width), bf16), shape((rows, width), f32), shape((8, width), f32)],
        (
            grad_pre_other,
            w_fc1_other,
            grad_pre,
            w_fc1,
            picked,
            attention,
            grad_picked,
            scale,
            ln2_gain,
        ),
    )
    grad_pre, grad_attn = tie((grad_pre, grad_attn))
    halves = mlp_weights(second, pack_par, width, grad_pre, grad_pre_par)

    def attention_back(w, saved, grad):
        return call(
            functools.partial(heads_back, images),
            [shape((rows, 3 * local), bf16)],
            (counts, grad, w, saved),
            scratch=[pltpu.VMEM((rows, local), bf16)],
        )[0]

    halves, grad_attn = tie((halves, grad_attn))
    grad_qkv_other = attention_back(w_proj_other, made_other, grad_attn)
    fc1_sums = waiting(halves, FC1_EARLY)
    grad_attn, grad_qkv_other = exchange(
        (*fc2_sums, *fc1_sums), count, (grad_attn, grad_qkv_other)
    )
    grad_attn_par = other_core(grad_attn)
    grad_qkv_par = other_core(grad_qkv_other)
    grad_qkv = attention_back(w_proj, made, grad_attn)
    halves = weights(
        attn_weights_kernel,
        (first, pack_par, grad_attn, grad_attn_par, grad_qkv, grad_qkv_par, mixed),
        width,
        2 * rows,
        local + local // 3,
    )
    attn_sums = waiting(halves, ATTN_EARLY)
    act = exchange((*fc2_sums, *fc1_sums, *attn_sums), count, act)
    update, grad_logit, router_sum = call(
        branch_kernel,
        [shape((rows, width), f32), shape((rows, 1), f32), shape((1, width), f32)],
        (
            picked,
            grad_picked,
            router,
            scale,
            attention,
            act,
            act_other,
            w_fc2,
            w_fc2_other,
            fc2_bias,
        ),
    )

    sum_rows = 7 + units // width
    grad_kept, keep, send = call(
        first_back_kernel,
        [
            shape((rows, width), f32),
            shape((sum_rows, width), f32),
            shape((sum_rows, width), f32),
        ],
        (
            w_qkv,
            ln1_gain,
            w_router,
            picked,
            grad_hidden,
            grad_logit,
            grad_qkv,
            grad_qkv_other,
            w_qkv_other,
            fc2_bias_sum,
            router_sum,
            back_sums,
            unit_own,
            unit_other,
        ),
    )

    def put_back(base, change, *small):
        return call(
            functools.partial(put_back_kernel, len(small)),
            [Far(shape(base.shape, bf16)), *[shape(x.shape, x.dtype) for x in small[:1]]],
            (index, base, change, *small),
        )

    got = other_core(send)
    update, keep = tie((update, keep))
    output, small = put_back(tokens, update, keep, got)
    got = swap(small, 0, count)
    grad_kept, output = tie((grad_kept, output))
    (input_grad,) = put_back(cotangent, grad_kept)
    input_grad, small = exchange(
        (*fc2_sums, *fc1_sums, *attn_sums), count, input_grad, (small, got)
    )
    got = swap(small, 1, count)
    input_grad, small = exchange((*fc1_sums, *attn_sums), count, input_grad, (small, got))
    small = arrived(fc2_sums, small)
    got = swap(small, 2, count)
    input_grad, small = exchange(attn_sums, count, input_grad, (small, got))
    for low in range(top):
        small = small + lax.ppermute(small, "dp", partners(count, low))
    got = swap(small, 3, count)
    unit = width // UNITS

    def final(streams):
        arrays, plans = listed(streams)
        return arrays, [
            (stream.part, stream.order, stream.unit, plan) for stream, plan in zip(streams, plans)
        ]

    arrays, plans = final((*fc2_sums, *fc1_sums))
    fc2_turned, fc1_grad = call(
        functools.partial(mlp_finish_kernel, len(arrays), plans),
        [Far(shape((unit, units), f32)), Far(shape((unit, units), f32))],
        tuple(arrays),
    )
    small, fc2_turned, fc1_grad = tie((small, fc2_turned, fc1_grad))
    arrays, plans = final(attn_sums)
    qkv_grad, proj_turned, *sums = call(
        functools.partial(attn_finish_kernel, len(arrays), 2, plans),
        [
            Far(shape((3, unit, local), f32)),
            Far(shape((unit, local), f32)),
            *[Far(shape((width,), f32))] * 7,
            Far(shape((units,), f32)),
        ],
        (*arrays, small, got),
    )
    fc2_turned, fc1_grad, proj_turned = (
        fewer_rows(grad, count, 0) for grad in (fc2_turned, fc1_grad, proj_turned)
    )
    qkv_grad = fewer_rows(qkv_grad, count, 1)
    return (
        output,
        input_grad,
        sums[0],
        sums[1],
        qkv_grad,
        proj_turned.T,
        sums[2],
        sums[3],
        sums[4],
        fc1_grad,
        sums[7],
        fc2_turned.T,
        sums[5],
        sums[6],
    )


def solution(mesh):
    batch = ("dp", "head")
    return jax.shard_map(
        on_device,
        mesh=mesh,
        in_specs=(
            P(batch, None, None),
            P(batch, None),
            P(batch),
            P(),
            P(),
            P(None, None, "head"),
            P("head", None),
            P(),
            P(),
            P(),
            P(None, "head"),
            P("head"),
            P("head", None),
            P(),
            P(),
            P(batch, None, None),
        ),
        out_specs=(
            P(batch, None, None),
            P(batch, None, None),
            P(),
            P(),
            P(None, "dp", "head"),
            P("head", "dp"),
            P(),
            P(),
            P(),
            P("dp", "head"),
            P("head"),
            P("head", "dp"),
            P(),
            P(),
        ),
        check_vma=False,
    )
```

```python
import functools

import jax
import jax.numpy as jnp
from jax import lax
from jax.experimental import pallas as pl
from jax.experimental.pallas import tpu as pltpu
from jax.sharding import PartitionSpec as P

HEAD_DIM = 64
norm_eps = 1e-06
root_half = 0.7071067811865476
inv_root_two_pi = 0.3989422804014327
f32, bf16 = jnp.float32, jnp.bfloat16


MIB = 1024 * 1024
SIDES = 2
FLOPS = 300_000_000
UNIT_BLOCK = 512


def rows_of(count):
    return -(-count // 16) * 16


def norm_stats(values):
    row_mean = jnp.mean(values, axis=-1, keepdims=True)
    centered = values - row_mean
    inv_std = lax.rsqrt(jnp.mean(centered * centered, axis=-1, keepdims=True) + norm_eps)
    return centered * inv_std, inv_std


def norm_back(grad_normed, gain, normed, inv_std):
    unit = grad_normed * gain
    return inv_std * (
        unit
        - jnp.mean(unit, axis=-1, keepdims=True)
        - normed * jnp.mean(unit * normed, axis=-1, keepdims=True)
    )


def dot(a, b, over=((1,), (0,))):
    return lax.dot_general(a, b, (over, ((), ())), preferred_element_type=f32)


def dot_turned(a, b):
    return dot(a, b, ((1,), (1,)))


def column_sum(values):
    return jnp.sum(values, axis=0, keepdims=True)


class Held:
    def __init__(self, ref, copy):
        self.ref, self.copy, self.shape = ref, copy, ref.shape

    def ready(self):
        if self.copy is not None:
            self.copy.wait()
            self.copy = None
        return self.ref

    def __getitem__(self, at):
        return self.ready()[at]


class Made:
    def __init__(self, ref, copy):
        self.ref, self.copy, self.shape, self.left = ref, copy, ref.shape, False

    def __getitem__(self, at):
        return self.ref[at]

    def __setitem__(self, at, value):
        self.ref[at] = value

    def leave(self):
        if not self.left:
            self.copy.start()
            self.left = True


class Far:
    def __init__(self, value):
        self.value = value


def call(kernel, out_shape, inputs, scratch=(), fetch=(), room=14):
    inputs = [*inputs, *[Far(x) for x in fetch]]
    values = [x.value if isinstance(x, Far) else x for x in inputs]
    shapes = [x.value if isinstance(x, Far) else x for x in out_shape]
    shapes += [shape(x.shape, x.dtype) for x in fetch]
    n_fetch, n_in, n_out = len(fetch), len(inputs), len(shapes)
    far_in = [i for i in range(n_in - n_fetch) if isinstance(inputs[i], Far)]
    far_out = [i for i, x in enumerate(out_shape) if isinstance(x, Far)]
    near, away = pl.BlockSpec(memory_space=pltpu.VMEM), pl.BlockSpec(memory_space=pltpu.HBM)
    in_hbm = [isinstance(x, Far) for x in inputs]

    def body(*refs):
        ins, outs, refs = list(refs[:n_in]), list(refs[n_in : n_in + n_out]), refs[n_in + n_out :]
        in_refs, refs = refs[: len(far_in)], refs[len(far_in) :]
        out_refs, refs = refs[: len(far_out)], refs[len(far_out) :]
        sems, extra = (refs[0], refs[1:]) if n_sems else (None, refs)
        for n, i in enumerate(far_in):
            copy = pltpu.make_async_copy(ins[i], in_refs[n], sems.at[n])
            copy.start()
            ins[i] = Held(in_refs[n], copy)
        for n, i in enumerate(far_out):
            copy = pltpu.make_async_copy(out_refs[n], outs[i], sems.at[len(far_in) + n])
            outs[i] = Made(out_refs[n], copy)
        fetched = []
        for n in range(n_fetch):
            copy = pltpu.make_async_copy(
                ins[n_in - n_fetch + n],
                outs[n_out - n_fetch + n],
                sems.at[len(far_in) + len(far_out) + n],
            )
            copy.start()
            fetched.append(copy)
        kernel(*ins[: n_in - n_fetch], *outs[: n_out - n_fetch], *extra)
        for i in far_in:
            ins[i].ready()
        for i in far_out:
            outs[i].leave()
        for copy in fetched:
            copy.wait()
        for i in far_out:
            outs[i].copy.wait()

    def landing(x):
        return (pltpu.SMEM if x.dtype == jnp.int32 and x.ndim == 1 else pltpu.VMEM)(x.shape, x.dtype)

    far_scratch = [landing(values[i]) for i in far_in]
    far_scratch += [pltpu.VMEM(shapes[i].shape, shapes[i].dtype) for i in far_out]
    n_sems = len(far_in) + len(far_out) + n_fetch
    if n_sems:
        far_scratch.append(pltpu.SemaphoreType.DMA((n_sems,)))
    values = [
        pltpu.with_memory_space_constraint(x, pltpu.HBM if far else pltpu.VMEM)
        for x, far in zip(values, in_hbm)
    ]
    return pl.pallas_call(
        body,
        out_shape=[
            (pltpu.HBM if i in far_out else pltpu.VMEM)(o.shape, o.dtype)
            for i, o in enumerate(shapes)
        ],
        in_specs=[away if far else near for far in in_hbm],
        out_specs=[away if i in far_out else near for i in range(n_out)],
        scratch_shapes=[*far_scratch, *scratch],
        compiler_params=pltpu.CompilerParams(vmem_limit_bytes=room * MIB),
        cost_estimate=pl.CostEstimate(flops=FLOPS, bytes_accessed=1, transcendentals=0),
    )(*values)


def line(ref):
    return ref[...].reshape(1, -1)


def shape(dims, kind):
    return jax.ShapeDtypeStruct(dims, kind)


def turned_hot(index_ref, image, slots, padded):
    place = lax.broadcasted_iota(jnp.int32, (slots, padded), 0)
    return jnp.where(place == index_ref[image : image + 1, :padded], 1.0, 0.0).astype(bf16)


def front_kernel(
    index_in_ref,
    tokens_ref,
    count_in_ref,
    router_w_ref,
    gain_ref,
    shift_ref,
    cotangent_ref,
    index_ref,
    count_ref,
    picked_ref,
    grad_picked_ref,
    first_ref,
    grad_mlp_ref,
    router_ref,
    scale_ref,
    fc2_bias_grad_ref,
):
    images, slots, _ = tokens_ref.shape
    padded = picked_ref.shape[0] // images
    index_ref[...] = jnp.full(index_ref.shape, -1, jnp.int32)
    index_ref[:images, : index_in_ref.shape[1]] = index_in_ref[...]
    for b in range(images):
        hot = turned_hot(index_ref, b, slots, padded)
        picked_ref[b * padded : (b + 1) * padded, :] = dot(hot, tokens_ref[b], ((0,), (0,))).astype(
            bf16
        )
    picked = picked_ref[...].astype(f32)
    router = jax.nn.sigmoid(jnp.sum(picked * line(router_w_ref), axis=-1, keepdims=True))
    router_ref[...] = router
    normed, _ = norm_stats(picked)
    first_ref[...] = (normed * line(gain_ref) + line(shift_ref)).astype(bf16)
    rows = lax.broadcasted_iota(jnp.int32, (padded, 1), 0)
    for b in range(images):
        count_ref[b : b + 1, :] = jnp.full((1, count_ref.shape[1]), count_in_ref[b], jnp.int32)
        at = slice(b * padded, (b + 1) * padded)
        live = jnp.where(rows < count_in_ref[b], 1.0, 0.0).astype(f32)
        scale_ref[at, :] = live * router_ref[at, :]
        hot = turned_hot(index_ref, b, slots, padded)
        grad_picked_ref[at, :] = dot(hot, cotangent_ref[b], ((0,), (0,))).astype(bf16)
    grad_branch = scale_ref[...] * grad_picked_ref[...].astype(f32)
    grad_mlp_ref[...] = grad_branch.astype(bf16)
    fc2_bias_grad_ref[...] = column_sum(grad_branch)


def stacked_heads(pair):
    lane = lax.broadcasted_iota(jnp.int32, pair.shape, 1)
    zero = jnp.zeros_like(pair)
    return jnp.concatenate(
        [jnp.where(lane < HEAD_DIM, pair, zero), jnp.where(lane < HEAD_DIM, zero, pair)], axis=0
    )


def joined_heads(stacked):
    half = stacked.shape[0] // 2
    lane = lax.broadcasted_iota(jnp.int32, (half, stacked.shape[1]), 1)
    return jnp.where(lane < HEAD_DIM, stacked[:half], stacked[half:])


def pairs_of_heads(images, padded, local):
    return [
        (b, slice(b * padded, (b + 1) * padded), at)
        for b in range(images)
        for at in range(0, local, 2 * HEAD_DIM)
    ]


def saved_qkv(made_ref, rows, at):
    local = made_ref.shape[1] // 3
    return [made_ref[rows, t * local + at : t * local + at + 2 * HEAD_DIM] for t in range(3)]


def probabilities(scores, count, axis):
    key = lax.broadcasted_iota(jnp.int32, scores.shape, axis)
    scores = jnp.where(key < count, scores, -1e30)
    raised = jnp.exp(scores - jnp.max(scores, axis=axis, keepdims=True))
    return raised * (1.0 / jnp.sum(raised, axis=axis, keepdims=True))


def project(first_ref, w_ref, made_ref):
    local = w_ref.shape[2]
    for t in range(3):
        made_ref[:, t * local : (t + 1) * local] = dot(first_ref[...], w_ref[t]).astype(bf16)


def attend(images, count_ref, made_ref, mixed_ref):
    padded, local = made_ref.shape[0] // images, mixed_ref.shape[1]
    units = pairs_of_heads(images, padded, local)
    qkv = [saved_qkv(made_ref, rows, at) for _, rows, at in units]
    scores = [dot_turned(stacked_heads(q), k) * HEAD_DIM ** (-0.5) for q, k, _ in qkv]
    probs = [
        probabilities(x, count_ref[b : b + 1, 0:1], 1).astype(bf16)
        for x, (b, _, _) in zip(scores, units)
    ]
    mixed = [joined_heads(dot(x, v)) for x, (_, _, v) in zip(probs, qkv)]
    for x, (_, rows, at) in zip(mixed, units):
        mixed_ref[rows, at : at + 2 * HEAD_DIM] = x.astype(bf16)


def attention_kernel(
    images,
    count_ref,
    first_ref,
    w_own_ref,
    w_other_ref,
    proj_own_ref,
    proj_other_ref,
    picked_ref,
    proj_bias_ref,
    gain_ref,
    shift_ref,
    made_own_ref,
    made_other_ref,
    mixed_own_ref,
    mixed_other_ref,
    attention_ref,
    second_ref,
    pack_ref,
):
    width = first_ref.shape[1]
    pack_ref[:, :width] = first_ref[...]
    project(first_ref, w_own_ref, made_own_ref)
    project(first_ref, w_other_ref, made_other_ref)
    attend(images, count_ref, made_own_ref, mixed_own_ref)
    attend(images, count_ref, made_other_ref, mixed_other_ref)
    total = line(proj_bias_ref) + dot(mixed_own_ref[...], proj_own_ref[...])
    total = total + dot(mixed_other_ref[...], proj_other_ref[...])
    attention_ref[...] = total
    normed, _ = norm_stats(picked_ref[...].astype(f32) + total)
    second = (normed * line(gain_ref) + line(shift_ref)).astype(bf16)
    second_ref[...] = second
    pack_ref[:, width : 2 * width] = second
    pack_ref[:, 2 * width :] = mixed_other_ref[...]


def hidden_kernel(second_ref, w_fc1_ref, bias_ref, act_ref, slope_ref):
    for at in range(0, act_ref.shape[1], UNIT_BLOCK):
        block = slice(at, at + UNIT_BLOCK)
        pre = dot(second_ref[...], w_fc1_ref[:, block]) + bias_ref[block].reshape(1, -1)
        half = 0.5 * (1.0 + lax.erf(pre * root_half))
        act_ref[:, block] = (pre * half).astype(bf16)
        slope_ref[:, block] = half + pre * inv_root_two_pi * jnp.exp(-0.5 * pre * pre)


def hidden_back_kernel(grad_mlp_ref, w_fc2_ref, slope_ref, grad_pre_ref, unit_sum_ref):
    for at in range(0, slope_ref.shape[1], UNIT_BLOCK):
        block = slice(at, at + UNIT_BLOCK)
        grad_pre = dot_turned(grad_mlp_ref[...], w_fc2_ref[block, :]) * slope_ref[:, block]
        unit_sum_ref[block] = column_sum(grad_pre).reshape(UNIT_BLOCK)
        grad_pre_ref[:, block] = grad_pre.astype(bf16)


TOP_BITS = 4
FC2_EARLY, FC1_EARLY, ATTN_EARLY = 0, 0, 0
UNITS = 1 << TOP_BITS


def my_bits():
    place = lax.axis_index("dp") >> (lax.axis_size("dp").bit_length() - 1 - TOP_BITS)
    return [(place >> bit) & 1 for bit in range(TOP_BITS)]


def order_of(part, early=0):
    order = [(part - j) % 3 for j in range(3)] + [3]
    return order[:2] + [3, order[2]] if part < early else order


def bits_left(order, step):
    return [bit for bit in range(TOP_BITS - 1, -1, -1) if bit not in order[:step]]


def every_choice(bits):
    for j in range(1 << len(bits)):
        yield j, {bit: (j >> (len(bits) - 1 - i)) & 1 for i, bit in enumerate(bits)}


def unit_rows(ref, spread, chosen, unit, base=0):
    place = 0
    for bit in spread:
        place = place * 2 + chosen[bit]
    return ref[pl.ds(pl.multiple_of(base + place * unit, 16), unit), :]


def arrange_rows(turned_ref, mine, part, arranged_ref):
    unit = turned_ref.shape[0] // UNITS
    order = order_of(part)
    bit = order[0]
    for side, value in enumerate((1 - mine[bit], mine[bit])):
        for j, chosen in every_choice(bits_left(order, 1)):
            chosen[bit] = value
            to = (side * UNITS // 2 + j) * unit
            arranged_ref[to : to + unit, :] = unit_rows(
                turned_ref, bits_left(order, 0), chosen, unit
            )


class Stream:
    def __init__(self, part, away, kept, early):
        self.part, self.step, self.away, self.terms = part, 0, away, [(kept, 0, 1)]
        self.order = order_of(part, early)
        self.unit = kept.shape[0] * 2 // UNITS

    def bit(self):
        return self.order[self.step]

    def rows(self):
        return self.unit * UNITS >> (self.step + 1)

    def sent(self, got, base):
        self.step += 1
        self.away = None
        self.terms.append((got, base, self.step))


def listed(streams):
    arrays, plans = [], []
    for stream in streams:
        terms = [(stream.away, 0, 0)] if stream.away is not None else stream.terms
        plan = []
        for array, base, step in terms:
            found = [n for n, x in enumerate(arrays) if x is array]
            if not found:
                found = [len(arrays)]
                arrays.append(array)
            plan.append((found[0], base, step))
        plans.append(plan)
    return arrays, plans


def plan_sum(refs, plan, order, chosen, unit):
    total = 0.0
    for n, base, step in plan:
        total = total + unit_rows(refs[n], bits_left(order, step), chosen, unit, base).astype(f32)
    return total


def step_kernel(n_arrays, n_small, plans, *refs):
    mine = my_bits()
    small, outs = refs[n_arrays : n_arrays + n_small], refs[n_arrays + n_small :]
    if n_small:
        outs[-1][...] = sum(ref[...] for ref in small)
    for order, step, made, unit, plan, out, base in plans:
        if made:
            ref = refs[plan[0][0]]
            outs[out][base : base + ref.shape[0], :] = ref[...]
            continue
        for j, chosen in every_choice(bits_left(order, step + 1)):
            for bit in order[:step]:
                chosen[bit] = mine[bit]
            chosen[order[step]] = 1 - mine[order[step]]
            to = base + j * unit
            outs[out][to : to + unit, :] = plan_sum(refs, plan, order, chosen, unit).astype(bf16)


def mlp_finish_kernel(n_arrays, plans, *refs):
    mine = my_bits()
    chosen = {bit: mine[bit] for bit in range(TOP_BITS)}
    outs = refs[n_arrays:]
    for i, (part, order, unit, plan) in enumerate(plans):
        total = plan_sum(refs, plan, order, chosen, unit)
        outs[i // 3][:, part * UNIT_BLOCK : (part + 1) * UNIT_BLOCK] = total


def attn_finish_kernel(n_arrays, n_small, plans, *refs):
    mine = my_bits()
    chosen = {bit: mine[bit] for bit in range(TOP_BITS)}
    small, (qkv_ref, proj_ref, *outs) = (
        refs[n_arrays : n_arrays + n_small],
        refs[n_arrays + n_small :],
    )
    local = qkv_ref.shape[2]
    third = local // 3
    for part, order, unit, plan in plans:
        total = plan_sum(refs, plan, order, chosen, unit)
        qkv_ref[part] = total[:, :local]
        proj_ref[:, part * third : (part + 1) * third] = total[:, local:]
    total = sum(ref[...] for ref in small)
    width = total.shape[1]
    for i, out_ref in enumerate(outs[:-1]):
        out_ref[...] = total[i : i + 1, :].reshape(width)
    for i in range(total.shape[0] - 7):
        outs[-1][i * width : (i + 1) * width] = total[7 + i : 8 + i, :].reshape(width)


def both_rows(own, other):
    return jnp.concatenate([own, other], axis=0)


def weight_tile(arranged_ref, right, away_ref, kept_ref, columns):
    half = away_ref.shape[0]
    away_ref[:, columns] = dot(arranged_ref[:half, :], right).astype(bf16)
    kept_ref[:, columns] = dot(arranged_ref[half:, :], right)


def mlp_weights_kernel(at_left, left_own_ref, left_par_ref, right_own_ref, right_par_ref, *outs):
    away_refs, kept_refs, (turned_ref, arranged_ref) = outs[:3], outs[3:6], outs[6:]
    mine = my_bits()
    left_par = left_par_ref[:, at_left : at_left + left_own_ref.shape[1]]
    turned_ref[...] = both_rows(left_own_ref[...], left_par).T
    columns = slice(0, UNIT_BLOCK)
    for part in range(3):
        at = slice(part * UNIT_BLOCK, (part + 1) * UNIT_BLOCK)
        right = both_rows(right_own_ref[:, at], right_par_ref[:, at])
        arrange_rows(turned_ref, mine, part, arranged_ref)
        weight_tile(arranged_ref, right, away_refs[part], kept_refs[part], columns)


def attn_weights_kernel(
    first_own_ref,
    pack_par_ref,
    grad_attn_own_ref,
    grad_attn_par_ref,
    qkv_own_ref,
    qkv_par_ref,
    mixed_own_ref,
    *outs,
):
    away_refs, kept_refs, (turned_ref, arranged_ref) = outs[:3], outs[3:6], outs[6:]
    mine = my_bits()
    width, local = first_own_ref.shape[1], mixed_own_ref.shape[1]
    third = local // 3
    turned_ref[...] = both_rows(first_own_ref[...], pack_par_ref[:, :width]).T
    for part in range(3):
        at = slice(part * local, (part + 1) * local)
        right = both_rows(qkv_own_ref[:, at], qkv_par_ref[:, at])
        arrange_rows(turned_ref, mine, part, arranged_ref)
        weight_tile(arranged_ref, right, away_refs[part], kept_refs[part], slice(0, local))
    turned_ref[...] = both_rows(grad_attn_own_ref[...], grad_attn_par_ref[...]).T
    for part in range(3):
        at = slice(part * third, (part + 1) * third)
        right = both_rows(mixed_own_ref[:, at], pack_par_ref[:, 2 * width + at.start : 2 * width + at.stop])
        arrange_rows(turned_ref, mine, part, arranged_ref)
        weight_tile(
            arranged_ref, right, away_refs[part], kept_refs[part], slice(local, local + third)
        )


def weights(kernel, arrays, width, depth, columns):
    half = width // 2
    return call(
        kernel,
        [shape((half, columns), bf16)] * 3 + [shape((half, columns), f32)] * 3,
        arrays,
        scratch=[pltpu.VMEM((width, depth), bf16), pltpu.VMEM((width, depth), bf16)],
    )


def heads_back(images, count_ref, grad_attn_ref, proj_ref, made_ref, out_ref, mixed_scratch):
    padded, local = made_ref.shape[0] // images, proj_ref.shape[0]
    factor = HEAD_DIM ** (-0.5)
    mixed_scratch[...] = dot_turned(grad_attn_ref[...], proj_ref[...]).astype(bf16)
    units = pairs_of_heads(images, padded, local)
    for first in range(0, len(units), 3):
        some = units[first : first + 3]
        q, k, v = zip(*[saved_qkv(made_ref, rows, at) for _, rows, at in some])
        q = [stacked_heads(x) for x in q]
        grad_mixed = [
            stacked_heads(mixed_scratch[rows, at : at + 2 * HEAD_DIM]) for _, rows, at in some
        ]
        scores = [dot_turned(x, y) * factor for x, y in zip(k, q)]
        grad_probs = [dot_turned(x, y) for x, y in zip(v, grad_mixed)]
        probs = [
            probabilities(x, count_ref[b : b + 1, 0:1], 0) for x, (b, _, _) in zip(scores, some)
        ]
        grad_scores = [
            (p * (g - jnp.sum(p * g, axis=0, keepdims=True))).astype(bf16)
            for p, g in zip(probs, grad_probs)
        ]
        grad_k = [dot(x, y) * factor for x, y in zip(grad_scores, q)]
        grad_v = [dot(x.astype(bf16), y) for x, y in zip(probs, grad_mixed)]
        grad_q = [joined_heads(dot(x, y, ((0,), (0,)))) * factor for x, y in zip(grad_scores, k)]
        for (_, rows, at), *found in zip(some, grad_q, grad_k, grad_v):
            for t in range(3):
                to = slice(t * local + at, t * local + at + 2 * HEAD_DIM)
                out_ref[rows, to] = found[t].astype(bf16)


def back_kernel(
    grad_pre_other_ref,
    w_fc1_other_ref,
    grad_pre_ref,
    w_fc1_ref,
    picked_ref,
    attention_ref,
    grad_picked_ref,
    scale_ref,
    gain_ref,
    grad_attn_ref,
    grad_hidden_ref,
    sums_ref,
):
    grad_second = dot_turned(grad_pre_other_ref[...], w_fc1_other_ref[...])
    grad_second = grad_second + dot_turned(grad_pre_ref[...], w_fc1_ref[...])
    normed, inv_std = norm_stats(picked_ref[...].astype(f32) + attention_ref[...])
    grad_hidden = norm_back(grad_second, line(gain_ref), normed, inv_std)
    grad_hidden_ref[...] = grad_hidden
    grad_attention = scale_ref[...] * grad_picked_ref[...].astype(f32) + grad_hidden
    grad_attn_ref[...] = grad_attention.astype(bf16)
    sums_ref[0:1, :] = column_sum(grad_attention)
    sums_ref[1:2, :] = column_sum(grad_second * normed)
    sums_ref[2:3, :] = column_sum(grad_second)


def branch_kernel(
    picked_ref,
    grad_picked_ref,
    router_ref,
    scale_ref,
    attention_ref,
    act_own_ref,
    act_other_ref,
    w_fc2_ref,
    w_fc2_other_ref,
    fc2_bias_ref,
    update_ref,
    grad_logit_ref,
    router_grad_ref,
):
    scale = scale_ref[...]
    mlp_out = dot(act_own_ref[...], w_fc2_ref[...]) + dot(act_other_ref[...], w_fc2_other_ref[...])
    branch = attention_ref[...] + (mlp_out + line(fc2_bias_ref))
    update_ref[...] = scale * branch
    grad_logit = (
        scale
        * (1.0 - router_ref[...])
        * jnp.sum(grad_picked_ref[...].astype(f32) * branch, axis=-1, keepdims=True)
    )
    grad_logit_ref[...] = grad_logit
    router_grad_ref[...] = column_sum(grad_logit * picked_ref[...].astype(f32))


def first_back_kernel(
    qkv_own_ref,
    gain_ref,
    router_w_ref,
    picked_ref,
    grad_hidden_ref,
    grad_logit_ref,
    grad_qkv_own_ref,
    grad_qkv_other_ref,
    qkv_other_ref,
    fc2_bias_grad_ref,
    router_grad_ref,
    back_sums_ref,
    unit_own_ref,
    unit_other_ref,
    grad_kept_ref,
    keep_ref,
    send_ref,
):
    width = picked_ref.shape[1]
    local = qkv_other_ref.shape[2]
    grad_first = jnp.zeros(picked_ref.shape, f32)
    for side in range(SIDES):
        for t in range(3):
            grad_first = grad_first + dot_turned(
                (grad_qkv_own_ref, grad_qkv_other_ref)[side][:, t * local : (t + 1) * local],
                (qkv_own_ref, qkv_other_ref)[side][t],
            )
    normed, inv_std = norm_stats(picked_ref[...].astype(f32))
    grad_kept_ref[...] = (
        norm_back(grad_first, line(gain_ref), normed, inv_std)
        + grad_hidden_ref[...]
        + grad_logit_ref[...] * line(router_w_ref)
    )
    sums = (
        column_sum(grad_first * normed),
        column_sum(grad_first),
        back_sums_ref[0:1, :],
        back_sums_ref[1:2, :],
        back_sums_ref[2:3, :],
        fc2_bias_grad_ref[...],
        router_grad_ref[...],
    )
    for i, values in enumerate(sums):
        keep_ref[i : i + 1, :] = values
        send_ref[i : i + 1, :] = values
    for i in range(unit_own_ref.shape[0] // width):
        at = slice(i * width, (i + 1) * width)
        keep_ref[7 + i : 8 + i, :] = unit_own_ref[at].reshape(1, width)
        send_ref[7 + i : 8 + i, :] = unit_other_ref[at].reshape(1, width)


def put_back_kernel(n_small, index_ref, base_ref, change_ref, *refs):
    small_refs, outs = refs[:n_small], refs[n_small:]
    if n_small:
        outs[1][...] = sum(ref[...] for ref in small_refs)
    images, slots, _ = base_ref.shape
    padded = change_ref.shape[0] // images
    for b in range(images):
        hot = turned_hot(index_ref, b, slots, padded)
        change = change_ref[b * padded : (b + 1) * padded, :]
        high = change.astype(bf16)
        low = (change - high.astype(f32)).astype(bf16)
        updated = base_ref[b].astype(f32) + (dot(hot, high) + dot(hot, low))
        outs[0][b] = updated.astype(bf16)


def other_core(value):
    return lax.ppermute(value, "head", [(0, 1), (1, 0)])


def partners(count, bit):
    return [(i, i ^ (1 << bit)) for i in range(count)]


def swap(value, bit, count):
    return lax.ppermute(value, "dp", partners(count, bit + count.bit_length() - 1 - TOP_BITS))


def waiting(halves, early=0):
    return [Stream(part, halves[part], halves[3 + part], early) for part in range(3)]


def begin(halves, count, early=0):
    streams = waiting(halves, early)
    for stream in streams:
        stream.sent(swap(stream.away, stream.bit(), count), 0)
    return streams


def exchange(streams, count, after, small=()):
    arrays, plans = listed(streams)
    tied, after = lax.optimization_barrier((tuple(arrays), after))
    bits = []
    for stream in streams:
        if stream.bit() not in bits:
            bits.append(stream.bit())
    sizes, full, bases = [0] * len(bits), [], []
    for stream, plan in zip(streams, plans):
        out = bits.index(stream.bit())
        made = stream.away is not None
        full.append((stream.order, stream.step, made, stream.unit, plan, out, sizes[out]))
        bases.append(sizes[out])
        sizes[out] += stream.rows()
    columns = arrays[0].shape[1]
    outs = [shape((size, columns), bf16) for size in sizes]
    outs += [shape(array.shape, array.dtype) for array in small[:1]]
    made = call(
        functools.partial(step_kernel, len(arrays), len(small), full), outs, (*tied, *small)
    )
    made, after = lax.optimization_barrier((made, after))
    got = [swap(made[n], bit, count) for n, bit in enumerate(bits)]
    for stream, base in zip(streams, bases):
        stream.sent(got[bits.index(stream.bit())], base)
    return (after, made[-1]) if small else after


def arrived(streams, after):
    arrays = []
    for stream in streams:
        if all(stream.terms[-1][0] is not x for x in arrays):
            arrays.append(stream.terms[-1][0])
    tied, after = lax.optimization_barrier((arrays, after))
    for stream in streams:
        array, base, step = stream.terms[-1]
        place = [x is array for x in arrays].index(True)
        stream.terms[-1] = (tied[place], base, step)
    return after


def fewer_rows(grad, count, axis):
    place = lax.axis_index("dp")
    for bit in range(count.bit_length() - 2 - TOP_BITS, -1, -1):
        half = grad.shape[axis] // 2
        mine = (place >> bit) & 1
        away = lax.dynamic_slice_in_dim(grad, (1 - mine) * half, half, axis).astype(bf16)
        kept = lax.dynamic_slice_in_dim(grad, mine * half, half, axis)
        grad = kept + lax.ppermute(away, "dp", partners(count, bit)).astype(f32)
    return grad


def on_device(
    tokens,
    kept_index,
    kept_count,
    ln1_gain,
    ln1_bias,
    w_qkv,
    w_proj,
    proj_bias,
    ln2_gain,
    ln2_bias,
    w_fc1,
    fc1_bias,
    w_fc2,
    fc2_bias,
    w_router,
    cotangent,
):
    images, slots, width = tokens.shape
    padded = rows_of(kept_index.shape[1])
    rows = images * padded
    local = w_qkv.shape[2]
    units = w_fc1.shape[1]
    count = lax.axis_size("dp")

    top = count.bit_length() - 1 - TOP_BITS
    w_qkv_other = other_core(w_qkv)
    w_proj_other = other_core(w_proj)
    bias_other = other_core(fc1_bias)
    tie = lax.optimization_barrier
    table = shape((8, 128), jnp.int32)
    (
        index,
        counts,
        picked,
        grad_picked,
        first,
        grad_mlp,
        router,
        scale,
        fc2_bias_sum,
        w_qkv,
        w_proj,
        proj_bias,
        ln2_gain,
        ln2_bias,
        bias_own,
        fc2_bias,
        ln1_gain,
        w_router,
    ) = call(
        front_kernel,
        [table, table]
        + [shape((rows, width), bf16)] * 4
        + [shape((rows, 1), f32)] * 2
        + [shape((1, width), f32)],
        (
            Far(kept_index),
            Far(tokens),
            Far(kept_count),
            Far(w_router),
            Far(ln1_gain),
            Far(ln1_bias),
            Far(cotangent),
        ),
        fetch=(
            w_qkv,
            w_proj,
            proj_bias,
            ln2_gain,
            ln2_bias,
            fc1_bias,
            fc2_bias,
            ln1_gain,
            w_router,
        ),
    )
    grad_mlp_par = other_core(grad_mlp)
    w_fc1_late, bias_other, first, w_qkv_other, w_proj_other = tie(
        (w_fc1, bias_other, first, w_qkv_other, w_proj_other)
    )
    w_fc1_other = other_core(w_fc1_late)

    made, made_other, mixed, mixed_other, attention, second, pack = call(
        functools.partial(attention_kernel, images),
        [
            shape((rows, 3 * local), bf16),
            shape((rows, 3 * local), bf16),
            shape((rows, local), bf16),
            shape((rows, local), bf16),
            shape((rows, width), f32),
            shape((rows, width), bf16),
            shape((rows, 2 * width + local), bf16),
        ],
        (
            counts,
            first,
            w_qkv,
            w_qkv_other,
            w_proj,
            w_proj_other,
            picked,
            proj_bias,
            ln2_gain,
            ln2_bias,
        ),
    )
    second, grad_mlp_par, w_fc2_late = tie((second, grad_mlp_par, w_fc2))
    w_fc2_other = other_core(w_fc2_late)

    def hidden(w, bias):
        return call(
            hidden_kernel,
            [shape((rows, units), bf16), shape((rows, units), f32)],
            (second, w, bias),
        )

    def hidden_back(w, slope):
        return call(
            hidden_back_kernel,
            [shape((rows, units), bf16), shape((units,), f32)],
            (grad_mlp, w, slope),
        )

    def mlp_weights(left, left_par, at_left, right, right_par):
        return weights(
            functools.partial(mlp_weights_kernel, at_left),
            (left, left_par, right, right_par),
            width,
            2 * rows,
            UNIT_BLOCK,
        )

    act_other, slope_other = hidden(w_fc1_other, bias_other)
    act_par = other_core(act_other)
    bias_own, act_other = tie((bias_own, act_other))
    act, slope = hidden(w_fc1, bias_own)
    grad_pre, unit_own = hidden_back(w_fc2, slope)
    slope_other, grad_pre = tie((slope_other, grad_pre))
    grad_pre_other, unit_other = hidden_back(w_fc2_other, slope_other)
    act, grad_pre, grad_pre_other, pack = tie((act, grad_pre, grad_pre_other, pack))
    halves = mlp_weights(grad_mlp, grad_mlp_par, 0, act, act_par)
    grad_pre_par = other_core(grad_pre_other)
    pack_par = other_core(pack)
    halves, grad_pre_other = tie((halves, grad_pre_other))
    fc2_sums = begin(halves, count, FC2_EARLY)
    grad_attn, grad_hidden, back_sums = call(
        back_kernel,
        [shape((rows, width), bf16), shape((rows, width), f32), shape((8, width), f32)],
        (
            grad_pre_other,
            w_fc1_other,
            grad_pre,
            w_fc1,
            picked,
            attention,
            grad_picked,
            scale,
            ln2_gain,
        ),
    )
    grad_pre, grad_attn = tie((grad_pre, grad_attn))
    halves = mlp_weights(second, pack_par, width, grad_pre, grad_pre_par)

    def attention_back(w, saved, grad):
        return call(
            functools.partial(heads_back, images),
            [shape((rows, 3 * local), bf16)],
            (counts, grad, w, saved),
            scratch=[pltpu.VMEM((rows, local), bf16)],
        )[0]

    halves, grad_attn = tie((halves, grad_attn))
    grad_qkv_other = attention_back(w_proj_other, made_other, grad_attn)
    fc1_sums = waiting(halves, FC1_EARLY)
    grad_attn, grad_qkv_other = exchange(
        (*fc2_sums, *fc1_sums), count, (grad_attn, grad_qkv_other)
    )
    grad_attn_par = other_core(grad_attn)
    grad_qkv_par = other_core(grad_qkv_other)
    grad_qkv = attention_back(w_proj, made, grad_attn)
    halves = weights(
        attn_weights_kernel,
        (first, pack_par, grad_attn, grad_attn_par, grad_qkv, grad_qkv_par, mixed),
        width,
        2 * rows,
        local + local // 3,
    )
    attn_sums = waiting(halves, ATTN_EARLY)
    act = exchange((*fc2_sums, *fc1_sums, *attn_sums), count, act)
    update, grad_logit, router_sum = call(
        branch_kernel,
        [shape((rows, width), f32), shape((rows, 1), f32), shape((1, width), f32)],
        (
            picked,
            grad_picked,
            router,
            scale,
            attention,
            act,
            act_other,
            w_fc2,
            w_fc2_other,
            fc2_bias,
        ),
    )

    sum_rows = 7 + units // width
    grad_kept, keep, send = call(
        first_back_kernel,
        [
            shape((rows, width), f32),
            shape((sum_rows, width), f32),
            shape((sum_rows, width), f32),
        ],
        (
            w_qkv,
            ln1_gain,
            w_router,
            picked,
            grad_hidden,
            grad_logit,
            grad_qkv,
            grad_qkv_other,
            w_qkv_other,
            fc2_bias_sum,
            router_sum,
            back_sums,
            unit_own,
            unit_other,
        ),
    )

    def put_back(base, change, *small):
        return call(
            functools.partial(put_back_kernel, len(small)),
            [Far(shape(base.shape, bf16)), *[shape(x.shape, x.dtype) for x in small[:1]]],
            (index, base, change, *small),
        )

    got = other_core(send)
    update, keep = tie((update, keep))
    output, small = put_back(tokens, update, keep, got)
    got = swap(small, 0, count)
    grad_kept, output = tie((grad_kept, output))
    (input_grad,) = put_back(cotangent, grad_kept)
    input_grad, small = exchange(
        (*fc2_sums, *fc1_sums, *attn_sums), count, input_grad, (small, got)
    )
    got = swap(small, 1, count)
    input_grad, small = exchange((*fc1_sums, *attn_sums), count, input_grad, (small, got))
    small = arrived(fc2_sums, small)
    got = swap(small, 2, count)
    input_grad, small = exchange(attn_sums, count, input_grad, (small, got))
    for low in range(top):
        small = small + lax.ppermute(small, "dp", partners(count, low))
    got = swap(small, 3, count)
    unit = width // UNITS

    def final(streams):
        arrays, plans = listed(streams)
        return arrays, [
            (stream.part, stream.order, stream.unit, plan) for stream, plan in zip(streams, plans)
        ]

    arrays, plans = final((*fc2_sums, *fc1_sums))
    fc2_turned, fc1_grad = call(
        functools.partial(mlp_finish_kernel, len(arrays), plans),
        [Far(shape((unit, units), f32)), Far(shape((unit, units), f32))],
        tuple(arrays),
    )
    small, fc2_turned, fc1_grad = tie((small, fc2_turned, fc1_grad))
    arrays, plans = final(attn_sums)
    qkv_grad, proj_turned, *sums = call(
        functools.partial(attn_finish_kernel, len(arrays), 2, plans),
        [
            Far(shape((3, unit, local), f32)),
            Far(shape((unit, local), f32)),
            *[Far(shape((width,), f32))] * 7,
            Far(shape((units,), f32)),
        ],
        (*arrays, small, got),
    )
    fc2_turned, fc1_grad, proj_turned = (
        fewer_rows(grad, count, 0) for grad in (fc2_turned, fc1_grad, proj_turned)
    )
    qkv_grad = fewer_rows(qkv_grad, count, 1)
    return (
        output,
        input_grad,
        sums[0],
        sums[1],
        qkv_grad,
        proj_turned.T,
        sums[2],
        sums[3],
        sums[4],
        fc1_grad,
        sums[7],
        fc2_turned.T,
        sums[5],
        sums[6],
    )


def solution(mesh):
    batch = ("dp", "head")
    return jax.shard_map(
        on_device,
        mesh=mesh,
        in_specs=(
            P(batch, None, None),
            P(batch, None),
            P(batch),
            P(),
            P(),
            P(None, None, "head"),
            P("head", None),
            P(),
            P(),
            P(),
            P(None, "head"),
            P("head"),
            P("head", None),
            P(),
            P(),
            P(batch, None, None),
        ),
        out_specs=(
            P(batch, None, None),
            P(batch, None, None),
            P(),
            P(),
            P(None, "dp", "head"),
            P("head", "dp"),
            P(),
            P(),
            P(),
            P("dp", "head"),
            P("head"),
            P("head", "dp"),
            P(),
            P(),
        ),
        check_vma=False,
    )
```
